32 devices in a mesh: lon: 8 (over y, x, core), lat: 4 (over z).
Axes of the slice: x: 2, y: 2, z: 4, core: 2. Of those that a mesh axis runs over, the one named last changes fastest.
Arguments:
- fields: bfloat16 [1, 64, 64, 1024], P(None, None, 'lat', 'lon'), may hold values from -6 to 6
- cotangent: bfloat16 [1, 64, 64, 1024], P(None, None, 'lat', 'lon'), may hold values from -6 to 6
- ocean_mask: int32 [64, 1024], P('lat', 'lon'), may hold values 0 or 1
- seam_partner: int32 [1024], replicated, may hold values from 0 to 1023, as said below
- depth_weight: bfloat16 [64, 7, 7], replicated, may hold values from -0.875 to 0.875
- norm_gain: bfloat16 [64], replicated, may hold values from 0.5 to 1.5
- layer_norm_bias: bfloat16 [64], replicated, may hold values from -3 to 3
- up_weight: bfloat16 [256, 64], replicated, may hold values from -0.75 to 0.75
- up_bias: bfloat16 [256], replicated, may hold values from -3 to 3
- down_weight: bfloat16 [64, 256], replicated, may hold values from -0.375 to 0.375
- layer_scale: bfloat16 [64], replicated, may hold values from 0.5 to 1.5
Outputs:
- output: bfloat16 [1, 64, 64, 1024], P(None, None, 'lat', 'lon')
- grad_fields: bfloat16 [1, 64, 64, 1024], P(None, None, 'lat', 'lon')
- grad_depth: float32 [64, 7, 7], replicated
- grad_gain: float32 [64], replicated
- grad_bias: float32 [64], replicated
- grad_up_weight: float32 [256, 64], replicated
- grad_up_bias: float32 [256], replicated
- grad_down_weight: float32 [64, 256], replicated
- grad_scale: float32 [64], replicated
The draws below stay inside these ranges and needn't reach their ends.
Inputs may be any that keep to these rules, and one draw needn't show every extreme that they name: seam_partner[i] = (s - i) mod 1024 for one whole number s, so it is its own inverse.
All inputs are finite; a program needn't handle non-finite values. No bound on the sum of `ocean_mask` on one device may be relied on, other than what follows from the above.
Results may differ from the reference program's by a relative error of at most 0.0068.
Values may be sent and summed in bfloat16 or wider, within the bound.
No kernel may reach another device: no remote copies, remote signals or barrier semaphores. Data moves between devices by JAX's collectives and lax.ppermute only.
A program may use at most 64 MiB of HBM per device.

```python
import math
import jax
import jax.numpy as jnp
from jax import lax

CHANNELS = 64
HIDDEN_SIZE = 256
SAMPLES = 1
LAT_DEV = 16
NLAT = 64
NLON = 1024


def draw_seam_partner(key, part):
    offset = jax.random.randint(jax.random.fold_in(key, 17), (), 0, NLON)
    return ((offset - jnp.arange(NLON, dtype=jnp.int32)) % NLON).astype(jnp.int32)


def set_ends(drawn, stream_key, least, largest):
    dims = drawn.shape
    index_at = [jax.random.randint(jax.random.fold_in(stream_key, axis), (), 0, dims[axis]) for axis in range(len(dims))]
    drawn = drawn.at[tuple(index_at)].set(least)
    longest = dims.index(max(dims))
    index_at[longest] = (index_at[longest] + 1) % dims[longest]
    return drawn.at[tuple(index_at)].set(largest)


def shard_levels(rng, dims, pieces, low, top_value):
    def one(dim, shards_of):
        steps = jax.random.uniform(jax.random.fold_in(jax.random.fold_in(rng, 6), dim), (shards_of,), jnp.float32, low / len(pieces), top_value / len(pieces))
        return jnp.repeat(jnp.exp(steps), dims[dim] // shards_of).reshape((-1,) + (1,) * (len(dims) - dim - 1))

    gain = one(*pieces[0])
    for cut in pieces[1:]:
        gain = gain * one(*cut)
    return gain


def bell_draw(stream_key, extent, deviation, reach, pieces=(), kind=jnp.bfloat16):
    result = deviation * jax.random.normal(stream_key, extent, jnp.float32)
    if pieces:
        result = result * shard_levels(stream_key, extent, pieces, -0.22, 0.18)
    return jnp.clip(result, -reach, reach).astype(kind)


def setup_inputs(seed: int = 0) -> dict:
    arg_keys = jax.random.split(jax.random.key(seed), 12)
    fields = bell_draw(arg_keys[0], (SAMPLES, CHANNELS, NLAT, NLON), 1.0, 6.0, ((2, 4), (3, 8)))
    cotangent = bell_draw(arg_keys[1], (SAMPLES, CHANNELS, NLAT, NLON), 1.0, 6.0, ((2, 4), (3, 8)))
    ocean_mask = set_ends((jax.random.randint(arg_keys[2], (NLAT, NLON), 0, 4) < 3).astype(jnp.int32), jax.random.fold_in(arg_keys[2], 1), 0, 1)
    seam_partner = draw_seam_partner(jax.random.fold_in(arg_keys[11], 71), 0)
    depth_weight = bell_draw(arg_keys[4], (CHANNELS, 7, 7), 49 ** -0.5, 0.875)
    norm_gain = jnp.clip(1.0 + 0.1 * jax.random.normal(arg_keys[5], (CHANNELS,), jnp.float32), 0.5, 1.5).astype(jnp.bfloat16)
    layer_norm_bias = bell_draw(arg_keys[6], (CHANNELS,), 0.5, 3.0)
    up_weight = bell_draw(arg_keys[7], (HIDDEN_SIZE, CHANNELS), CHANNELS ** -0.5, 0.75)
    up_bias = bell_draw(arg_keys[8], (HIDDEN_SIZE,), 0.5, 3.0)
    down_weight = bell_draw(arg_keys[9], (CHANNELS, HIDDEN_SIZE), HIDDEN_SIZE ** -0.5, 0.375)
    layer_scale = jnp.clip(jax.random.uniform(arg_keys[10], (CHANNELS,), jnp.float32, 0.5, 1.5), 0.5, 1.5).astype(jnp.bfloat16)
    return {"fields": fields, "cotangent": cotangent, "ocean_mask": ocean_mask, "seam_partner": seam_partner, "depth_weight": depth_weight, "norm_gain": norm_gain, "layer_norm_bias": layer_norm_bias, "up_weight": up_weight, "up_bias": up_bias, "down_weight": down_weight, "layer_scale": layer_scale}


def extend_field(field, partner):
    rows = field.shape[1]
    upper = field[:, rows - 3:, :][:, ::-1, :]
    upper = jnp.take(upper, partner, axis=2)
    lower = jnp.zeros((field.shape[0], 3, field.shape[2]), field.dtype)
    tall = jnp.concatenate([lower, field, upper], axis=1)
    return jnp.concatenate([tall[:, :, -3:], tall, tall[:, :, :3]], axis=2)

def depth_conv(extended, weight, rows, cols):
    weight_f = weight.astype(jnp.float32)
    total = jnp.zeros((extended.shape[0], rows, cols), jnp.float32)
    for row_tap in range(7):
        for col_tap in range(7):
            total = total + weight_f[:, row_tap, col_tap][:, None, None] * extended[:, row_tap:row_tap + rows, col_tap:col_tap + cols].astype(jnp.float32)
    return total

def gelu_slope(pre):
    cdf = 0.5 * (1.0 + lax.erf(pre / math.sqrt(2.0)))
    return cdf + pre * jnp.exp(-0.5 * pre * pre) / math.sqrt(2.0 * math.pi)

def cell_terms(conv, field, cot, mask, norm_gain, layer_norm_bias, up_weight, up_bias, down_weight, layer_scale):
    mean_c = lax.optimization_barrier(jnp.mean(conv, axis=0, keepdims=True))
    centered_input = conv - mean_c
    var_c = lax.optimization_barrier(jnp.mean(centered_input * centered_input, axis=0, keepdims=True))
    reciprocal_deviation = lax.rsqrt(var_c + 1e-06)
    standardized_input = centered_input * reciprocal_deviation
    layer_norm_gain = norm_gain.astype(jnp.float32)[:, None]
    normalized_output = (standardized_input * layer_norm_gain + layer_norm_bias.astype(jnp.float32)[:, None]).astype(jnp.bfloat16)
    pre = jnp.dot(up_weight, normalized_output, preferred_element_type=jnp.float32) + up_bias.astype(jnp.float32)[:, None]
    hidden = jax.nn.gelu(pre, approximate=False).astype(jnp.bfloat16)
    branch = jnp.dot(down_weight, hidden, preferred_element_type=jnp.float32)
    scale = layer_scale.astype(jnp.float32)[:, None]
    out = (mask * (field.astype(jnp.float32) + scale * branch)).astype(jnp.bfloat16)
    grad_in = mask * cot.astype(jnp.float32)
    d_branch = (grad_in * scale).astype(jnp.bfloat16)
    g_scale = lax.optimization_barrier(jnp.sum(grad_in * branch, axis=1))
    contract_cells = (((1,), (1,)), ((), ()))
    contract_first = (((0,), (0,)), ((), ()))
    g_down = lax.dot_general(d_branch, hidden, contract_cells, preferred_element_type=jnp.float32)
    d_hidden = lax.dot_general(down_weight, d_branch, contract_first, preferred_element_type=jnp.float32)
    d_pre = (d_hidden * gelu_slope(pre)).astype(jnp.bfloat16)
    g_up_b = lax.optimization_barrier(jnp.sum(d_pre.astype(jnp.float32), axis=1))
    g_up_w = lax.dot_general(d_pre, normalized_output, contract_cells, preferred_element_type=jnp.float32)
    normalized_gradient = lax.dot_general(up_weight, d_pre, contract_first, preferred_element_type=jnp.float32)
    gain_gradient = lax.optimization_barrier(jnp.sum(normalized_gradient * standardized_input, axis=1))
    g_bias = lax.optimization_barrier(jnp.sum(normalized_gradient, axis=1))
    gradient_through_norm = normalized_gradient * layer_norm_gain
    convolution_gradient = reciprocal_deviation * (gradient_through_norm - lax.optimization_barrier(jnp.mean(gradient_through_norm, axis=0, keepdims=True)) - standardized_input * lax.optimization_barrier(jnp.mean(gradient_through_norm * standardized_input, axis=0, keepdims=True)))
    return (out, convolution_gradient.astype(jnp.bfloat16), (gain_gradient, g_bias, g_up_w, g_up_b, g_down, g_scale))

def reference(fields, cotangent, ocean_mask, seam_partner, depth_weight, norm_gain, layer_norm_bias, up_weight, up_bias, down_weight, layer_scale):
    samples, chans, rows, cols = fields.shape
    hidden_n = up_weight.shape[0]
    mask_f = ocean_mask.astype(jnp.float32)
    block = LAT_DEV
    count = rows // block

    def split(arr):
        return jnp.transpose(arr.reshape(arr.shape[0], count, block, cols), (1, 0, 2, 3)).reshape(count, arr.shape[0], block * cols)

    def unsplit(arr):
        return jnp.transpose(arr.reshape(count, arr.shape[1], block, cols), (1, 0, 2, 3)).reshape(arr.shape[1], rows, cols)
    totals = (jnp.zeros((chans,), jnp.float32), jnp.zeros((chans,), jnp.float32), jnp.zeros((hidden_n, chans), jnp.float32), jnp.zeros((hidden_n,), jnp.float32), jnp.zeros((chans, hidden_n), jnp.float32), jnp.zeros((chans,), jnp.float32))
    g_depth = jnp.zeros((chans, 7, 7), jnp.float32)
    outputs = []
    grads = []
    weight_f = depth_weight.astype(jnp.float32)
    for sample in range(samples):
        field = fields[sample]
        cot = cotangent[sample]
        extended = extend_field(field, seam_partner)
        conv = depth_conv(extended, depth_weight, rows, cols)

        def step(carry, inputs):
            conv_b, field_b, cot_b, mask_b = inputs
            out_b, dconv_b, parts = cell_terms(conv_b, field_b, cot_b, mask_b, norm_gain, layer_norm_bias, up_weight, up_bias, down_weight, layer_scale)
            return (jax.tree.map(lambda left, right: left + right, carry, parts), (out_b, dconv_b))
        mask_blocks = split(mask_f[None])
        totals, (out_blocks, dconv_blocks) = lax.scan(step, totals, (split(conv), split(field), split(cot), mask_blocks))
        outputs.append(unsplit(out_blocks))
        convolution_gradient = unsplit(dconv_blocks).astype(jnp.float32)
        taps = []
        for row_tap in range(7):
            line = []
            for col_tap in range(7):
                line.append(lax.optimization_barrier(jnp.sum(convolution_gradient * extended[:, row_tap:row_tap + rows, col_tap:col_tap + cols].astype(jnp.float32), axis=(1, 2))))
            taps.append(jnp.stack(line, axis=1))
        g_depth = g_depth + jnp.stack(taps, axis=1)
        padded = jnp.pad(convolution_gradient, ((0, 0), (6, 6), (6, 6)))
        d_ext = jnp.zeros((chans, rows + 6, cols + 6), jnp.float32)
        for row_tap in range(7):
            for col_tap in range(7):
                d_ext = d_ext + weight_f[:, row_tap, col_tap][:, None, None] * padded[:, 6 - row_tap:12 - row_tap + rows, 6 - col_tap:12 - col_tap + cols]
        grid = d_ext[:, 3:rows + 3, 3:cols + 3]
        grid = grid.at[:, :, :3].add(d_ext[:, 3:rows + 3, cols + 3:])
        grid = grid.at[:, :, cols - 3:].add(d_ext[:, 3:rows + 3, :3])
        margin = d_ext[:, rows + 3:, :]
        wrapped = margin[:, :, 3:cols + 3]
        wrapped = wrapped.at[:, :, :3].add(margin[:, :, cols + 3:])
        wrapped = wrapped.at[:, :, cols - 3:].add(margin[:, :, :3])
        folded = jnp.take(wrapped, seam_partner, axis=2)
        grid = grid.at[:, rows - 3:, :].add(folded[:, ::-1, :])
        grads.append((mask_f[None] * cot.astype(jnp.float32) + grid).astype(jnp.bfloat16))
    gain_gradient, g_bias, g_up_w, g_up_b, g_down, g_scale = totals
    return (jnp.stack(outputs), jnp.stack(grads), g_depth, gain_gradient, g_bias, g_up_w, g_up_b, g_down, g_scale)
```

```python
import functools
import math

import jax
import jax.numpy as jnp
from jax import lax
from jax.experimental import pallas as pl
from jax.experimental.pallas import tpu as pltpu
from jax.sharding import PartitionSpec as P

BF = jnp.bfloat16
F32 = jnp.float32
LANES = 128
NT = (((1,), (1,)), ((), ()))


def shift(x, amount, axis=1):
    size = x.shape[axis]
    amount %= size
    return x if amount == 0 else pltpu.roll(x, amount, axis)


def lane_iota(shape):
    return lax.broadcasted_iota(jnp.int32, shape, 1)


def pack_kernel(flags, fields, cot, mask, ft, gt, first, second, plane):
    chans, rows, _ = fields.shape
    groups = chans // 8
    sea = mask[...].astype(F32)
    for turn, dst in ((0, ft), (1, gt)):
        for c in range(chans):
            if turn == 0:
                cell = fields[c].astype(F32)
            else:
                cell = cot[c].astype(F32) * sea
            plane[turn, c * rows : (c + 1) * rows, :] = cell
        for r in range(rows):
            parts = [plane[turn, pl.ds(g * 8 * rows + r, 8, stride=rows), :] for g in range(groups)]
            dst[r] = jnp.concatenate(parts, axis=0).astype(BF)

    def edge(dst, top):
        base = rows - 6 if top else 0
        gbase = rows - 3 if top else 0
        dst[0:6] = ft[base : base + 6]
        dst[6:9] = gt[gbase : gbase + 3]

    @pl.when(flags[0] == 0)
    def _():
        edge(first, True)
        edge(second, False)

    @pl.when(flags[0] == 1)
    def _():
        edge(first, False)
        edge(second, True)


def edge_kernel(fold_first, flags, partner, got_a, got_b, got_c, ft, gt, low, up, sent_l, sent_r):
    rows, chans, cols = ft.shape

    @pl.when(flags[0] == 1)
    def _():
        low[...] = got_a[...]

    @pl.when(flags[0] == 0)
    def _():
        low[...] = got_b[...]

    @pl.when(flags[1] == 1)
    def _():
        got_1 = got_a if fold_first else got_b
        src = lax.broadcasted_iota(jnp.int32, (cols, cols), 0)
        want = jnp.broadcast_to(partner[...], (cols, cols))
        pick_1 = (src + flags[2] == want).astype(F32).astype(BF)
        pick_2 = (src + flags[3] == want).astype(F32).astype(BF)
        for k in range(9):
            m = 5 - k if k < 6 else 14 - k
            mixed = jnp.dot(got_1[m], pick_1, preferred_element_type=F32)
            mixed = mixed + jnp.dot(got_c[m], pick_2, preferred_element_type=F32)
            up[k] = mixed.astype(BF)

    @pl.when((flags[1] == 0) & (flags[0] == 0))
    def _():
        up[...] = got_a[...]

    @pl.when((flags[1] == 0) & (flags[0] == 1))
    def _():
        up[...] = got_b[...]

    lane = lane_iota((chans, LANES))
    acc = {key: jnp.zeros((chans, LANES), F32) for key in ((0, 0), (0, 1), (1, 0), (1, 1))}

    def place(side, value, source, lane_to, width):
        moved = shift(value, lane_to - source)
        for half in (0, 1):
            lo = max(lane_to - half * LANES, 0)
            hi = min(lane_to + width - half * LANES, LANES)
            if lo < hi:
                acc[side, half] = jnp.where((lane >= lo) & (lane < hi), moved, acc[side, half])

    for r in range(rows + 12):
        if r < 6:
            value = low[r]
        elif r < rows + 6:
            value = ft[r - 6]
        else:
            value = up[r - rows - 6]
        value = value.astype(F32)
        place(1, value, cols - 6, 9 * r, 6)
        place(0, value, 0, 9 * r + 3, 6)
    for r in range(rows + 6):
        if r < 3:
            value = low[6 + r]
        elif r < rows + 3:
            value = gt[r - 3]
        else:
            value = up[6 + r - rows - 3]
        value = value.astype(F32)
        place(1, value, cols - 3, 9 * r + 6, 3)
        place(0, value, 0, 9 * r, 3)
    for side, dst in ((0, sent_l), (1, sent_r)):
        dst[...] = jnp.concatenate([acc[side, 0], acc[side, 1]], axis=1).astype(BF)


def normal_terms(v):
    cdf = 0.5 * (1.0 + lax.erf(v * (1.0 / math.sqrt(2.0))))
    dens = jnp.exp(-0.5 * v * v) * (1.0 / math.sqrt(2.0 * math.pi))
    return cdf, dens


def main_kernel(
    ft,
    gt,
    low,
    up,
    sent_l,
    sent_r,
    got_l,
    got_r,
    mask,
    taps,
    taps_up,
    vecs,
    up_aug,
    up_t,
    down,
    down_t,
    out,
    grad,
    red,
    ext,
    side_in,
    side_s,
    moved,
    conv,
    cots,
    dconv,
    wide,
    wide_up,
    plane,
    g_down,
    g_up,
    sums,
):
    rows, chans, cols = ft.shape
    groups = chans // 8
    ext_rows = rows + 12
    mid_rows = rows + 6
    sides = mid_rows
    hidden_n = up_t.shape[1]

    for r in range(ext_rows):
        if r < 6:
            ext[r] = low[r].astype(F32)
        elif r < rows + 6:
            ext[r] = ft[r - 6].astype(F32)
        else:
            ext[r] = up[r - rows - 6].astype(F32)
    for r in range(rows):
        cots[r] = gt[r].astype(F32)
    for r in range(3):
        cots[rows + r] = low[6 + r].astype(F32)
        cots[rows + 3 + r] = up[6 + r].astype(F32)
    lane2 = lane_iota((chans, 2 * LANES))
    slot = lane2 % 9
    from_l = got_l[...].astype(F32)
    from_r = got_r[...].astype(F32)
    side_in[0] = jnp.where(slot < 6, from_l, shift(sent_l[...].astype(F32), 3))
    side_in[1] = jnp.where(slot >= 3, from_r, shift(sent_r[...].astype(F32), -3))
    valid = (slot < 3) & (lane2 < 9 * mid_rows)
    for side, value in ((0, shift(from_l, -6)), (1, from_r)):
        value = jnp.where(valid, value, 0.0)
        cots[sides + 2 * side] = value[:, :LANES]
        cots[sides + 2 * side + 1] = value[:, LANES:]

    lane = lane_iota((8, LANES))

    def row_slot(r):
        return rows + r if r < 3 else r - 3 if r < rows + 3 else r

    def edge_lanes(lo, hi, start):
        if start + 2 < LANES:
            return lo
        if start >= LANES:
            return hi
        return jnp.where(lane < 64, hi, lo)

    def neighbour(left, right, start):
        r_part = shift(edge_lanes(right[0], right[1], start), -start)
        l_part = shift(edge_lanes(left[0], left[1], start), LANES - 3 - start)
        return jnp.where(lane < 64, r_part, l_part)

    def slide(value, side, s):
        if s == 0:
            return value
        if s > 0:
            return shift(jnp.where(lane < s, side, value), -s)
        return shift(jnp.where(lane >= LANES + s, side, value), -s)

    def conv_group(g, _):
        at = pl.ds(pl.multiple_of(g * 8, 8), 8)
        plain = taps[at, :]
        turned = taps_up[at, :]
        for t in range(49):
            wide[t, at, :] = jnp.broadcast_to(plain[:, t : t + 1], (8, LANES))
            wide_up[t, at, :] = jnp.broadcast_to(turned[:, t : t + 1], (8, LANES))
        pair = [[side_in[s, at, 0:LANES], side_in[s, at, LANES : 2 * LANES]] for s in (0, 1)]
        for r in range(ext_rows):
            side_s[r] = neighbour(pair[0], pair[1], 9 * r + 3)
        acc = [None] * mid_rows
        for q in range(7):
            w = [wide[a * 7 + q, at, :] for a in range(7)]
            wu = [wide_up[a * 7 + q, at, :] for a in range(7)]
            for r in range(ext_rows):
                value = slide(ext[r, at, :], side_s[r], q - 3)
                moved[q, r, at, :] = value
                for a in range(7):
                    o = r - a
                    if 0 <= o < mid_rows:
                        term = value * (wu[a] if o >= rows + 3 else w[a])
                        acc[o] = term if acc[o] is None else acc[o] + term
        for o in range(mid_rows):
            conv[row_slot(o), at, :] = acc[o]
        first_up = 9 * (rows + 3)
        for side in (0, 1):
            lo, hi = pair[side]
            acc_lo = jnp.zeros((8, LANES), F32)
            acc_hi = jnp.zeros((8, LANES), F32)
            for a in range(7):
                for q in range(7):
                    d = 9 * a + q
                    r_lo, r_hi = shift(lo, -d), shift(hi, -d)
                    x_lo = r_lo if d == 0 else jnp.where(lane < LANES - d, r_lo, r_hi)
                    w = wide[a * 7 + q, at, :]
                    wu = wide_up[a * 7 + q, at, :]
                    acc_lo = acc_lo + x_lo * jnp.where(lane >= first_up, wu, w)
                    acc_hi = acc_hi + r_hi * jnp.where(lane >= first_up - LANES, wu, w)
            conv[sides + 2 * side, at, :] = acc_lo
            conv[sides + 2 * side + 1, at, :] = acc_hi
        return 0

    lax.fori_loop(0, groups, conv_group, 0)

    g_down[...] = jnp.zeros_like(g_down)
    g_up[...] = jnp.zeros_like(g_up)
    sums[...] = jnp.zeros_like(sums)
    pad_rows = up_aug.shape[1] - chans
    ones = (lax.broadcasted_iota(jnp.int32, (pad_rows, 2 * LANES), 0) == 0).astype(F32).astype(BF)

    def twice(x):
        return jnp.concatenate([x, x], axis=1)

    def pair_of(ref, u):
        return jnp.concatenate([ref[u], ref[u + 1]], axis=1)

    def block(u, own):
        gain, bias, scale = twice(vecs[0]), twice(vecs[1]), twice(vecs[2])
        x = pair_of(conv, u)
        centred = x - jnp.mean(x, axis=0, keepdims=True)
        var = jnp.mean(centred * centred, axis=0, keepdims=True)
        rstd = lax.rsqrt(var + 1e-06)
        xhat = centred * rstd
        normed = (xhat * gain + bias).astype(BF)
        normed = jnp.concatenate([normed, ones], axis=0)
        pre = jnp.dot(up_aug[...], normed, preferred_element_type=F32)
        cdf, dens = normal_terms(pre)
        g = pair_of(cots, u)
        d_branch = (g * scale).astype(BF)
        d_hidden = jnp.dot(down_t[...], d_branch, preferred_element_type=F32)
        d_pre = (d_hidden * (cdf + pre * dens)).astype(BF)
        d_normed = jnp.dot(up_t[...], d_pre, preferred_element_type=F32)
        if own:
            hidden = (pre * cdf).astype(BF)
            branch = jnp.dot(down[...], hidden, preferred_element_type=F32)
            sea = [mask[pl.ds(u + k, 1), :].astype(F32) for k in (0, 1)]
            fields = jnp.concatenate([ext[u + 6], ext[u + 7]], axis=1)
            res = (fields + scale * branch) * jnp.concatenate(sea, axis=1)
            for k in (0, 1):
                for gr in range(groups):
                    plane[0, pl.ds(gr * 8 * rows + u + k, 8, stride=rows), :] = res[
                        gr * 8 : gr * 8 + 8, k * LANES : (k + 1) * LANES
                    ]
            g_down[...] += lax.dot_general(d_branch, hidden, NT, preferred_element_type=F32)
            g_up[...] += lax.dot_general(normed, d_pre, NT, preferred_element_type=F32)
            for k, value in enumerate((d_normed * xhat, d_normed, g * branch)):
                sums[k] += value[:, :LANES] + value[:, LANES:]
        gd = d_normed * gain
        m1 = jnp.mean(gd, axis=0, keepdims=True)
        m2 = jnp.mean(gd * xhat, axis=0, keepdims=True)
        dx = (rstd * (gd - m1 - xhat * m2)).astype(BF).astype(F32)
        dconv[u] = dx[:, :LANES]
        dconv[u + 1] = dx[:, LANES:]

    def own_block(b, _):
        block(b * 2, True)
        return 0

    def halo_block(b, _):
        block(rows + b * 2, False)
        return 0

    lax.fori_loop(0, rows // 2, own_block, 0)
    lax.fori_loop(0, 5, halo_block, 0)

    def adjoint_group(g, _):
        at = pl.ds(pl.multiple_of(g * 8, 8), 8)
        pair = [[dconv[sides + 2 * s, at, :], dconv[sides + 2 * s + 1, at, :]] for s in (0, 1)]
        for r in range(mid_rows):
            side_s[r] = neighbour(pair[0], pair[1], 9 * r)
        acc = [None] * rows
        for q in range(7):
            w = [wide[(6 - a) * 7 + 6 - q, at, :] for a in range(7)]
            wu = [wide_up[(6 - a) * 7 + 6 - q, at, :] for a in range(7)]
            for r in range(mid_rows):
                value = slide(dconv[row_slot(r), at, :], side_s[r], q - 3)
                for a in range(7):
                    o = r - a
                    if 0 <= o < rows:
                        term = value * (wu[a] if r >= rows + 3 else w[a])
                        acc[o] = term if acc[o] is None else acc[o] + term
        for o in range(rows):
            plane[1, pl.ds(g * (8 * rows) + o, 8, stride=rows), :] = acc[o] + cots[o, at, :]
        line = jnp.zeros((8, LANES), F32)
        own = [dconv[o, at, :] for o in range(rows)]
        for q in range(7):
            tot = [None] * 7
            for r in range(mid_rows):
                value = moved[q, r + 3, at, :]
                for a in range(7):
                    o = r - a
                    if 0 <= o < rows:
                        term = value * own[o]
                        tot[a] = term if tot[a] is None else tot[a] + term
            for a in range(7):
                total = jnp.sum(tot[a], axis=1, keepdims=True)
                line = jnp.where(lane == a * 7 + q, total, line)
        for k in range(3):
            total = jnp.sum(sums[k, at, :], axis=1, keepdims=True)
            line = jnp.where(lane == 49 + k, total, line)
        red[pl.ds(pl.multiple_of(4 * chans + 16 + g * 8, 8), 8), :] = line
        return 0

    lax.fori_loop(0, groups, adjoint_group, 0)

    for h in range(hidden_n // LANES):
        red[h * chans : (h + 1) * chans, :] = g_down[:, h * LANES : (h + 1) * LANES]
        red[(2 + h) * chans : (3 + h) * chans, :] = g_up[0:chans, h * LANES : (h + 1) * LANES]
        red[4 * chans + 8 * h : 4 * chans + 8 * h + 8, :] = g_up[chans : chans + 8, h * LANES : (h + 1) * LANES]
    tail = 5 * chans + 16
    red[tail:, :] = jnp.zeros((red.shape[0] - tail, LANES), F32)
    for c in range(chans):
        out[c] = plane[0, c * rows : (c + 1) * rows, :].astype(BF)
        grad[c] = plane[1, c * rows : (c + 1) * rows, :].astype(BF)


def vmem(n):
    return [pl.BlockSpec(memory_space=pltpu.VMEM)] * n


def smem():
    return pl.BlockSpec(memory_space=pltpu.SMEM)


def shards(
    fields,
    cotangent,
    ocean_mask,
    seam_partner,
    depth_weight,
    norm_gain,
    layer_norm_bias,
    up_weight,
    up_bias,
    down_weight,
    layer_scale,
):
    _, chans, rows, cols = fields.shape
    hidden_n = up_weight.shape[0]
    n_lon, n_lat = lax.axis_size("lon"), lax.axis_size("lat")
    x, z = lax.axis_index("lon"), lax.axis_index("lat")
    odd = z % 2
    is_top = z == n_lat - 1
    sds = jax.ShapeDtypeStruct
    ft, gt, first, second = pl.pallas_call(
        pack_kernel,
        out_shape=[sds((rows, chans, cols), BF)] * 2 + [sds((9, chans, cols), BF)] * 2,
        in_specs=[smem()] + vmem(3),
        out_specs=vmem(4),
        scratch_shapes=[pltpu.VMEM((2, chans * rows, cols), F32)],
        name="pack",
    )(odd.astype(jnp.int32)[None], fields[0], cotangent[0], ocean_mask)

    at = lambda lon, lat: (lon % n_lon) * n_lat + lat
    rounds = [[], []]
    for lat in range(n_lat - 1):
        for lon in range(n_lon):
            rounds[lat % 2] += [(at(lon, lat), at(lon, lat + 1)), (at(lon, lat + 1), at(lon, lat))]
    fold_round = (n_lat - 1) % 2

    def exchange(k):
        def run(first, second):
            mirror = [
                [(at(lon, n_lat - 1), at(k - j - lon, n_lat - 1)) for lon in range(n_lon)] for j in (0, 1)
            ]
            plan = [list(rounds[0]), list(rounds[1])]
            plan[fold_round] += mirror[0]
            axes = ("lon", "lat")
            top = first if fold_round == 0 else second
            return (
                lax.ppermute(first, axes, plan[0]),
                lax.ppermute(second, axes, plan[1]),
                lax.ppermute(top, axes, mirror[1]),
            )

        return run

    turn = seam_partner[0] // cols
    got_a, got_b, got_c = lax.switch(turn, [exchange(k) for k in range(n_lon)], first, second)
    own_partner = lax.dynamic_slice_in_dim(seam_partner, x * cols, cols)[None]
    flags = jnp.stack(
        [
            odd,
            is_top.astype(jnp.int32),
            (turn - x) % n_lon * cols,
            (turn - 1 - x) % n_lon * cols,
        ]
    ).astype(jnp.int32)
    low, up, sent_l, sent_r = pl.pallas_call(
        functools.partial(edge_kernel, fold_round == 0),
        out_shape=[sds((9, chans, cols), BF)] * 2 + [sds((chans, 2 * cols), BF)] * 2,
        in_specs=[smem()] + vmem(6),
        out_specs=vmem(4),
        name="edges",
    )(flags, own_partner, got_a, got_b, got_c, ft, gt)
    got_l = lax.ppermute(sent_r, "lon", [(i, (i + 1) % n_lon) for i in range(n_lon)])
    got_r = lax.ppermute(sent_l, "lon", [(i, (i - 1) % n_lon) for i in range(n_lon)])

    flat = depth_weight.reshape(chans, 49).astype(F32)
    taps = jnp.pad(flat, ((0, 0), (0, LANES - 49)))
    taps_up = jnp.pad(jnp.where(is_top, flat[:, ::-1], flat), ((0, 0), (0, LANES - 49)))
    vecs = jnp.broadcast_to(
        jnp.stack([norm_gain, layer_norm_bias, layer_scale]).astype(F32)[:, :, None], (3, chans, LANES)
    )
    up_aug = jnp.concatenate(
        [up_weight, up_bias[:, None], jnp.zeros((hidden_n, 15), BF)], axis=1
    )
    units = rows + 10
    red_rows = 5 * chans + 32
    output, grad, red = pl.pallas_call(
        main_kernel,
        out_shape=[sds((chans, rows, cols), BF)] * 2 + [sds((red_rows, LANES), F32)],
        in_specs=vmem(16),
        out_specs=vmem(3),
        scratch_shapes=[
            pltpu.VMEM((rows + 12, chans, cols), F32),
            pltpu.VMEM((2, chans, 2 * cols), F32),
            pltpu.VMEM((rows + 12, 8, cols), F32),
            pltpu.VMEM((7, rows + 12, chans, cols), F32),
            pltpu.VMEM((units, chans, cols), F32),
            pltpu.VMEM((units, chans, cols), F32),
            pltpu.VMEM((units, chans, cols), F32),
            pltpu.VMEM((49, chans, LANES), F32),
            pltpu.VMEM((49, chans, LANES), F32),
            pltpu.VMEM((2, chans * rows, cols), F32),
            pltpu.VMEM((chans, hidden_n), F32),
            pltpu.VMEM((chans + 16, hidden_n), F32),
            pltpu.VMEM((3, chans, LANES), F32),
        ],
        name="block",
    )(
        ft,
        gt,
        low,
        up,
        sent_l,
        sent_r,
        got_l,
        got_r,
        ocean_mask,
        taps,
        taps_up,
        vecs,
        up_aug,
        up_weight.T,
        down_weight,
        down_weight.T,
    )

    half = red_rows // 2
    bit = x % 2
    kept = lax.dynamic_slice_in_dim(red, bit * half, half)
    passed = lax.dynamic_slice_in_dim(red, (1 - bit) * half, half)
    flip = lambda y, axis, b: lax.ppermute(y, axis, [(i, i ^ b) for i in range(lax.axis_size(axis))])
    total = kept + flip(passed, "lon", 1)
    for axis, b in [("lon", 1 << i) for i in range(1, n_lon.bit_length() - 1)] + [
        ("lat", 1 << i) for i in range(n_lat.bit_length() - 1)
    ]:
        total = total + flip(total, axis, b)
    other = flip(total, "lon", 1)
    summed = jnp.concatenate([jnp.where(bit == 0, total, other), jnp.where(bit == 0, other, total)], axis=0)
    down_g = jnp.concatenate([summed[:chans], summed[chans : 2 * chans]], axis=1)
    up_g = jnp.concatenate([summed[2 * chans : 3 * chans].T, summed[3 * chans : 4 * chans].T], axis=0)
    up_b_g = jnp.concatenate([summed[4 * chans], summed[4 * chans + 8]])
    small = summed[4 * chans + 16 : 5 * chans + 16]
    return (
        output[None],
        grad[None],
        small[:, :49].reshape(chans, 7, 7),
        small[:, 49],
        small[:, 50],
        up_g,
        up_b_g,
        down_g,
        small[:, 51],
    )


def solution(mesh):
    block = P(None, None, "lat", "lon")
    placed = (block, block, P("lat", "lon")) + (P(),) * 8
    return jax.shard_map(
        shards, mesh=mesh, in_specs=placed, out_specs=(block, block) + (P(),) * 7, check_vma=False
    )
```

```python
import functools
import math

import jax
import jax.numpy as jnp
from jax import lax
from jax.experimental import pallas as pl
from jax.experimental.pallas import tpu as pltpu
from jax.sharding import PartitionSpec as P

BF = jnp.bfloat16
F32 = jnp.float32
LANES = 128
NT = (((1,), (1,)), ((), ()))


def shift(x, amount, axis=1):
    size = x.shape[axis]
    amount %= size
    return x if amount == 0 else pltpu.roll(x, amount, axis)


def lane_iota(shape):
    return lax.broadcasted_iota(jnp.int32, shape, 1)


def pack_kernel(fields, cot, mask, ft, gt, first, second, plane):
    chans, rows, _ = fields.shape
    groups = chans // 8
    sea = mask[...].astype(F32)
    for turn, dst in ((0, ft), (1, gt)):
        for c in range(chans):
            if turn == 0:
                cell = fields[c].astype(F32)
            else:
                cell = cot[c].astype(F32) * sea
            plane[turn, c * rows : (c + 1) * rows, :] = cell
        for r in range(rows):
            parts = [plane[turn, pl.ds(g * 8 * rows + r, 8, stride=rows), :] for g in range(groups)]
            dst[r] = jnp.concatenate(parts, axis=0).astype(BF)

    def edge(dst, top):
        base = rows - 6 if top else 0
        gbase = rows - 3 if top else 0
        dst[0:6] = ft[base : base + 6]
        dst[6:9] = gt[gbase : gbase + 3]

    odd = lax.axis_index("lat") % 2

    @pl.when(odd == 0)
    def _():
        edge(first, True)
        edge(second, False)

    @pl.when(odd == 1)
    def _():
        edge(first, False)
        edge(second, True)


def field_lane(r):
    return LANES * (r // 14) + 6 * (r % 14)


def cot_lane(g):
    return LANES * (g // 11) + 84 + 3 * (g % 11)


def edge_kernel(fold_first, seam, partner, got_a, got_b, got_c, ft, gt, low, up, sent_l, sent_r):
    rows, chans, cols = ft.shape
    n_lon = partner.shape[0]
    x = lax.axis_index("lon")
    z = lax.axis_index("lat")
    odd = z % 2
    top = z == lax.axis_size("lat") - 1

    @pl.when(odd == 1)
    def _():
        low[...] = got_a[...]

    @pl.when(odd == 0)
    def _():
        low[...] = got_b[...]

    @pl.when(top)
    def _():
        got_1 = got_a if fold_first else got_b
        src = lax.broadcasted_iota(jnp.int32, (cols, cols), 0)
        want = jnp.broadcast_to(partner[pl.ds(x, 1), :], (cols, cols))
        near = (seam[0] // cols - x + n_lon) % n_lon
        far = (near + n_lon - 1) % n_lon
        pick_1 = (src + near * cols == want).astype(F32).astype(BF)
        pick_2 = (src + far * cols == want).astype(F32).astype(BF)
        for k in range(9):
            m = 5 - k if k < 6 else 14 - k
            mixed = jnp.dot(got_1[m], pick_1, preferred_element_type=F32)
            mixed = mixed + jnp.dot(got_c[m], pick_2, preferred_element_type=F32)
            up[k] = mixed.astype(BF)

    @pl.when(jnp.logical_not(top) & (odd == 0))
    def _():
        up[...] = got_a[...]

    @pl.when(jnp.logical_not(top) & (odd == 1))
    def _():
        up[...] = got_b[...]

    lane = lane_iota((chans, LANES))
    acc = {key: jnp.zeros((chans, LANES), F32) for key in ((0, 0), (0, 1), (1, 0), (1, 1))}

    def place(side, value, source, lane_to, width):
        half, at = lane_to // LANES, lane_to % LANES
        moved = shift(value, at - source)
        acc[side, half] = jnp.where((lane >= at) & (lane < at + width), moved, acc[side, half])

    for r in range(rows + 12):
        if r < 6:
            value = low[r]
        elif r < rows + 6:
            value = ft[r - 6]
        else:
            value = up[r - rows - 6]
        value = value.astype(F32)
        place(1, value, cols - 6, field_lane(r), 6)
        place(0, value, 0, field_lane(r), 6)
    for r in range(rows + 6):
        if r < 3:
            value = low[6 + r]
        elif r < rows + 3:
            value = gt[r - 3]
        else:
            value = up[6 + r - rows - 3]
        value = value.astype(F32)
        place(1, value, cols - 3, cot_lane(r), 3)
        place(0, value, 0, cot_lane(r), 3)
    for side, dst in ((0, sent_l), (1, sent_r)):
        dst[...] = jnp.concatenate([acc[side, 0], acc[side, 1]], axis=1).astype(BF)


def weight_kernel(taps, gain, bias, scale, up_b, up_t, down, plain, turned, vecs, up_aug, down_t, line):
    chans, hidden_n = up_t.shape
    line[...] = jnp.zeros_like(line)
    for a in range(7):
        block = taps[a].astype(F32)
        for q in range(7):
            line[0, q, 8 * a : 8 * a + 1, 0:chans] = block[q : q + 1]
            line[1, 6 - q, 48 - 8 * a : 49 - 8 * a, 0:chans] = block[q : q + 1]
    for q in range(7):
        plain[q] = line[0, q].T[:chans]
        turned[q] = line[1, q].T[:chans]
    wide = LANES - chans
    columns = jnp.concatenate(
        [v[...].astype(F32).reshape(1, chans) for v in (gain, bias, scale)] + [jnp.zeros((5, chans), F32)],
        axis=0,
    )
    columns = jnp.concatenate([columns, jnp.zeros((8, wide), F32)], axis=1).T
    for k in range(3):
        vecs[k] = jnp.broadcast_to(columns[:chans, k : k + 1], (chans, LANES))
    tall = jnp.concatenate(
        [
            up_t[...].astype(F32),
            up_b[...].astype(F32).reshape(1, hidden_n),
            jnp.zeros((wide - 1, hidden_n), F32),
        ],
        axis=0,
    )
    up_aug[...] = tall.T[:, : chans + 16].astype(BF)
    tall = jnp.concatenate([down[...].astype(F32), jnp.zeros((wide, hidden_n), F32)], axis=0)
    down_t[...] = tall.T[:, :chans].astype(BF)


def normal_terms(v):
    cdf = 0.5 * (1.0 + lax.erf(v * (1.0 / math.sqrt(2.0))))
    dens = jnp.exp(-0.5 * v * v) * (1.0 / math.sqrt(2.0 * math.pi))
    return cdf, dens


def main_kernel(
    ft,
    gt,
    low,
    up,
    got_l,
    got_r,
    mask,
    plain,
    turned,
    vecs,
    up_aug,
    up_t,
    down,
    down_t,
    out,
    grad,
    kept,
    passed,
    ext,
    rim,
    rhs,
    conv,
    cots,
    dcv,
    plane,
    band,
    band_up,
    prod_1,
    prod_2,
    prod_3,
    g_down,
    g_up,
    sums,
    taps_g,
):
    rows, chans, cols = ft.shape
    groups = chans // 8
    mid = rows + 6
    odd_core = lax.axis_index("lon") % 2
    top = lax.axis_index("lat") == lax.axis_size("lat") - 1
    lane = lane_iota((8, LANES))
    wide = slice(0, LANES), slice(LANES, 2 * LANES)

    for r in range(rows):
        cots[(r + 3) * chans : (r + 4) * chans, :] = gt[r].astype(F32)
    for r in range(3):
        cots[r * chans : (r + 1) * chans, :] = low[6 + r].astype(F32)
        cots[(rows + 3 + r) * chans : (rows + 4 + r) * chans, :] = up[6 + r].astype(F32)
    lane_c = lane_iota((chans, LANES))
    for k, got in ((0, got_l), (1, got_r)):
        first = shift(got[:, wide[0]].astype(F32), -84)
        second = shift(got[:, wide[1]].astype(F32), 33 - 84)
        value = jnp.where(lane_c < 33, first, jnp.where(lane_c < 3 * mid, second, 0.0))
        cots[(mid + k) * chans : (mid + k + 1) * chans, :] = value

    def edge_mask(s):
        return lane < s if s > 0 else lane >= LANES + s

    def at_row(r, g):
        return pl.ds(pl.multiple_of(r * chans + g * 8, 8), 8)

    def conv_group(g, _):
        at = pl.ds(pl.multiple_of(g * 8, 8), 8)
        left = [got_l[at, w].astype(F32) for w in wide]
        right = [got_r[at, w].astype(F32) for w in wide]
        for r0 in range(0, rows + 12, 2):
            pair = []
            for r in (r0, r0 + 1):
                if r < 6:
                    value = low[r, at, :]
                elif r < rows + 6:
                    value = ft[r - 6, at, :]
                else:
                    value = up[r - rows - 6, at, :]
                value = value.astype(F32)
                half, start = field_lane(r) // LANES, field_lane(r) % LANES
                beyond = jnp.where(lane < 64, shift(right[half], -start), shift(left[half], LANES - 6 - start))
                ext[at_row(r, g), :] = value
                rim[at_row(r, g), :] = beyond
                pair.append(jnp.concatenate([value, beyond], axis=1))
            rhs[8 * r0 : 8 * r0 + 16, :] = jnp.concatenate(pair, axis=0).astype(BF)
        for q in range(7):
            one, two = plain[q, at, :], turned[q, at, :]
            above = jnp.where(top, two, one)
            band[q * 80 : q * 80 + 80, :] = jnp.concatenate(
                [pltpu.roll(one, 8 * i, 1, stride=1, stride_axis=0) for i in range(10)], axis=0
            ).astype(BF)
            band_up[q * 32 : q * 32 + 32, :] = jnp.concatenate(
                [pltpu.roll(above, 8 * i, 1, stride=1, stride_axis=0) for i in range(6, 10)], axis=0
            ).astype(BF)
        prod_1[...] = jnp.dot(band[...], rhs[0:128, :], preferred_element_type=F32)
        prod_2[...] = jnp.dot(band[...], rhs[80:208, :], preferred_element_type=F32)
        prod_3[0:224, :] = jnp.dot(band_up[0:224, :], rhs[96:224, :], preferred_element_type=F32)
        sides = [jnp.zeros((8, LANES), F32)] * 2
        for o in range(mid):
            if o < 10:
                prod, step, i = prod_1, 80, o
            elif o < rows + 3:
                prod, step, i = prod_2, 80, o - 10
            else:
                prod, step, i = prod_3, 32, o - 18
            inner = outer = None
            for q in range(7):
                part = slice(q * step + 8 * i, q * step + 8 * i + 8)
                mine, edge = prod[part, wide[0]], prod[part, wide[1]]
                if q != 3:
                    swap = edge_mask(q - 3)
                    mine, edge = jnp.where(swap, edge, mine), jnp.where(swap, mine, edge)
                    mine, edge = shift(mine, 3 - q), shift(edge, 3 - q)
                inner = mine if inner is None else inner + mine
                outer = edge if outer is None else outer + edge
            conv[at_row(o, g), :] = inner
            inside = (lane >= 3 * o) & (lane < 3 * o + 3)
            sides[0] = jnp.where(inside, shift(outer, 3 * o + 3), sides[0])
            sides[1] = jnp.where(inside, shift(outer, 3 * o), sides[1])
        for k in (0, 1):
            conv[at_row(mid + k, g), :] = sides[k]
        return 0

    lax.fori_loop(0, groups, conv_group, 0)

    g_down[...] = jnp.zeros_like(g_down)
    g_up[...] = jnp.zeros_like(g_up)
    sums[...] = jnp.zeros_like(sums)
    pad_rows = up_aug.shape[1] - chans
    ones = (lax.broadcasted_iota(jnp.int32, (pad_rows, 2 * LANES), 0) == 0).astype(F32).astype(BF)

    def twice(x):
        return jnp.concatenate([x, x], axis=1)

    def unit(u):
        return pl.ds(pl.multiple_of(u * chans, chans), chans)

    def pair_of(ref, units):
        return jnp.concatenate([ref[unit(u), :] for u in units], axis=1)

    def block(units, own):
        gain, bias, scale = twice(vecs[0]), twice(vecs[1]), twice(vecs[2])
        x = pair_of(conv, units)
        centred = x - jnp.mean(x, axis=0, keepdims=True)
        var = jnp.mean(centred * centred, axis=0, keepdims=True)
        rstd = lax.rsqrt(var + 1e-06)
        xhat = centred * rstd
        normed = (xhat * gain + bias).astype(BF)
        normed = jnp.concatenate([normed, ones], axis=0)
        pre = jnp.dot(up_aug[...], normed, preferred_element_type=F32)
        cdf, dens = normal_terms(pre)
        g = pair_of(cots, units)
        d_branch = (g * scale).astype(BF)
        d_hidden = jnp.dot(down_t[...], d_branch, preferred_element_type=F32)
        d_pre = (d_hidden * (cdf + pre * dens)).astype(BF)
        d_normed = jnp.dot(up_t[...], d_pre, preferred_element_type=F32)
        if own:
            hidden = (pre * cdf).astype(BF)
            branch = jnp.dot(down[...], hidden, preferred_element_type=F32)
            sea = [mask[pl.ds(u - 3, 1), :].astype(F32) for u in units]
            fields = jnp.concatenate([ext[unit(u + 3), :] for u in units], axis=1)
            res = (fields + scale * branch) * jnp.concatenate(sea, axis=1)
            for k, u in enumerate(units):
                for gr in range(groups):
                    plane[0, pl.ds(gr * 8 * rows + u - 3, 8, stride=rows), :] = res[gr * 8 : gr * 8 + 8, wide[k]]
            g_down[...] += lax.dot_general(d_branch, hidden, NT, preferred_element_type=F32)
            g_up[...] += lax.dot_general(normed, d_pre, NT, preferred_element_type=F32)
            for k, value in enumerate((d_normed * xhat, d_normed, g * branch)):
                sums[k] += value[:, :LANES] + value[:, LANES:]
        gd = d_normed * gain
        m1 = jnp.mean(gd, axis=0, keepdims=True)
        m2 = jnp.mean(gd * xhat, axis=0, keepdims=True)
        dx = (rstd * (gd - m1 - xhat * m2)).astype(BF).astype(F32)
        for k, u in enumerate(units):
            dcv[unit(u), :] = dx[:, wide[k]]

    def own_block(b, _):
        block((b * 2 + 3, b * 2 + 4), True)
        return 0

    def halo_block(b, _):
        one = jnp.where(b < 2, 2 * b, rows + 2 * b)
        two = jnp.where(b == 0, 1, rows + 1 + 2 * b)
        block((one, two), False)
        return 0

    lax.fori_loop(0, rows // 2, own_block, 0)
    lax.fori_loop(0, 4, halo_block, 0)

    def adjoint_group(g, _):
        at = pl.ds(pl.multiple_of(g * 8, 8), 8)
        left, right = dcv[at_row(mid, g), :], dcv[at_row(mid + 1, g), :]
        for r0 in range(0, mid, 2):
            pair = []
            for r in (r0, r0 + 1):
                value = dcv[at_row(r, g), :]
                beyond = jnp.where(lane < 64, shift(right, -3 * r), shift(left, LANES - 3 - 3 * r))
                pair.append(jnp.concatenate([value, beyond], axis=1))
            rhs[8 * r0 : 8 * r0 + 16, :] = jnp.concatenate(pair, axis=0).astype(BF)
        for q in range(7):
            one, two = turned[q, at, :], plain[q, at, :]
            above = jnp.where(top, two, one)
            moved = [pltpu.roll(one, 8 * i, 1, stride=1, stride_axis=0) for i in range(10)]
            band[q * 80 : q * 80 + 80, :] = jnp.concatenate(moved, axis=0).astype(BF)
            late = moved[:3]
            for i in range(3, 6):
                other = pltpu.roll(above, 8 * i, 1, stride=1, stride_axis=0)
                late.append(jnp.where(lane >= 8 * (rows + 3 - 10), other, moved[i]))
            band_up[q * 48 : q * 48 + 48, :] = jnp.concatenate(late, axis=0).astype(BF)
        prod_1[...] = jnp.dot(band[...], rhs[0:128, :], preferred_element_type=F32)
        prod_3[...] = jnp.dot(band_up[:, 0:96], rhs[80:176, :], preferred_element_type=F32)
        for o in range(rows):
            prod, step, i = (prod_1, 80, o) if o < 10 else (prod_3, 48, o - 10)
            inner = cots[at_row(o + 3, g), :]
            for q in range(7):
                part = slice(q * step + 8 * i, q * step + 8 * i + 8)
                mine = prod[part, wide[0]]
                if q != 3:
                    mine = shift(jnp.where(edge_mask(q - 3), prod[part, wide[1]], mine), 3 - q)
                inner = inner + mine
            plane[1, pl.ds(g * (8 * rows) + o, 8, stride=rows), :] = inner
        line = jnp.zeros((8, LANES), F32)
        for q in range(7):
            own = [shift(dcv[at_row(o + 3, g), :], q - 3) for o in range(rows)]
            tot = [None] * 7
            for r in range(mid):
                value = ext[at_row(r + 3, g), :]
                if q != 3:
                    value = jnp.where(edge_mask(q - 3), rim[at_row(r + 3, g), :], value)
                for a in range(7):
                    o = r - a
                    if 0 <= o < rows:
                        term = value * own[o]
                        tot[a] = term if tot[a] is None else tot[a] + term
            for a in range(7):
                total = jnp.sum(tot[a], axis=1, keepdims=True)
                line = jnp.where(lane == 8 * a + q, total, line)
        for k in range(3):
            total = jnp.sum(sums[k, at, :], axis=1, keepdims=True)
            line = jnp.where(lane == 56 + k, total, line)
        taps_g[at, :] = line
        return 0

    lax.fori_loop(0, groups, adjoint_group, 0)
    small = taps_g[...]
    cut = 40

    def fill(lower, upper):
        for h, w in enumerate(wide):
            lower[h * chans : (h + 1) * chans, :] = g_down[:, w]
            upper[h * chans : (h + 1) * chans, :] = g_up[0:chans, w]
            upper[2 * chans + 24 + 8 * h : 2 * chans + 32 + 8 * h, :] = g_up[chans : chans + 8, w]
        lower[2 * chans : 2 * chans + cut, :] = small[:cut]
        upper[2 * chans : 2 * chans + 24, :] = small[cut:]

    @pl.when(odd_core == 0)
    def _():
        fill(kept, passed)

    @pl.when(odd_core == 1)
    def _():
        fill(passed, kept)

    for c in range(chans):
        out[c] = plane[0, c * rows : (c + 1) * rows, :].astype(BF)
        grad[c] = plane[1, c * rows : (c + 1) * rows, :].astype(BF)


def finish_kernel(total, other, g_depth, g_gain, g_bias, g_up, g_up_b, g_down, g_scale):
    chans, hidden_n = g_down.shape

    def unpack(lower, upper):
        for h in range(hidden_n // LANES):
            w = slice(h * LANES, (h + 1) * LANES)
            g_down[:, w] = lower[h * chans : (h + 1) * chans, :]
            g_up[:, w] = upper[h * chans : (h + 1) * chans, :]
            at = 2 * chans + 24 + 8 * h
            g_up_b[w] = upper[at : at + 1, :].reshape(LANES)
        small = jnp.concatenate(
            [
                lower[2 * chans : 2 * chans + 40, :],
                upper[2 * chans : 2 * chans + 24, :],
                jnp.zeros((LANES - chans, LANES), F32),
            ],
            axis=0,
        ).T
        for k, dst in enumerate((g_gain, g_bias, g_scale)):
            dst[...] = small[56 + k : 57 + k, :chans].reshape(chans)
        for a in range(7):
            g_depth[a] = small[8 * a : 8 * a + 7, :chans]

    odd_core = lax.axis_index("lon") % 2

    @pl.when(odd_core == 0)
    def _():
        unpack(total, other)

    @pl.when(odd_core == 1)
    def _():
        unpack(other, total)


def vmem(n):
    return [pl.BlockSpec(memory_space=pltpu.VMEM)] * n


def smem():
    return pl.BlockSpec(memory_space=pltpu.SMEM)


def shards(
    fields,
    cotangent,
    ocean_mask,
    seam_partner,
    depth_weight,
    norm_gain,
    layer_norm_bias,
    up_weight,
    up_bias,
    down_weight,
    layer_scale,
):
    _, chans, rows, cols = fields.shape
    hidden_n = up_weight.shape[0]
    n_lon, n_lat = lax.axis_size("lon"), lax.axis_size("lat")
    sds = jax.ShapeDtypeStruct
    ft, gt, first, second = pl.pallas_call(
        pack_kernel,
        out_shape=[sds((rows, chans, cols), BF)] * 2 + [sds((9, chans, cols), BF)] * 2,
        in_specs=vmem(3),
        out_specs=vmem(4),
        scratch_shapes=[pltpu.VMEM((2, chans * rows, cols), F32)],
        name="pack",
    )(fields[0], cotangent[0], ocean_mask)

    at = lambda lon, lat: (lon % n_lon) * n_lat + lat
    rounds = [[], []]
    for lat in range(n_lat - 1):
        for lon in range(n_lon):
            rounds[lat % 2] += [(at(lon, lat), at(lon, lat + 1)), (at(lon, lat + 1), at(lon, lat))]
    fold_round = (n_lat - 1) % 2

    def exchange(k):
        def run(first, second):
            mirror = [
                [(at(lon, n_lat - 1), at(k - j - lon, n_lat - 1)) for lon in range(n_lon)] for j in (0, 1)
            ]
            plan = [list(rounds[0]), list(rounds[1])]
            plan[fold_round] += mirror[0]
            axes = ("lon", "lat")
            top = first if fold_round == 0 else second
            return (
                lax.ppermute(first, axes, plan[0]),
                lax.ppermute(second, axes, plan[1]),
                lax.ppermute(top, axes, mirror[1]),
            )

        return run

    turn = lax.div(seam_partner[0], jnp.int32(cols))
    got_a, got_b, got_c = lax.switch(turn, [exchange(k) for k in range(n_lon)], first, second)
    low, up, sent_l, sent_r = pl.pallas_call(
        functools.partial(edge_kernel, fold_round == 0),
        out_shape=[sds((9, chans, cols), BF)] * 2 + [sds((chans, 2 * cols), BF)] * 2,
        in_specs=[smem()] + vmem(6),
        out_specs=vmem(4),
        name="edges",
    )(seam_partner, seam_partner.reshape(n_lon, cols), got_a, got_b, got_c, ft, gt)
    got_l = lax.ppermute(sent_r, "lon", [(i, (i + 1) % n_lon) for i in range(n_lon)])
    got_r = lax.ppermute(sent_l, "lon", [(i, (i - 1) % n_lon) for i in range(n_lon)])

    plain, turned, vecs, up_aug, down_t = pl.pallas_call(
        weight_kernel,
        out_shape=[
            sds((7, chans, LANES), F32),
            sds((7, chans, LANES), F32),
            sds((3, chans, LANES), F32),
            sds((hidden_n, chans + 16), BF),
            sds((hidden_n, chans), BF),
        ],
        in_specs=vmem(7),
        out_specs=vmem(5),
        scratch_shapes=[pltpu.VMEM((2, 7, LANES, LANES), F32)],
        name="weights",
    )(
        depth_weight.transpose(1, 2, 0),
        norm_gain,
        layer_norm_bias,
        layer_scale,
        up_bias,
        up_weight.T,
        down_weight,
    )
    units = rows + 8
    big, small = 2 * chans, 40
    output, grad, kept, passed = pl.pallas_call(
        main_kernel,
        out_shape=[sds((chans, rows, cols), BF)] * 2 + [sds((big + small, LANES), F32)] * 2,
        in_specs=vmem(14),
        out_specs=vmem(4),
        scratch_shapes=[
            pltpu.VMEM(((rows + 12) * chans, cols), F32),
            pltpu.VMEM(((rows + 12) * chans, cols), F32),
            pltpu.VMEM(((rows + 12) * 8, 2 * cols), BF),
            pltpu.VMEM((units * chans, cols), F32),
            pltpu.VMEM((units * chans, cols), F32),
            pltpu.VMEM((units * chans, cols), F32),
            pltpu.VMEM((2, chans * rows, cols), F32),
            pltpu.VMEM((7 * 80, LANES), BF),
            pltpu.VMEM((7 * 48, LANES), BF),
            pltpu.VMEM((7 * 80, 2 * cols), F32),
            pltpu.VMEM((7 * 80, 2 * cols), F32),
            pltpu.VMEM((7 * 48, 2 * cols), F32),
            pltpu.VMEM((chans, hidden_n), F32),
            pltpu.VMEM((chans + 16, hidden_n), F32),
            pltpu.VMEM((3, chans, LANES), F32),
            pltpu.VMEM((chans, LANES), F32),
        ],
        name="block",
    )(
        ft,
        gt,
        low,
        up,
        got_l,
        got_r,
        ocean_mask,
        plain,
        turned,
        vecs,
        up_aug,
        up_weight.T,
        down_weight,
        down_t,
    )

    flip = lambda y, axis, b: lax.ppermute(y, axis, [(i, i ^ b) for i in range(lax.axis_size(axis))])
    total = kept + flip(passed, "lon", 1)
    for axis, b in [("lon", 1 << i) for i in range(1, n_lon.bit_length() - 1)] + [
        ("lat", 1 << i) for i in range(n_lat.bit_length() - 1)
    ]:
        total = total + flip(total, axis, b)
    other = flip(total, "lon", 1)
    g_depth, g_gain, g_bias, g_up, g_up_b, g_down, g_scale = pl.pallas_call(
        finish_kernel,
        out_shape=[
            sds((7, 7, chans), F32),
            sds((chans,), F32),
            sds((chans,), F32),
            sds((chans, hidden_n), F32),
            sds((hidden_n,), F32),
            sds((chans, hidden_n), F32),
            sds((chans,), F32),
        ],
        in_specs=vmem(2),
        out_specs=vmem(7),
        name="finish",
    )(total, other)
    return (
        output[None],
        grad[None],
        g_depth.transpose(2, 0, 1),
        g_gain,
        g_bias,
        g_up.T,
        g_up_b,
        g_down,
        g_scale,
    )


def solution(mesh):
    block = P(None, None, "lat", "lon")
    placed = (block, block, P("lat", "lon")) + (P(),) * 8
    return jax.shard_map(
        shards, mesh=mesh, in_specs=placed, out_specs=(block, block) + (P(),) * 7, check_vma=False
    )
```

```python
import functools
import math

import jax
import jax.numpy as jnp
from jax import lax
from jax.experimental import pallas as pl
from jax.experimental.pallas import tpu as pltpu
from jax.sharding import PartitionSpec as P

BF = jnp.bfloat16
F32 = jnp.float32
LANES = 128
NT = (((1,), (1,)), ((), ()))


def shift(x, amount, axis=1):
    size = x.shape[axis]
    amount %= size
    return x if amount == 0 else pltpu.roll(x, amount, axis)


def lane_iota(shape):
    return lax.broadcasted_iota(jnp.int32, shape, 1)


def pack_kernel(fields, cot, mask, ft, gt, first, second, plane):
    chans, rows, _ = fields.shape
    groups = chans // 8
    sea = mask[...].astype(F32)
    for turn, dst in ((0, ft), (1, gt)):
        for c in range(chans):
            if turn == 0:
                cell = fields[c].astype(F32)
            else:
                cell = cot[c].astype(F32) * sea
            plane[turn, c * rows : (c + 1) * rows, :] = cell
        for r in range(rows):
            parts = [plane[turn, pl.ds(g * 8 * rows + r, 8, stride=rows), :] for g in range(groups)]
            dst[r] = jnp.concatenate(parts, axis=0).astype(BF)

    def edge(dst, top):
        base = rows - 6 if top else 0
        gbase = rows - 3 if top else 0
        dst[0:6] = ft[base : base + 6]
        dst[6:9] = gt[gbase : gbase + 3]

    odd = lax.axis_index("lat") % 2

    @pl.when(odd == 0)
    def _():
        edge(first, True)
        edge(second, False)

    @pl.when(odd == 1)
    def _():
        edge(first, False)
        edge(second, True)


def field_lane(r):
    return LANES * (r // 14) + 6 * (r % 14)


def cot_lane(g):
    return LANES * (g // 11) + 84 + 3 * (g % 11)


def edge_kernel(fold_first, seam, partner, got_a, got_b, got_c, ft, gt, low, up, sent_l, sent_r):
    rows, chans, cols = ft.shape
    n_lon = partner.shape[0]
    x = lax.axis_index("lon")
    z = lax.axis_index("lat")
    odd = z % 2
    top = z == lax.axis_size("lat") - 1

    @pl.when(odd == 1)
    def _():
        low[...] = got_a[...]

    @pl.when(odd == 0)
    def _():
        low[...] = got_b[...]

    @pl.when(top)
    def _():
        got_1 = got_a if fold_first else got_b
        src = lax.broadcasted_iota(jnp.int32, (cols, cols), 0)
        want = jnp.broadcast_to(partner[pl.ds(x, 1), :], (cols, cols))
        near = (seam[0] // cols - x + n_lon) % n_lon
        far = (near + n_lon - 1) % n_lon
        pick_1 = (src + near * cols == want).astype(F32).astype(BF)
        pick_2 = (src + far * cols == want).astype(F32).astype(BF)
        for k in range(9):
            m = 5 - k if k < 6 else 14 - k
            mixed = jnp.dot(got_1[m], pick_1, preferred_element_type=F32)
            mixed = mixed + jnp.dot(got_c[m], pick_2, preferred_element_type=F32)
            up[k] = mixed.astype(BF)

    @pl.when(jnp.logical_not(top) & (odd == 0))
    def _():
        up[...] = got_a[...]

    @pl.when(jnp.logical_not(top) & (odd == 1))
    def _():
        up[...] = got_b[...]

    lane = lane_iota((chans, LANES))
    acc = {key: jnp.zeros((chans, LANES), F32) for key in ((0, 0), (0, 1), (1, 0), (1, 1))}

    def place(side, value, source, lane_to, width):
        half, at = lane_to // LANES, lane_to % LANES
        moved = shift(value, at - source)
        acc[side, half] = jnp.where((lane >= at) & (lane < at + width), moved, acc[side, half])

    for r in range(rows + 12):
        if r < 6:
            value = low[r]
        elif r < rows + 6:
            value = ft[r - 6]
        else:
            value = up[r - rows - 6]
        value = value.astype(F32)
        place(1, value, cols - 6, field_lane(r), 6)
        place(0, value, 0, field_lane(r), 6)
    for r in range(rows + 6):
        if r < 3:
            value = low[6 + r]
        elif r < rows + 3:
            value = gt[r - 3]
        else:
            value = up[6 + r - rows - 3]
        value = value.astype(F32)
        place(1, value, cols - 3, cot_lane(r), 3)
        place(0, value, 0, cot_lane(r), 3)
    for side, dst in ((0, sent_l), (1, sent_r)):
        dst[...] = jnp.concatenate([acc[side, 0], acc[side, 1]], axis=1).astype(BF)


def weight_kernel(taps, gain, bias, scale, up_b, up_t, down, plain, turned, vecs, up_aug, down_t, line):
    chans, hidden_n = up_t.shape
    line[...] = jnp.zeros_like(line)
    for a in range(7):
        block = taps[a].astype(F32)
        for q in range(7):
            line[0, q, 8 * a : 8 * a + 1, 0:chans] = block[q : q + 1]
            line[1, 6 - q, 48 - 8 * a : 49 - 8 * a, 0:chans] = block[q : q + 1]
    for q in range(7):
        plain[q] = line[0, q].T[:chans]
        turned[q] = line[1, q].T[:chans]
    wide = LANES - chans
    columns = jnp.concatenate(
        [v[...].astype(F32).reshape(1, chans) for v in (gain, bias, scale)] + [jnp.zeros((5, chans), F32)],
        axis=0,
    )
    columns = jnp.concatenate([columns, jnp.zeros((8, wide), F32)], axis=1).T
    for k in range(3):
        vecs[k] = jnp.broadcast_to(columns[:chans, k : k + 1], (chans, LANES))
    tall = jnp.concatenate(
        [
            up_t[...].astype(F32),
            up_b[...].astype(F32).reshape(1, hidden_n),
            jnp.zeros((wide - 1, hidden_n), F32),
        ],
        axis=0,
    )
    up_aug[...] = tall.T[:, : chans + 16].astype(BF)
    tall = jnp.concatenate([down[...].astype(F32), jnp.zeros((wide, hidden_n), F32)], axis=0)
    down_t[...] = tall.T[:, :chans].astype(BF)


def normal_terms(v):
    cdf = 0.5 * (1.0 + lax.erf(v * (1.0 / math.sqrt(2.0))))
    dens = jnp.exp2(v * v * (-0.5 / math.log(2.0)) - 0.5 * math.log2(2.0 * math.pi))
    return cdf, dens


def main_kernel(
    ft,
    gt,
    low,
    up,
    got_l,
    got_r,
    mask,
    plain,
    turned,
    vecs,
    up_aug,
    up_t,
    down,
    down_t,
    out,
    grad,
    kept,
    passed,
    ext,
    rim,
    rhs,
    conv,
    cots,
    dcv,
    plane,
    band,
    band_up,
    prod_1,
    prod_2,
    prod_3,
    g_down,
    g_up,
    sums,
    taps_g,
):
    rows, chans, cols = ft.shape
    groups = chans // 8
    mid = rows + 6
    odd_core = lax.axis_index("lon") % 2
    top = lax.axis_index("lat") == lax.axis_size("lat") - 1
    lane = lane_iota((8, LANES))
    wide = slice(0, LANES), slice(LANES, 2 * LANES)

    for r in range(rows):
        cots[(r + 3) * chans : (r + 4) * chans, :] = gt[r].astype(F32)
    for r in range(3):
        cots[r * chans : (r + 1) * chans, :] = low[6 + r].astype(F32)
        cots[(rows + 3 + r) * chans : (rows + 4 + r) * chans, :] = up[6 + r].astype(F32)
    lane_c = lane_iota((chans, LANES))
    for k, got in ((0, got_l), (1, got_r)):
        first = shift(got[:, wide[0]].astype(F32), -84)
        second = shift(got[:, wide[1]].astype(F32), 33 - 84)
        value = jnp.where(lane_c < 33, first, jnp.where(lane_c < 3 * mid, second, 0.0))
        cots[(mid + k) * chans : (mid + k + 1) * chans, :] = value

    def edge_mask(s):
        return lane < s if s > 0 else lane >= LANES + s

    def at_row(r, g):
        return pl.ds(pl.multiple_of(r * chans + g * 8, 8), 8)

    def conv_group(g, _):
        at = pl.ds(pl.multiple_of(g * 8, 8), 8)
        left = [got_l[at, w].astype(F32) for w in wide]
        right = [got_r[at, w].astype(F32) for w in wide]
        for r0 in range(0, rows + 12, 2):
            pair = []
            for r in (r0, r0 + 1):
                if r < 6:
                    value = low[r, at, :]
                elif r < rows + 6:
                    value = ft[r - 6, at, :]
                else:
                    value = up[r - rows - 6, at, :]
                value = value.astype(F32)
                half, start = field_lane(r) // LANES, field_lane(r) % LANES
                beyond = jnp.where(lane < 64, shift(right[half], -start), shift(left[half], LANES - 6 - start))
                ext[at_row(r, g), :] = value
                rim[at_row(r, g), :] = beyond
                pair.append(jnp.concatenate([value, beyond], axis=1))
            rhs[8 * r0 : 8 * r0 + 16, :] = jnp.concatenate(pair, axis=0).astype(BF)
        for q in range(7):
            one, two = plain[q, at, :], turned[q, at, :]
            above = jnp.where(top, two, one)
            band[q * 80 : q * 80 + 80, :] = jnp.concatenate(
                [pltpu.roll(one, 8 * i, 1, stride=1, stride_axis=0) for i in range(10)], axis=0
            ).astype(BF)
            band_up[q * 32 : q * 32 + 32, :] = jnp.concatenate(
                [pltpu.roll(above, 8 * i, 1, stride=1, stride_axis=0) for i in range(6, 10)], axis=0
            ).astype(BF)
        prod_1[...] = jnp.dot(band[...], rhs[0:128, :], preferred_element_type=F32)
        prod_2[...] = jnp.dot(band[...], rhs[80:208, :], preferred_element_type=F32)
        prod_3[0:224, :] = jnp.dot(band_up[0:224, :], rhs[96:224, :], preferred_element_type=F32)
        sides = [jnp.zeros((8, LANES), F32)] * 2
        for o in range(mid):
            if o < 10:
                prod, step, i = prod_1, 80, o
            elif o < rows + 3:
                prod, step, i = prod_2, 80, o - 10
            else:
                prod, step, i = prod_3, 32, o - 18
            inner = outer = None
            for q in range(7):
                part = slice(q * step + 8 * i, q * step + 8 * i + 8)
                mine, edge = prod[part, wide[0]], prod[part, wide[1]]
                if q != 3:
                    swap = edge_mask(q - 3)
                    mine, edge = jnp.where(swap, edge, mine), jnp.where(swap, mine, edge)
                    mine, edge = shift(mine, 3 - q), shift(edge, 3 - q)
                inner = mine if inner is None else inner + mine
                outer = edge if outer is None else outer + edge
            conv[at_row(o, g), :] = inner
            inside = (lane >= 3 * o) & (lane < 3 * o + 3)
            sides[0] = jnp.where(inside, shift(outer, 3 * o + 3), sides[0])
            sides[1] = jnp.where(inside, shift(outer, 3 * o), sides[1])
        for k in (0, 1):
            conv[at_row(mid + k, g), :] = sides[k]
        return 0

    lax.fori_loop(0, groups, conv_group, 0)

    g_down[...] = jnp.zeros_like(g_down)
    g_up[...] = jnp.zeros_like(g_up)
    sums[...] = jnp.zeros_like(sums)
    pad_rows = up_aug.shape[1] - chans
    ones = (lax.broadcasted_iota(jnp.int32, (pad_rows, 2 * LANES), 0) == 0).astype(F32).astype(BF)

    def twice(x):
        return jnp.concatenate([x, x], axis=1)

    def unit(u):
        return pl.ds(pl.multiple_of(u * chans, chans), chans)

    def pair_of(ref, units):
        return jnp.concatenate([ref[unit(u), :] for u in units], axis=1)

    def block(units, own):
        gain, bias, scale = twice(vecs[0]), twice(vecs[1]), twice(vecs[2])
        x = pair_of(conv, units)
        centred = x - jnp.mean(x, axis=0, keepdims=True)
        var = jnp.mean(centred * centred, axis=0, keepdims=True)
        rstd = lax.rsqrt(var + 1e-06)
        xhat = centred * rstd
        normed = (xhat * gain + bias).astype(BF)
        normed = jnp.concatenate([normed, ones], axis=0)
        pre = jnp.dot(up_aug[...], normed, preferred_element_type=F32)
        cdf, dens = normal_terms(pre)
        g = pair_of(cots, units)
        d_branch = (g * scale).astype(BF)
        d_hidden = jnp.dot(down_t[...], d_branch, preferred_element_type=F32)
        d_pre = (d_hidden * (cdf + pre * dens)).astype(BF)
        d_normed = jnp.dot(up_t[...], d_pre, preferred_element_type=F32)
        if own:
            hidden = (pre * cdf).astype(BF)
            branch = jnp.dot(down[...], hidden, preferred_element_type=F32)
            sea = [mask[pl.ds(u - 3, 1), :].astype(F32) for u in units]
            fields = jnp.concatenate([ext[unit(u + 3), :] for u in units], axis=1)
            res = (fields + scale * branch) * jnp.concatenate(sea, axis=1)
            for k, u in enumerate(units):
                for gr in range(groups):
                    plane[0, pl.ds(gr * 8 * rows + u - 3, 8, stride=rows), :] = res[gr * 8 : gr * 8 + 8, wide[k]]
            g_down[...] += lax.dot_general(d_branch, hidden, NT, preferred_element_type=F32)
            g_up[...] += lax.dot_general(normed, d_pre, NT, preferred_element_type=F32)
            for k, value in enumerate((d_normed * xhat, d_normed, g * branch)):
                sums[k] += value[:, :LANES] + value[:, LANES:]
        gd = d_normed * gain
        m1 = jnp.mean(gd, axis=0, keepdims=True)
        m2 = jnp.mean(gd * xhat, axis=0, keepdims=True)
        dx = (rstd * (gd - m1 - xhat * m2)).astype(BF).astype(F32)
        for k, u in enumerate(units):
            dcv[unit(u), :] = dx[:, wide[k]]

    def own_block(b, _):
        block((b * 2 + 3, b * 2 + 4), True)
        return 0

    def halo_block(b, _):
        one = jnp.where(b < 2, 2 * b, rows + 2 * b)
        two = jnp.where(b == 0, 1, rows + 1 + 2 * b)
        block((one, two), False)
        return 0

    lax.fori_loop(0, rows // 2, own_block, 0)
    lax.fori_loop(0, 4, halo_block, 0)

    def adjoint_group(g, _):
        at = pl.ds(pl.multiple_of(g * 8, 8), 8)
        left, right = dcv[at_row(mid, g), :], dcv[at_row(mid + 1, g), :]
        for r0 in range(0, mid, 2):
            pair = []
            for r in (r0, r0 + 1):
                value = dcv[at_row(r, g), :]
                beyond = jnp.where(lane < 64, shift(right, -3 * r), shift(left, LANES - 3 - 3 * r))
                pair.append(jnp.concatenate([value, beyond], axis=1))
            rhs[8 * r0 : 8 * r0 + 16, :] = jnp.concatenate(pair, axis=0).astype(BF)
        for q in range(7):
            one, two = turned[q, at, :], plain[q, at, :]
            above = jnp.where(top, two, one)
            moved = [pltpu.roll(one, 8 * i, 1, stride=1, stride_axis=0) for i in range(10)]
            band[q * 80 : q * 80 + 80, :] = jnp.concatenate(moved, axis=0).astype(BF)
            late = moved[:3]
            for i in range(3, 6):
                other = pltpu.roll(above, 8 * i, 1, stride=1, stride_axis=0)
                late.append(jnp.where(lane >= 8 * (rows + 3 - 10), other, moved[i]))
            band_up[q * 48 : q * 48 + 48, :] = jnp.concatenate(late, axis=0).astype(BF)
        prod_1[...] = jnp.dot(band[...], rhs[0:128, :], preferred_element_type=F32)
        prod_3[...] = jnp.dot(band_up[:, 0:96], rhs[80:176, :], preferred_element_type=F32)
        for o in range(rows):
            prod, step, i = (prod_1, 80, o) if o < 10 else (prod_3, 48, o - 10)
            inner = cots[at_row(o + 3, g), :]
            for q in range(7):
                part = slice(q * step + 8 * i, q * step + 8 * i + 8)
                mine = prod[part, wide[0]]
                if q != 3:
                    mine = shift(jnp.where(edge_mask(q - 3), prod[part, wide[1]], mine), 3 - q)
                inner = inner + mine
            plane[1, pl.ds(g * (8 * rows) + o, 8, stride=rows), :] = inner
        line = jnp.zeros((8, LANES), F32)
        for q in range(7):
            own = [shift(dcv[at_row(o + 3, g), :], q - 3) for o in range(rows)]
            tot = [None] * 7
            for r in range(mid):
                value = ext[at_row(r + 3, g), :]
                if q != 3:
                    value = jnp.where(edge_mask(q - 3), rim[at_row(r + 3, g), :], value)
                for a in range(7):
                    o = r - a
                    if 0 <= o < rows:
                        term = value * own[o]
                        tot[a] = term if tot[a] is None else tot[a] + term
            for a in range(7):
                total = jnp.sum(tot[a], axis=1, keepdims=True)
                line = jnp.where(lane == 8 * a + q, total, line)
        for k in range(3):
            total = jnp.sum(sums[k, at, :], axis=1, keepdims=True)
            line = jnp.where(lane == 56 + k, total, line)
        taps_g[at, :] = line
        return 0

    lax.fori_loop(0, groups, adjoint_group, 0)
    small = taps_g[...]
    cut = 40

    def fill(lower, upper):
        for h, w in enumerate(wide):
            lower[h * chans : (h + 1) * chans, :] = g_down[:, w]
            upper[h * chans : (h + 1) * chans, :] = g_up[0:chans, w]
            upper[2 * chans + 24 + 8 * h : 2 * chans + 32 + 8 * h, :] = g_up[chans : chans + 8, w]
        lower[2 * chans : 2 * chans + cut, :] = small[:cut]
        upper[2 * chans : 2 * chans + 24, :] = small[cut:]

    @pl.when(odd_core == 0)
    def _():
        fill(kept, passed)

    @pl.when(odd_core == 1)
    def _():
        fill(passed, kept)

    for c in range(chans):
        out[c] = plane[0, c * rows : (c + 1) * rows, :].astype(BF)
        grad[c] = plane[1, c * rows : (c + 1) * rows, :].astype(BF)


def finish_kernel(total, other, g_depth, g_gain, g_bias, g_up, g_up_b, g_down, g_scale):
    chans, hidden_n = g_down.shape

    def unpack(lower, upper):
        for h in range(hidden_n // LANES):
            w = slice(h * LANES, (h + 1) * LANES)
            g_down[:, w] = lower[h * chans : (h + 1) * chans, :]
            g_up[:, w] = upper[h * chans : (h + 1) * chans, :]
            at = 2 * chans + 24 + 8 * h
            g_up_b[w] = upper[at : at + 1, :].reshape(LANES)
        small = jnp.concatenate(
            [
                lower[2 * chans : 2 * chans + 40, :],
                upper[2 * chans : 2 * chans + 24, :],
                jnp.zeros((LANES - chans, LANES), F32),
            ],
            axis=0,
        ).T
        for k, dst in enumerate((g_gain, g_bias, g_scale)):
            dst[...] = small[56 + k : 57 + k, :chans].reshape(chans)
        for a in range(7):
            g_depth[a] = small[8 * a : 8 * a + 7, :chans]

    odd_core = lax.axis_index("lon") % 2

    @pl.when(odd_core == 0)
    def _():
        unpack(total, other)

    @pl.when(odd_core == 1)
    def _():
        unpack(other, total)


def vmem(n):
    return [pl.BlockSpec(memory_space=pltpu.VMEM)] * n


def smem():
    return pl.BlockSpec(memory_space=pltpu.SMEM)


def shards(
    fields,
    cotangent,
    ocean_mask,
    seam_partner,
    depth_weight,
    norm_gain,
    layer_norm_bias,
    up_weight,
    up_bias,
    down_weight,
    layer_scale,
):
    _, chans, rows, cols = fields.shape
    hidden_n = up_weight.shape[0]
    n_lon, n_lat = lax.axis_size("lon"), lax.axis_size("lat")
    sds = jax.ShapeDtypeStruct
    ft, gt, first, second = pl.pallas_call(
        pack_kernel,
        out_shape=[sds((rows, chans, cols), BF)] * 2 + [sds((9, chans, cols), BF)] * 2,
        in_specs=vmem(3),
        out_specs=vmem(4),
        scratch_shapes=[pltpu.VMEM((2, chans * rows, cols), F32)],
        compiler_params=pltpu.CompilerParams(vmem_limit_bytes=8 * 2**20),
        name="pack",
    )(fields[0], cotangent[0], ocean_mask)

    at = lambda lon, lat: (lon % n_lon) * n_lat + lat
    rounds = [[], []]
    for lat in range(n_lat - 1):
        for lon in range(n_lon):
            rounds[lat % 2] += [(at(lon, lat), at(lon, lat + 1)), (at(lon, lat + 1), at(lon, lat))]
    fold_round = (n_lat - 1) % 2

    axes = ("lon", "lat")
    plain_round = 1 - fold_round
    sends = (first, second)
    met = lax.ppermute(sends[plain_round], axes, rounds[plain_round])
    seam, top = lax.optimization_barrier((seam_partner, sends[fold_round]))

    def exchange(k):
        def run(top):
            mirror = [
                [(at(lon, n_lat - 1), at(k - j - lon, n_lat - 1)) for lon in range(n_lon)] for j in (0, 1)
            ]
            plan = rounds[fold_round] + mirror[0]
            return lax.ppermute(top, axes, plan), lax.ppermute(top, axes, mirror[1])

        return run

    turn = lax.div(seam[0], jnp.int32(cols))
    folded, got_c = lax.switch(turn, [exchange(k) for k in range(n_lon)], top)
    got_a, got_b = (folded, met) if fold_round == 0 else (met, folded)
    low, up, sent_l, sent_r = pl.pallas_call(
        functools.partial(edge_kernel, fold_round == 0),
        out_shape=[sds((9, chans, cols), BF)] * 2 + [sds((chans, 2 * cols), BF)] * 2,
        in_specs=[smem()] + vmem(6),
        out_specs=vmem(4),
        compiler_params=pltpu.CompilerParams(vmem_limit_bytes=8 * 2**20),
        name="edges",
    )(seam_partner, seam_partner.reshape(n_lon, cols), got_a, got_b, got_c, ft, gt)
    got_l = lax.ppermute(sent_r, "lon", [(i, (i + 1) % n_lon) for i in range(n_lon)])
    got_r = lax.ppermute(sent_l, "lon", [(i, (i - 1) % n_lon) for i in range(n_lon)])

    plain, turned, vecs, up_aug, down_t = pl.pallas_call(
        weight_kernel,
        out_shape=[
            sds((7, chans, LANES), F32),
            sds((7, chans, LANES), F32),
            sds((3, chans, LANES), F32),
            sds((hidden_n, chans + 16), BF),
            sds((hidden_n, chans), BF),
        ],
        in_specs=vmem(7),
        out_specs=vmem(5),
        scratch_shapes=[pltpu.VMEM((2, 7, LANES, LANES), F32)],
        compiler_params=pltpu.CompilerParams(vmem_limit_bytes=8 * 2**20),
        name="weights",
    )(
        depth_weight.transpose(1, 2, 0),
        norm_gain,
        layer_norm_bias,
        layer_scale,
        up_bias,
        up_weight.T,
        down_weight,
    )
    units = rows + 8
    big, small = 2 * chans, 40
    output, grad, kept, passed = pl.pallas_call(
        main_kernel,
        out_shape=[sds((chans, rows, cols), BF)] * 2 + [sds((big + small, LANES), F32)] * 2,
        in_specs=vmem(14),
        out_specs=vmem(4),
        scratch_shapes=[
            pltpu.VMEM(((rows + 12) * chans, cols), F32),
            pltpu.VMEM(((rows + 12) * chans, cols), F32),
            pltpu.VMEM(((rows + 12) * 8, 2 * cols), BF),
            pltpu.VMEM((units * chans, cols), F32),
            pltpu.VMEM((units * chans, cols), F32),
            pltpu.VMEM((units * chans, cols), F32),
            pltpu.VMEM((2, chans * rows, cols), F32),
            pltpu.VMEM((7 * 80, LANES), BF),
            pltpu.VMEM((7 * 48, LANES), BF),
            pltpu.VMEM((7 * 80, 2 * cols), F32),
            pltpu.VMEM((7 * 80, 2 * cols), F32),
            pltpu.VMEM((7 * 48, 2 * cols), F32),
            pltpu.VMEM((chans, hidden_n), F32),
            pltpu.VMEM((chans + 16, hidden_n), F32),
            pltpu.VMEM((3, chans, LANES), F32),
            pltpu.VMEM((chans, LANES), F32),
        ],
        compiler_params=pltpu.CompilerParams(vmem_limit_bytes=20 * 2**20),
        name="block",
    )(
        ft,
        gt,
        low,
        up,
        got_l,
        got_r,
        ocean_mask,
        plain,
        turned,
        vecs,
        up_aug,
        up_weight.T,
        down_weight,
        down_t,
    )

    flip = lambda y, axis, b: lax.ppermute(y, axis, [(i, i ^ b) for i in range(lax.axis_size(axis))])
    total = kept + flip(passed, "lon", 1)
    for axis, b in [("lon", 1 << i) for i in range(1, n_lon.bit_length() - 1)] + [
        ("lat", 1 << i) for i in range(n_lat.bit_length() - 1)
    ]:
        total = total + flip(total, axis, b)
    other = flip(total, "lon", 1)
    g_depth, g_gain, g_bias, g_up, g_up_b, g_down, g_scale = pl.pallas_call(
        finish_kernel,
        out_shape=[
            sds((7, 7, chans), F32),
            sds((chans,), F32),
            sds((chans,), F32),
            sds((chans, hidden_n), F32),
            sds((hidden_n,), F32),
            sds((chans, hidden_n), F32),
            sds((chans,), F32),
        ],
        in_specs=vmem(2),
        out_specs=vmem(7),
        compiler_params=pltpu.CompilerParams(vmem_limit_bytes=6 * 2**20),
        name="finish",
    )(total, other)
    return (
        output[None],
        grad[None],
        g_depth.transpose(2, 0, 1),
        g_gain,
        g_bias,
        g_up.T,
        g_up_b,
        g_down,
        g_scale,
    )


def solution(mesh):
    block = P(None, None, "lat", "lon")
    placed = (block, block, P("lat", "lon")) + (P(),) * 8
    return jax.shard_map(
        shards, mesh=mesh, in_specs=placed, out_specs=(block, block) + (P(),) * 7, check_vma=False
    )
```

```python
import functools
import math

import jax
import jax.numpy as jnp
from jax import lax
from jax.experimental import pallas as pl
from jax.experimental.pallas import tpu as pltpu
from jax.sharding import PartitionSpec as P

BF = jnp.bfloat16
F32 = jnp.float32
LANES = 128
NT = (((1,), (1,)), ((), ()))


def shift(x, amount, axis=1):
    size = x.shape[axis]
    amount %= size
    return x if amount == 0 else pltpu.roll(x, amount, axis)


def lane_iota(shape):
    return lax.broadcasted_iota(jnp.int32, shape, 1)


def pack_kernel(fields_far, cot_far, mask_far, ft, gt, first, second, plane, fields, cot, mask, arrived):
    chans, rows, _ = fields.shape
    groups = chans // 8
    pairs = ((fields_far, fields), (cot_far, cot), (mask_far, mask))
    copies = [pltpu.make_async_copy(src, dst, arrived.at[k]) for k, (src, dst) in enumerate(pairs)]
    for copy in copies:
        copy.start()
    for turn, dst in ((0, ft), (1, gt)):
        copies[turn].wait()
        if turn == 1:
            copies[2].wait()
            sea = mask[...].astype(F32)
        for c in range(chans):
            if turn == 0:
                cell = fields[c].astype(F32)
            else:
                cell = cot[c].astype(F32) * sea
            plane[turn, c * rows : (c + 1) * rows, :] = cell
        for r in range(rows):
            parts = [plane[turn, pl.ds(g * 8 * rows + r, 8, stride=rows), :] for g in range(groups)]
            dst[r] = jnp.concatenate(parts, axis=0).astype(BF)

    def edge(dst, top):
        base = rows - 6 if top else 0
        gbase = rows - 3 if top else 0
        dst[0:6] = ft[base : base + 6]
        dst[6:9] = gt[gbase : gbase + 3]

    odd = lax.axis_index("lat") % 2

    @pl.when(odd == 0)
    def _():
        edge(first, True)
        edge(second, False)

    @pl.when(odd == 1)
    def _():
        edge(first, False)
        edge(second, True)


def field_lane(r):
    return LANES * (r // 14) + 6 * (r % 14)


def cot_lane(g):
    return LANES * (g // 11) + 84 + 3 * (g % 11)


def edge_kernel(fold_first, seam, partner, got_a, got_b, got_c, ft, gt, low, up, sent_l, sent_r):
    rows, chans, cols = ft.shape
    n_lon = partner.shape[0]
    x = lax.axis_index("lon")
    z = lax.axis_index("lat")
    odd = z % 2
    top = z == lax.axis_size("lat") - 1

    @pl.when(odd == 1)
    def _():
        low[...] = got_a[...]

    @pl.when(odd == 0)
    def _():
        low[...] = got_b[...]

    @pl.when(top)
    def _():
        got_1 = got_a if fold_first else got_b
        src = lax.broadcasted_iota(jnp.int32, (cols, cols), 0)
        want = jnp.broadcast_to(partner[pl.ds(x, 1), :], (cols, cols))
        near = (seam[0] // cols - x + n_lon) % n_lon
        far = (near + n_lon - 1) % n_lon
        pick_1 = (src + near * cols == want).astype(F32).astype(BF)
        pick_2 = (src + far * cols == want).astype(F32).astype(BF)
        for k in range(9):
            m = 5 - k if k < 6 else 14 - k
            mixed = jnp.dot(got_1[m], pick_1, preferred_element_type=F32)
            mixed = mixed + jnp.dot(got_c[m], pick_2, preferred_element_type=F32)
            up[k] = mixed.astype(BF)

    @pl.when(jnp.logical_not(top) & (odd == 0))
    def _():
        up[...] = got_a[...]

    @pl.when(jnp.logical_not(top) & (odd == 1))
    def _():
        up[...] = got_b[...]

    lane = lane_iota((chans, LANES))
    acc = {key: jnp.zeros((chans, LANES), F32) for key in ((0, 0), (0, 1), (1, 0), (1, 1))}

    def place(side, value, source, lane_to, width):
        half, at = lane_to // LANES, lane_to % LANES
        moved = shift(value, at - source)
        acc[side, half] = jnp.where((lane >= at) & (lane < at + width), moved, acc[side, half])

    for r in range(rows + 12):
        if r < 6:
            value = low[r]
        elif r < rows + 6:
            value = ft[r - 6]
        else:
            value = up[r - rows - 6]
        value = value.astype(F32)
        place(1, value, cols - 6, field_lane(r), 6)
        place(0, value, 0, field_lane(r), 6)
    for r in range(rows + 6):
        if r < 3:
            value = low[6 + r]
        elif r < rows + 3:
            value = gt[r - 3]
        else:
            value = up[6 + r - rows - 3]
        value = value.astype(F32)
        place(1, value, cols - 3, cot_lane(r), 3)
        place(0, value, 0, cot_lane(r), 3)
    for side, dst in ((0, sent_l), (1, sent_r)):
        dst[...] = jnp.concatenate([acc[side, 0], acc[side, 1]], axis=1).astype(BF)


def weight_kernel(taps, gain, bias, scale, up_b, up_t, down, plain, turned, vecs, up_aug, down_t, line):
    chans, hidden_n = up_t.shape
    line[...] = jnp.zeros_like(line)
    for a in range(7):
        block = taps[a].astype(F32)
        for q in range(7):
            line[0, q, 8 * a : 8 * a + 1, 0:chans] = block[q : q + 1]
            line[1, 6 - q, 48 - 8 * a : 49 - 8 * a, 0:chans] = block[q : q + 1]
    for q in range(7):
        plain[q] = line[0, q].T[:chans]
        turned[q] = line[1, q].T[:chans]
    wide = LANES - chans
    columns = jnp.concatenate(
        [v[...].astype(F32).reshape(1, chans) for v in (gain, bias, scale)] + [jnp.zeros((5, chans), F32)],
        axis=0,
    )
    columns = jnp.concatenate([columns, jnp.zeros((8, wide), F32)], axis=1).T
    for k in range(3):
        vecs[k] = jnp.broadcast_to(columns[:chans, k : k + 1], (chans, LANES))
    tall = jnp.concatenate(
        [
            up_t[...].astype(F32),
            up_b[...].astype(F32).reshape(1, hidden_n),
            jnp.zeros((wide - 1, hidden_n), F32),
        ],
        axis=0,
    )
    up_aug[...] = tall.T[:, : chans + 16].astype(BF)
    tall = jnp.concatenate([down[...].astype(F32), jnp.zeros((wide, hidden_n), F32)], axis=0)
    down_t[...] = tall.T[:, :chans].astype(BF)


def normal_terms(v):
    cdf = 0.5 * (1.0 + lax.erf(v * (1.0 / math.sqrt(2.0))))
    dens = jnp.exp2(v * v * (-0.5 / math.log(2.0)) - 0.5 * math.log2(2.0 * math.pi))
    return cdf, dens


def edge_mask(lane, s):
    return lane < s if s > 0 else lane >= LANES + s


def rows_of(r, g, chans):
    return pl.ds(pl.multiple_of(r * chans + g * 8, 8), 8)


def twice(x):
    return jnp.concatenate([x, x], axis=1)


def norm_and_back(x, g, vecs, up_aug, up_t, down_t):
    gain, bias, scale = twice(vecs[0]), twice(vecs[1]), twice(vecs[2])
    centred = x - jnp.mean(x, axis=0, keepdims=True)
    var = jnp.mean(centred * centred, axis=0, keepdims=True)
    rstd = lax.rsqrt(var + 1e-06)
    xhat = centred * rstd
    pad = (up_aug.shape[1] - x.shape[0], x.shape[1])
    ones = (lax.broadcasted_iota(jnp.int32, pad, 0) == 0).astype(F32).astype(BF)
    normed = jnp.concatenate([(xhat * gain + bias).astype(BF), ones], axis=0)
    pre = jnp.dot(up_aug[...], normed, preferred_element_type=F32)
    cdf, dens = normal_terms(pre)
    d_branch = (g * scale).astype(BF)
    d_hidden = jnp.dot(down_t[...], d_branch, preferred_element_type=F32)
    d_pre = (d_hidden * (cdf + pre * dens)).astype(BF)
    d_normed = jnp.dot(up_t[...], d_pre, preferred_element_type=F32)
    gd = d_normed * gain
    m1 = jnp.mean(gd, axis=0, keepdims=True)
    m2 = jnp.mean(gd * xhat, axis=0, keepdims=True)
    dx = (rstd * (gd - m1 - xhat * m2)).astype(BF).astype(F32)
    return dx, (pre, cdf, d_branch, d_pre, d_normed, normed, xhat, scale)


def own_kernel(
    ft,
    gt,
    low,
    up,
    got_l,
    got_r,
    mask,
    plain,
    turned,
    vecs,
    up_aug,
    up_t,
    down,
    down_t,
    out,
    conv_halo,
    dcv,
    kept,
    passed,
    ext,
    rim,
    rhs,
    conv,
    plane,
    band,
    band_up,
    prod_1,
    prod_2,
    prod_3,
    g_down,
    g_up,
    sums,
    taps_g,
):
    rows, chans, cols = ft.shape
    groups = chans // 8
    mid = rows + 6
    odd_core = lax.axis_index("lon") % 2
    top = lax.axis_index("lat") == lax.axis_size("lat") - 1
    lane = lane_iota((8, LANES))
    wide = slice(0, LANES), slice(LANES, 2 * LANES)
    at_row = lambda r, g: rows_of(r, g, chans)

    def conv_group(g, _):
        at = pl.ds(pl.multiple_of(g * 8, 8), 8)
        left = [got_l[at, w].astype(F32) for w in wide]
        right = [got_r[at, w].astype(F32) for w in wide]
        for r0 in range(0, rows + 12, 2):
            pair = []
            for r in (r0, r0 + 1):
                if r < 6:
                    value = low[r, at, :]
                elif r < rows + 6:
                    value = ft[r - 6, at, :]
                else:
                    value = up[r - rows - 6, at, :]
                value = value.astype(F32)
                half, start = field_lane(r) // LANES, field_lane(r) % LANES
                beyond = jnp.where(lane < 64, shift(right[half], -start), shift(left[half], LANES - 6 - start))
                ext[at_row(r, g), :] = value
                rim[at_row(r, g), :] = beyond
                pair.append(jnp.concatenate([value, beyond], axis=1))
            rhs[8 * r0 : 8 * r0 + 16, :] = jnp.concatenate(pair, axis=0).astype(BF)
        for q in range(7):
            one, two = plain[q, at, :], turned[q, at, :]
            above = jnp.where(top, two, one)
            band[q * 80 : q * 80 + 80, :] = jnp.concatenate(
                [pltpu.roll(one, 8 * i, 1, stride=1, stride_axis=0) for i in range(10)], axis=0
            ).astype(BF)
            band_up[q * 32 : q * 32 + 32, :] = jnp.concatenate(
                [pltpu.roll(above, 8 * i, 1, stride=1, stride_axis=0) for i in range(6, 10)], axis=0
            ).astype(BF)
        prod_1[...] = jnp.dot(band[...], rhs[0:128, :], preferred_element_type=F32)
        prod_2[...] = jnp.dot(band[...], rhs[80:208, :], preferred_element_type=F32)
        prod_3[0:224, :] = jnp.dot(band_up[0:224, :], rhs[96:224, :], preferred_element_type=F32)
        sides = [jnp.zeros((8, LANES), F32)] * 2
        for o in range(mid):
            if o < 10:
                prod, step, i = prod_1, 80, o
            elif o < rows + 3:
                prod, step, i = prod_2, 80, o - 10
            else:
                prod, step, i = prod_3, 32, o - 18
            inner = outer = None
            for q in range(7):
                part = slice(q * step + 8 * i, q * step + 8 * i + 8)
                mine, edge = prod[part, wide[0]], prod[part, wide[1]]
                if q != 3:
                    swap = edge_mask(lane, q - 3)
                    mine, edge = jnp.where(swap, edge, mine), jnp.where(swap, mine, edge)
                    mine, edge = shift(mine, 3 - q), shift(edge, 3 - q)
                inner = mine if inner is None else inner + mine
                outer = edge if outer is None else outer + edge
            if o < 3:
                conv_halo[at_row(o, g), :] = inner
            elif o < rows + 3:
                conv[at_row(o - 3, g), :] = inner
            else:
                conv_halo[at_row(o - rows, g), :] = inner
            inside = (lane >= 3 * o) & (lane < 3 * o + 3)
            sides[0] = jnp.where(inside, shift(outer, 3 * o + 3), sides[0])
            sides[1] = jnp.where(inside, shift(outer, 3 * o), sides[1])
        for k in (0, 1):
            conv_halo[at_row(6 + k, g), :] = sides[k]
        return 0

    lax.fori_loop(0, groups, conv_group, 0)

    g_down[...] = jnp.zeros_like(g_down)
    g_up[...] = jnp.zeros_like(g_up)
    sums[...] = jnp.zeros_like(sums)

    def unit(u):
        return pl.ds(pl.multiple_of(u * chans, chans), chans)

    def own_block(b, _):
        units = (b * 2, b * 2 + 1)
        x = jnp.concatenate([conv[unit(u), :] for u in units], axis=1)
        g = jnp.concatenate([gt[u].astype(F32) for u in units], axis=1)
        dx, (pre, cdf, d_branch, d_pre, d_normed, normed, xhat, scale) = norm_and_back(
            x, g, vecs, up_aug, up_t, down_t
        )
        hidden = (pre * cdf).astype(BF)
        branch = jnp.dot(down[...], hidden, preferred_element_type=F32)
        sea = [mask[pl.ds(u, 1), :].astype(F32) for u in units]
        fields = jnp.concatenate([ft[u].astype(F32) for u in units], axis=1)
        res = (fields + scale * branch) * jnp.concatenate(sea, axis=1)
        for k, u in enumerate(units):
            for gr in range(groups):
                plane[pl.ds(gr * 8 * rows + u, 8, stride=rows), :] = res[gr * 8 : gr * 8 + 8, wide[k]]
            dcv[unit(u), :] = dx[:, wide[k]]
        g_down[...] += lax.dot_general(d_branch, hidden, NT, preferred_element_type=F32)
        g_up[...] += lax.dot_general(normed, d_pre, NT, preferred_element_type=F32)
        for k, value in enumerate((d_normed * xhat, d_normed, g * branch)):
            sums[k] += value[:, :LANES] + value[:, LANES:]
        return 0

    lax.fori_loop(0, rows // 2, own_block, 0)

    def taps_group(g, _):
        at = pl.ds(pl.multiple_of(g * 8, 8), 8)
        line = jnp.zeros((8, LANES), F32)
        for q in range(7):
            own = [shift(dcv[at_row(o, g), :], q - 3) for o in range(rows)]
            tot = [None] * 7
            for r in range(mid):
                value = ext[at_row(r + 3, g), :]
                if q != 3:
                    value = jnp.where(edge_mask(lane, q - 3), rim[at_row(r + 3, g), :], value)
                for a in range(7):
                    o = r - a
                    if 0 <= o < rows:
                        term = value * own[o]
                        tot[a] = term if tot[a] is None else tot[a] + term
            for a in range(7):
                total = jnp.sum(tot[a], axis=1, keepdims=True)
                line = jnp.where(lane == 8 * a + q, total, line)
        for k in range(3):
            total = jnp.sum(sums[k, at, :], axis=1, keepdims=True)
            line = jnp.where(lane == 56 + k, total, line)
        taps_g[at, :] = line
        return 0

    lax.fori_loop(0, groups, taps_group, 0)
    small = taps_g[...]
    cut = 40

    def fill(lower, upper):
        for h, w in enumerate(wide):
            lower[h * chans : (h + 1) * chans, :] = g_down[:, w]
            upper[h * chans : (h + 1) * chans, :] = g_up[0:chans, w]
            upper[2 * chans + 24 + 8 * h : 2 * chans + 32 + 8 * h, :] = g_up[chans : chans + 8, w]
        lower[2 * chans : 2 * chans + cut, :] = small[:cut]
        upper[2 * chans : 2 * chans + 24, :] = small[cut:]

    @pl.when(odd_core == 0)
    def _():
        fill(kept, passed)

    @pl.when(odd_core == 1)
    def _():
        fill(passed, kept)

    for c in range(chans):
        out[c] = plane[c * rows : (c + 1) * rows, :].astype(BF)


def halo_kernel(conv_halo, low, up, got_l, got_r, vecs, up_aug, up_t, down_t, dcv_halo, cots):
    _, chans, _ = low.shape
    lane_c = lane_iota((chans, LANES))
    wide = slice(0, LANES), slice(LANES, 2 * LANES)
    for r in range(3):
        cots[r * chans : (r + 1) * chans, :] = low[6 + r].astype(F32)
        cots[(3 + r) * chans : (4 + r) * chans, :] = up[6 + r].astype(F32)
    for k, got in ((0, got_l), (1, got_r)):
        first = shift(got[:, wide[0]].astype(F32), -84)
        second = shift(got[:, wide[1]].astype(F32), 33 - 84)
        value = jnp.where(lane_c < 33, first, jnp.where(lane_c < 66, second, 0.0))
        cots[(6 + k) * chans : (7 + k) * chans, :] = value

    def halo_block(b, _):
        units = [pl.ds(pl.multiple_of((2 * b + k) * chans, chans), chans) for k in (0, 1)]
        x = jnp.concatenate([conv_halo[u, :] for u in units], axis=1)
        g = jnp.concatenate([cots[u, :] for u in units], axis=1)
        dx, _ = norm_and_back(x, g, vecs, up_aug, up_t, down_t)
        for k, u in enumerate(units):
            dcv_halo[u, :] = dx[:, wide[k]]
        return 0

    lax.fori_loop(0, 4, halo_block, 0)


def adjoint_kernel(part, *refs):
    dcv, dcv_halo, gt, plain, turned = refs[:5]
    grad, rhs, plane, band, band_up, prod_1, prod_3 = refs[-7:]
    rows, chans, cols = gt.shape
    some = grad.shape[0]
    first = part * (some // 8)
    mid = rows + 6
    top = lax.axis_index("lat") == lax.axis_size("lat") - 1
    lane = lane_iota((8, LANES))
    wide = slice(0, LANES), slice(LANES, 2 * LANES)
    at_row = lambda r, g: rows_of(r, g, chans)

    def adjoint_group(g, _):
        at = pl.ds(pl.multiple_of(g * 8, 8), 8)
        left, right = dcv_halo[at_row(6, g), :], dcv_halo[at_row(7, g), :]
        for r0 in range(0, mid, 2):
            pair = []
            for r in (r0, r0 + 1):
                if r < 3:
                    value = dcv_halo[at_row(r, g), :]
                elif r < rows + 3:
                    value = dcv[at_row(r - 3, g), :]
                else:
                    value = dcv_halo[at_row(r - rows, g), :]
                beyond = jnp.where(lane < 64, shift(right, -3 * r), shift(left, LANES - 3 - 3 * r))
                pair.append(jnp.concatenate([value, beyond], axis=1))
            rhs[8 * r0 : 8 * r0 + 16, :] = jnp.concatenate(pair, axis=0).astype(BF)
        for q in range(7):
            one, two = turned[q, at, :], plain[q, at, :]
            above = jnp.where(top, two, one)
            moved = [pltpu.roll(one, 8 * i, 1, stride=1, stride_axis=0) for i in range(10)]
            band[q * 80 : q * 80 + 80, :] = jnp.concatenate(moved, axis=0).astype(BF)
            late = moved[:3]
            for i in range(3, 6):
                other = pltpu.roll(above, 8 * i, 1, stride=1, stride_axis=0)
                late.append(jnp.where(lane >= 8 * (rows + 3 - 10), other, moved[i]))
            band_up[q * 48 : q * 48 + 48, :] = jnp.concatenate(late, axis=0).astype(BF)
        prod_1[...] = jnp.dot(band[...], rhs[0:128, :], preferred_element_type=F32)
        prod_3[...] = jnp.dot(band_up[:, 0:96], rhs[80:176, :], preferred_element_type=F32)
        for o in range(rows):
            prod, step, i = (prod_1, 80, o) if o < 10 else (prod_3, 48, o - 10)
            inner = gt[o, at, :].astype(F32)
            for q in range(7):
                part = slice(q * step + 8 * i, q * step + 8 * i + 8)
                mine = prod[part, wide[0]]
                if q != 3:
                    mine = shift(jnp.where(edge_mask(lane, q - 3), prod[part, wide[1]], mine), 3 - q)
                inner = inner + mine
            plane[pl.ds((g - first) * (8 * rows) + o, 8, stride=rows), :] = inner
        return 0

    lax.fori_loop(first, first + some // 8, adjoint_group, 0)
    for c in range(some):
        grad[c] = plane[c * rows : (c + 1) * rows, :].astype(BF)


def finish_kernel(total, other, g_depth, g_gain, g_bias, g_up, g_up_b, g_down, g_scale):
    chans, hidden_n = g_down.shape

    def unpack(lower, upper):
        for h in range(hidden_n // LANES):
            w = slice(h * LANES, (h + 1) * LANES)
            g_down[:, w] = lower[h * chans : (h + 1) * chans, :]
            g_up[:, w] = upper[h * chans : (h + 1) * chans, :]
            at = 2 * chans + 24 + 8 * h
            g_up_b[w] = upper[at : at + 1, :].reshape(LANES)
        small = jnp.concatenate(
            [
                lower[2 * chans : 2 * chans + 40, :],
                upper[2 * chans : 2 * chans + 24, :],
                jnp.zeros((LANES - chans, LANES), F32),
            ],
            axis=0,
        ).T
        for k, dst in enumerate((g_gain, g_bias, g_scale)):
            dst[...] = small[56 + k : 57 + k, :chans].reshape(chans)
        for a in range(7):
            g_depth[a] = small[8 * a : 8 * a + 7, :chans]

    odd_core = lax.axis_index("lon") % 2

    @pl.when(odd_core == 0)
    def _():
        unpack(total, other)

    @pl.when(odd_core == 1)
    def _():
        unpack(other, total)


def vmem(n):
    return [pl.BlockSpec(memory_space=pltpu.VMEM)] * n


def smem():
    return pl.BlockSpec(memory_space=pltpu.SMEM)


def shards(
    fields,
    cotangent,
    ocean_mask,
    seam_partner,
    depth_weight,
    norm_gain,
    layer_norm_bias,
    up_weight,
    up_bias,
    down_weight,
    layer_scale,
):
    _, chans, rows, cols = fields.shape
    hidden_n = up_weight.shape[0]
    n_lon, n_lat = lax.axis_size("lon"), lax.axis_size("lat")
    sds = jax.ShapeDtypeStruct
    ft, gt, first, second = pl.pallas_call(
        pack_kernel,
        out_shape=[sds((rows, chans, cols), BF)] * 2 + [sds((9, chans, cols), BF)] * 2,
        in_specs=[pl.BlockSpec(memory_space=pltpu.HBM)] * 3,
        out_specs=vmem(4),
        scratch_shapes=[
            pltpu.VMEM((2, chans * rows, cols), F32),
            pltpu.VMEM((chans, rows, cols), BF),
            pltpu.VMEM((chans, rows, cols), BF),
            pltpu.VMEM((rows, cols), jnp.int32),
            pltpu.SemaphoreType.DMA((3,)),
        ],
        compiler_params=pltpu.CompilerParams(vmem_limit_bytes=8 * 2**20),
        name="pack",
    )(*[pltpu.with_memory_space_constraint(v, pltpu.HBM) for v in (fields[0], cotangent[0], ocean_mask)])

    at = lambda lon, lat: (lon % n_lon) * n_lat + lat
    rounds = [[], []]
    for lat in range(n_lat - 1):
        for lon in range(n_lon):
            rounds[lat % 2] += [(at(lon, lat), at(lon, lat + 1)), (at(lon, lat + 1), at(lon, lat))]
    fold_round = (n_lat - 1) % 2

    axes = ("lon", "lat")
    plain_round = 1 - fold_round
    sends = (first, second)
    met = lax.ppermute(sends[plain_round], axes, rounds[plain_round])
    seam, top = lax.optimization_barrier((seam_partner, sends[fold_round]))

    def exchange(k):
        def run(top):
            mirror = [
                [(at(lon, n_lat - 1), at(k - j - lon, n_lat - 1)) for lon in range(n_lon)] for j in (0, 1)
            ]
            plan = rounds[fold_round] + mirror[0]
            last = lax.ppermute(top, axes, mirror[1])
            return lax.ppermute(top, axes, plan), last

        return run

    turn = lax.div(seam[0], jnp.int32(cols))
    folded, got_c = lax.switch(turn, [exchange(k) for k in range(n_lon)], top)
    got_a, got_b = (folded, met) if fold_round == 0 else (met, folded)
    low, up, sent_l, sent_r = pl.pallas_call(
        functools.partial(edge_kernel, fold_round == 0),
        out_shape=[sds((9, chans, cols), BF)] * 2 + [sds((chans, 2 * cols), BF)] * 2,
        in_specs=[smem()] + vmem(6),
        out_specs=vmem(4),
        compiler_params=pltpu.CompilerParams(vmem_limit_bytes=8 * 2**20),
        name="edges",
    )(seam_partner, seam_partner.reshape(n_lon, cols), got_a, got_b, got_c, ft, gt)
    got_l = lax.ppermute(sent_r, "lon", [(i, (i + 1) % n_lon) for i in range(n_lon)])
    got_r = lax.ppermute(sent_l, "lon", [(i, (i - 1) % n_lon) for i in range(n_lon)])

    plain, turned, vecs, up_aug, down_t = pl.pallas_call(
        weight_kernel,
        out_shape=[
            sds((7, chans, LANES), F32),
            sds((7, chans, LANES), F32),
            sds((3, chans, LANES), F32),
            sds((hidden_n, chans + 16), BF),
            sds((hidden_n, chans), BF),
        ],
        in_specs=vmem(7),
        out_specs=vmem(5),
        scratch_shapes=[pltpu.VMEM((2, 7, LANES, LANES), F32)],
        compiler_params=pltpu.CompilerParams(vmem_limit_bytes=8 * 2**20),
        name="weights",
    )(
        depth_weight.transpose(1, 2, 0),
        norm_gain,
        layer_norm_bias,
        layer_scale,
        up_bias,
        up_weight.T,
        down_weight,
    )
    big, small = 2 * chans, 40
    up_t = up_weight.T
    band_rows = (rows + 12) * 8
    output, conv_halo, dcv, kept, passed = pl.pallas_call(
        own_kernel,
        out_shape=[
            sds((chans, rows, cols), BF),
            sds((8 * chans, cols), F32),
            sds((rows * chans, cols), F32),
            sds((big + small, LANES), F32),
            sds((big + small, LANES), F32),
        ],
        in_specs=vmem(14),
        out_specs=vmem(5),
        scratch_shapes=[
            pltpu.VMEM(((rows + 12) * chans, cols), F32),
            pltpu.VMEM(((rows + 12) * chans, cols), F32),
            pltpu.VMEM((band_rows, 2 * cols), BF),
            pltpu.VMEM((rows * chans, cols), F32),
            pltpu.VMEM((chans * rows, cols), F32),
            pltpu.VMEM((7 * 80, LANES), BF),
            pltpu.VMEM((7 * 32, LANES), BF),
            pltpu.VMEM((7 * 80, 2 * cols), F32),
            pltpu.VMEM((7 * 80, 2 * cols), F32),
            pltpu.VMEM((7 * 32, 2 * cols), F32),
            pltpu.VMEM((chans, hidden_n), F32),
            pltpu.VMEM((chans + 16, hidden_n), F32),
            pltpu.VMEM((3, chans, LANES), F32),
            pltpu.VMEM((chans, LANES), F32),
        ],
        compiler_params=pltpu.CompilerParams(vmem_limit_bytes=20 * 2**20),
        name="own",
    )(
        ft,
        gt,
        low,
        up,
        got_l,
        got_r,
        ocean_mask,
        plain,
        turned,
        vecs,
        up_aug,
        up_t,
        down_weight,
        down_t,
    )

    dcv_halo = pl.pallas_call(
        halo_kernel,
        out_shape=sds((8 * chans, cols), F32),
        in_specs=vmem(9),
        out_specs=vmem(1)[0],
        scratch_shapes=[pltpu.VMEM((8 * chans, cols), F32)],
        cost_estimate=pl.CostEstimate(flops=150_000_000, bytes_accessed=2**20, transcendentals=2**18),
        compiler_params=pltpu.CompilerParams(vmem_limit_bytes=8 * 2**20),
        name="halo",
    )(conv_halo, low, up, got_l, got_r, vecs, up_aug, up_t, down_t)

    def adjoint(part, *earlier):
        half = chans // 2
        return pl.pallas_call(
            functools.partial(adjoint_kernel, part),
            grid=(1,),
            out_shape=sds((chans, rows, cols), BF),
            in_specs=vmem(5) + [pl.BlockSpec(memory_space=pl.ANY)] * len(earlier),
            out_specs=pl.BlockSpec((half, rows, cols), lambda _: (part, 0, 0)),
            scratch_shapes=[
                pltpu.VMEM((band_rows, 2 * cols), BF),
                pltpu.VMEM((half * rows, cols), F32),
                pltpu.VMEM((7 * 80, LANES), BF),
                pltpu.VMEM((7 * 48, LANES), BF),
                pltpu.VMEM((7 * 80, 2 * cols), F32),
                pltpu.VMEM((7 * 48, 2 * cols), F32),
            ],
            input_output_aliases={5: 0} if earlier else {},
            cost_estimate=pl.CostEstimate(flops=200_000_000, bytes_accessed=2**21, transcendentals=0),
            compiler_params=pltpu.CompilerParams(vmem_limit_bytes=12 * 2**20),
            name="adjoint",
        )(dcv, dcv_halo, gt, plain, turned, *earlier)

    flip = lambda y, axis, b: lax.ppermute(y, axis, [(i, i ^ b) for i in range(lax.axis_size(axis))])
    total = kept + flip(passed, "lon", 1)
    steps = [("lon", 1 << i) for i in range(1, n_lon.bit_length() - 1)]
    steps += [("lat", 1 << i) for i in range(n_lat.bit_length() - 1)]
    grad = None
    for k, (axis, b) in enumerate(steps):
        total = total + flip(total, axis, b)
        if k == 0:
            total, dcv_halo = lax.optimization_barrier((total, dcv_halo))
        elif k == 1:
            grad = adjoint(0)
            total, grad = lax.optimization_barrier((total, grad))
        elif k == 2:
            grad = adjoint(1, grad)
            total, grad = lax.optimization_barrier((total, grad))
    other = flip(total, "lon", 1)
    g_depth, g_gain, g_bias, g_up, g_up_b, g_down, g_scale = pl.pallas_call(
        finish_kernel,
        out_shape=[
            sds((7, 7, chans), F32),
            sds((chans,), F32),
            sds((chans,), F32),
            sds((chans, hidden_n), F32),
            sds((hidden_n,), F32),
            sds((chans, hidden_n), F32),
            sds((chans,), F32),
        ],
        in_specs=vmem(2),
        out_specs=vmem(7),
        compiler_params=pltpu.CompilerParams(vmem_limit_bytes=6 * 2**20),
        name="finish",
    )(total, other)
    return (
        output[None],
        grad[None],
        g_depth.transpose(2, 0, 1),
        g_gain,
        g_bias,
        g_up.T,
        g_up_b,
        g_down,
        g_scale,
    )


def solution(mesh):
    block = P(None, None, "lat", "lon")
    placed = (block, block, P("lat", "lon")) + (P(),) * 8
    return jax.shard_map(
        shards, mesh=mesh, in_specs=placed, out_specs=(block, block) + (P(),) * 7, check_vma=False
    )
```

```python
import functools
import math

import jax
import jax.numpy as jnp
from jax import lax
from jax.experimental import pallas as pl
from jax.experimental.pallas import tpu as pltpu
from jax.sharding import PartitionSpec as P

BF = jnp.bfloat16
F32 = jnp.float32
LANES = 128
NT = (((1,), (1,)), ((), ()))


def shift(x, amount, axis=1):
    size = x.shape[axis]
    amount %= size
    return x if amount == 0 else pltpu.roll(x, amount, axis)


def lane_iota(shape):
    return lax.broadcasted_iota(jnp.int32, shape, 1)


def pack_kernel(
    seam, fields_far, cot_far, mask_far, ft, gt, first, second, partner, turn, *scratch
):
    plane, fields, cot, mask, head, index, arrived = scratch
    chans, rows, cols = fields.shape
    groups = chans // 8
    pairs = (
        (fields_far, fields),
        (cot_far, cot),
        (mask_far, mask),
        (seam.at[pl.ds(0, 1), :], head),
        (seam.at[pl.ds(lax.axis_index("lon"), 1), :], partner),
    )
    copies = [pltpu.make_async_copy(src, dst, arrived.at[k]) for k, (src, dst) in enumerate(pairs)]
    for k in (3, 0, 1, 2, 4):
        copies[k].start()
    copies[3].wait()
    index[0] = head[0, 0] // cols
    answer = pltpu.make_async_copy(index, turn, arrived.at[5])
    answer.start()
    for k, dst in ((0, ft), (1, gt)):
        copies[k].wait()
        if k == 1:
            copies[2].wait()
            sea = mask[...].astype(F32)
        for c in range(chans):
            if k == 0:
                cell = fields[c].astype(F32)
            else:
                cell = cot[c].astype(F32) * sea
            plane[k, c * rows : (c + 1) * rows, :] = cell
        for r in range(rows):
            parts = [plane[k, pl.ds(g * 8 * rows + r, 8, stride=rows), :] for g in range(groups)]
            dst[r] = jnp.concatenate(parts, axis=0).astype(BF)

    def edge(dst, top):
        base = rows - 6 if top else 0
        gbase = rows - 3 if top else 0
        dst[0:6] = ft[base : base + 6]
        dst[6:9] = gt[gbase : gbase + 3]

    odd = lax.axis_index("lat") % 2

    @pl.when(odd == 0)
    def _():
        edge(first, True)
        edge(second, False)

    @pl.when(odd == 1)
    def _():
        edge(first, False)
        edge(second, True)

    copies[4].wait()
    answer.wait()


def field_lane(r):
    return LANES * (r // 14) + 6 * (r % 14)


def cot_lane(g):
    return LANES * (g // 11) + 84 + 3 * (g % 11)


def edge_kernel(fold_first, partner, got_a, got_b, got_c, ft, gt, low, up, sent_l, sent_r):
    rows, chans, cols = ft.shape
    total = lax.axis_size("lon") * cols
    z = lax.axis_index("lat")
    odd = z % 2
    top = z == lax.axis_size("lat") - 1

    @pl.when(odd == 1)
    def _():
        low[...] = got_a[...]

    @pl.when(odd == 0)
    def _():
        low[...] = got_b[...]

    @pl.when(top)
    def _():
        got_1 = got_a if fold_first else got_b
        src = lax.broadcasted_iota(jnp.int32, (cols, cols), 0)
        want = jnp.broadcast_to(partner[...], (cols, cols))
        leading = jnp.broadcast_to(partner[:, 0:1], (cols, cols))
        near = leading - lax.rem(leading, jnp.full_like(leading, cols))
        far = jnp.where(near == 0, total, near) - cols
        pick_1 = (src + near == want).astype(F32).astype(BF)
        pick_2 = (src + far == want).astype(F32).astype(BF)
        for k in range(9):
            m = 5 - k if k < 6 else 14 - k
            mixed = jnp.dot(got_1[m], pick_1, preferred_element_type=F32)
            mixed = mixed + jnp.dot(got_c[m], pick_2, preferred_element_type=F32)
            up[k] = mixed.astype(BF)

    @pl.when(jnp.logical_not(top) & (odd == 0))
    def _():
        up[...] = got_a[...]

    @pl.when(jnp.logical_not(top) & (odd == 1))
    def _():
        up[...] = got_b[...]

    lane = lane_iota((chans, LANES))
    acc = {key: jnp.zeros((chans, LANES), F32) for key in ((0, 0), (0, 1), (1, 0), (1, 1))}

    def place(side, value, source, lane_to, width):
        half, at = lane_to // LANES, lane_to % LANES
        moved = shift(value, at - source)
        acc[side, half] = jnp.where((lane >= at) & (lane < at + width), moved, acc[side, half])

    for r in range(rows + 12):
        if r < 6:
            value = low[r]
        elif r < rows + 6:
            value = ft[r - 6]
        else:
            value = up[r - rows - 6]
        value = value.astype(F32)
        place(1, value, cols - 6, field_lane(r), 6)
        place(0, value, 0, field_lane(r), 6)
    for r in range(rows + 6):
        if r < 3:
            value = low[6 + r]
        elif r < rows + 3:
            value = gt[r - 3]
        else:
            value = up[6 + r - rows - 3]
        value = value.astype(F32)
        place(1, value, cols - 3, cot_lane(r), 3)
        place(0, value, 0, cot_lane(r), 3)
    for side, dst in ((0, sent_l), (1, sent_r)):
        dst[...] = jnp.concatenate([acc[side, 0], acc[side, 1]], axis=1).astype(BF)


def weight_kernel(
    taps, gain, bias, scale, up_b, up_t, down, plain, turned, vecs, up_aug, down_t, band, band_up, line
):
    chans, hidden_n = up_t.shape
    top = lax.axis_index("lat") == lax.axis_size("lat") - 1
    line[...] = jnp.zeros_like(line)
    for a in range(7):
        block = taps[a].astype(F32)
        for q in range(7):
            line[0, q, 8 * a : 8 * a + 1, 0:chans] = block[q : q + 1]
            line[1, 6 - q, 48 - 8 * a : 49 - 8 * a, 0:chans] = block[q : q + 1]
    for q in range(7):
        plain[q] = line[0, q].T[:chans]
        turned[q] = line[1, q].T[:chans]

    def spread(g, _):
        at = pl.ds(pl.multiple_of(g * 8, 8), 8)
        for q in range(7):
            one, two = plain[q, at, :], turned[q, at, :]
            above = jnp.where(top, two, one)
            band[g, q * 80 : q * 80 + 80, :] = jnp.concatenate(
                [pltpu.roll(one, 8 * i, 1, stride=1, stride_axis=0) for i in range(10)], axis=0
            ).astype(BF)
            band_up[g, q * 32 : q * 32 + 32, :] = jnp.concatenate(
                [pltpu.roll(above, 8 * i, 1, stride=1, stride_axis=0) for i in range(6, 10)], axis=0
            ).astype(BF)
        return 0

    lax.fori_loop(0, chans // 8, spread, 0)
    wide = LANES - chans
    columns = jnp.concatenate(
        [v[...].astype(F32).reshape(1, chans) for v in (gain, bias, scale)] + [jnp.zeros((5, chans), F32)],
        axis=0,
    )
    columns = jnp.concatenate([columns, jnp.zeros((8, wide), F32)], axis=1).T
    for k in range(3):
        vecs[k] = jnp.broadcast_to(columns[:chans, k : k + 1], (chans, LANES))
    tall = jnp.concatenate(
        [
            up_t[...].astype(F32),
            up_b[...].astype(F32).reshape(1, hidden_n),
            jnp.zeros((wide - 1, hidden_n), F32),
        ],
        axis=0,
    )
    up_aug[...] = tall.T[:, : chans + 16].astype(BF)
    tall = jnp.concatenate([down[...].astype(F32), jnp.zeros((wide, hidden_n), F32)], axis=0)
    down_t[...] = tall.T[:, :chans].astype(BF)


def normal_terms(v):
    cdf = 0.5 * (1.0 + lax.erf(v * (1.0 / math.sqrt(2.0))))
    dens = jnp.exp2(v * v * (-0.5 / math.log(2.0)) - 0.5 * math.log2(2.0 * math.pi))
    return cdf, dens


def edge_mask(lane, s):
    return lane < s if s > 0 else lane >= LANES + s


def rows_of(r, g, chans):
    return pl.ds(pl.multiple_of(r * chans + g * 8, 8), 8)


def twice(x):
    return jnp.concatenate([x, x], axis=1)


def norm_and_back(x, g, vecs, up_aug, up_t, down_t):
    gain, bias, scale = twice(vecs[0]), twice(vecs[1]), twice(vecs[2])
    centred = x - jnp.mean(x, axis=0, keepdims=True)
    var = jnp.mean(centred * centred, axis=0, keepdims=True)
    rstd = lax.rsqrt(var + 1e-06)
    xhat = centred * rstd
    pad = (up_aug.shape[1] - x.shape[0], x.shape[1])
    ones = (lax.broadcasted_iota(jnp.int32, pad, 0) == 0).astype(F32).astype(BF)
    normed = jnp.concatenate([(xhat * gain + bias).astype(BF), ones], axis=0)
    pre = jnp.dot(up_aug[...], normed, preferred_element_type=F32)
    cdf, dens = normal_terms(pre)
    d_branch = (g * scale).astype(BF)
    d_hidden = jnp.dot(down_t[...], d_branch, preferred_element_type=F32)
    d_pre = (d_hidden * (cdf + pre * dens)).astype(BF)
    d_normed = jnp.dot(up_t[...], d_pre, preferred_element_type=F32)
    gd = d_normed * gain
    m1 = jnp.mean(gd, axis=0, keepdims=True)
    m2 = jnp.mean(gd * xhat, axis=0, keepdims=True)
    dx = (rstd * (gd - m1 - xhat * m2)).astype(BF).astype(F32)
    return dx, (pre, cdf, d_branch, d_pre, d_normed, normed, xhat, scale)


def own_kernel(
    ft,
    gt,
    low,
    up,
    got_l,
    got_r,
    mask,
    band,
    band_up,
    vecs,
    up_aug,
    up_t,
    down,
    down_t,
    out,
    conv_halo,
    dcv,
    kept,
    passed,
    ext,
    rim,
    rhs,
    conv,
    plane,
    prod_1,
    prod_2,
    prod_3,
    g_down,
    g_up,
    sums,
    taps_g,
):
    rows, chans, cols = ft.shape
    groups = chans // 8
    mid = rows + 6
    odd_core = lax.axis_index("lon") % 2
    lane = lane_iota((8, LANES))
    wide = slice(0, LANES), slice(LANES, 2 * LANES)
    at_row = lambda r, g: rows_of(r, g, chans)

    def conv_group(g, _):
        at = pl.ds(pl.multiple_of(g * 8, 8), 8)
        left = [got_l[at, w].astype(F32) for w in wide]
        right = [got_r[at, w].astype(F32) for w in wide]
        for r0 in range(0, rows + 12, 2):
            pair = []
            for r in (r0, r0 + 1):
                if r < 6:
                    value = low[r, at, :]
                elif r < rows + 6:
                    value = ft[r - 6, at, :]
                else:
                    value = up[r - rows - 6, at, :]
                value = value.astype(F32)
                half, start = field_lane(r) // LANES, field_lane(r) % LANES
                beyond = jnp.where(lane < 64, shift(right[half], -start), shift(left[half], LANES - 6 - start))
                ext[at_row(r, g), :] = value
                rim[at_row(r, g), :] = beyond
                pair.append(jnp.concatenate([value, beyond], axis=1))
            rhs[8 * r0 : 8 * r0 + 16, :] = jnp.concatenate(pair, axis=0).astype(BF)
        prod_1[...] = jnp.dot(band[g], rhs[0:128, :], preferred_element_type=F32)
        prod_2[...] = jnp.dot(band[g], rhs[80:208, :], preferred_element_type=F32)
        prod_3[...] = jnp.dot(band_up[g], rhs[96:224, :], preferred_element_type=F32)
        sides = [jnp.zeros((8, LANES), F32)] * 2
        for o in range(mid):
            if o < 10:
                prod, step, i = prod_1, 80, o
            elif o < rows + 3:
                prod, step, i = prod_2, 80, o - 10
            else:
                prod, step, i = prod_3, 32, o - 18
            inner = outer = None
            for q in range(7):
                part = slice(q * step + 8 * i, q * step + 8 * i + 8)
                mine, edge = prod[part, wide[0]], prod[part, wide[1]]
                if q != 3:
                    swap = edge_mask(lane, q - 3)
                    mine, edge = jnp.where(swap, edge, mine), jnp.where(swap, mine, edge)
                    mine, edge = shift(mine, 3 - q), shift(edge, 3 - q)
                inner = mine if inner is None else inner + mine
                outer = edge if outer is None else outer + edge
            if o < 3:
                conv_halo[at_row(o, g), :] = inner
            elif o < rows + 3:
                conv[at_row(o - 3, g), :] = inner
            else:
                conv_halo[at_row(o - rows, g), :] = inner
            inside = (lane >= 3 * o) & (lane < 3 * o + 3)
            sides[0] = jnp.where(inside, shift(outer, 3 * o + 3), sides[0])
            sides[1] = jnp.where(inside, shift(outer, 3 * o), sides[1])
        for k in (0, 1):
            conv_halo[at_row(6 + k, g), :] = sides[k]
        return 0

    lax.fori_loop(0, groups, conv_group, 0)

    g_down[...] = jnp.zeros_like(g_down)
    g_up[...] = jnp.zeros_like(g_up)
    sums[...] = jnp.zeros_like(sums)

    def unit(u):
        return pl.ds(pl.multiple_of(u * chans, chans), chans)

    def own_block(b, _):
        units = (b * 2, b * 2 + 1)
        x = jnp.concatenate([conv[unit(u), :] for u in units], axis=1)
        g = jnp.concatenate([gt[u].astype(F32) for u in units], axis=1)
        dx, (pre, cdf, d_branch, d_pre, d_normed, normed, xhat, scale) = norm_and_back(
            x, g, vecs, up_aug, up_t, down_t
        )
        hidden = (pre * cdf).astype(BF)
        branch = jnp.dot(down[...], hidden, preferred_element_type=F32)
        sea = [mask[pl.ds(u, 1), :].astype(F32) for u in units]
        fields = jnp.concatenate([ft[u].astype(F32) for u in units], axis=1)
        res = (fields + scale * branch) * jnp.concatenate(sea, axis=1)
        for k, u in enumerate(units):
            for gr in range(groups):
                plane[pl.ds(gr * 8 * rows + u, 8, stride=rows), :] = res[gr * 8 : gr * 8 + 8, wide[k]]
            dcv[unit(u), :] = dx[:, wide[k]]
        g_down[...] += lax.dot_general(d_branch, hidden, NT, preferred_element_type=F32)
        g_up[...] += lax.dot_general(normed, d_pre, NT, preferred_element_type=F32)
        for k, value in enumerate((d_normed * xhat, d_normed, g * branch)):
            sums[k] += value[:, :LANES] + value[:, LANES:]
        return 0

    lax.fori_loop(0, rows // 2, own_block, 0, unroll=2)

    def taps_group(g, _):
        at = pl.ds(pl.multiple_of(g * 8, 8), 8)
        line = jnp.zeros((8, LANES), F32)
        for q in range(7):
            own = [shift(dcv[at_row(o, g), :], q - 3) for o in range(rows)]
            tot = [None] * 7
            for r in range(mid):
                value = ext[at_row(r + 3, g), :]
                if q != 3:
                    value = jnp.where(edge_mask(lane, q - 3), rim[at_row(r + 3, g), :], value)
                for a in range(7):
                    o = r - a
                    if 0 <= o < rows:
                        term = value * own[o]
                        tot[a] = term if tot[a] is None else tot[a] + term
            for a in range(7):
                total = jnp.sum(tot[a], axis=1, keepdims=True)
                line = jnp.where(lane == 8 * a + q, total, line)
        for k in range(3):
            total = jnp.sum(sums[k, at, :], axis=1, keepdims=True)
            line = jnp.where(lane == 56 + k, total, line)
        taps_g[at, :] = line
        return 0

    lax.fori_loop(0, groups, taps_group, 0)
    small = taps_g[...]
    cut = 40

    def fill(lower, upper):
        for h, w in enumerate(wide):
            lower[h * chans : (h + 1) * chans, :] = g_down[:, w]
            upper[h * chans : (h + 1) * chans, :] = g_up[0:chans, w]
            upper[2 * chans + 24 + 8 * h : 2 * chans + 32 + 8 * h, :] = g_up[chans : chans + 8, w]
        lower[2 * chans : 2 * chans + cut, :] = small[:cut]
        upper[2 * chans : 2 * chans + 24, :] = small[cut:]

    @pl.when(odd_core == 0)
    def _():
        fill(kept, passed)

    @pl.when(odd_core == 1)
    def _():
        fill(passed, kept)

    for c in range(chans):
        out[c] = plane[c * rows : (c + 1) * rows, :].astype(BF)


def halo_kernel(conv_halo, low, up, got_l, got_r, vecs, up_aug, up_t, down_t, dcv_halo, cots):
    _, chans, _ = low.shape
    lane_c = lane_iota((chans, LANES))
    wide = slice(0, LANES), slice(LANES, 2 * LANES)
    for r in range(3):
        cots[r * chans : (r + 1) * chans, :] = low[6 + r].astype(F32)
        cots[(3 + r) * chans : (4 + r) * chans, :] = up[6 + r].astype(F32)
    for k, got in ((0, got_l), (1, got_r)):
        first = shift(got[:, wide[0]].astype(F32), -84)
        second = shift(got[:, wide[1]].astype(F32), 33 - 84)
        value = jnp.where(lane_c < 33, first, jnp.where(lane_c < 66, second, 0.0))
        cots[(6 + k) * chans : (7 + k) * chans, :] = value

    def halo_block(b, _):
        units = [pl.ds(pl.multiple_of((2 * b + k) * chans, chans), chans) for k in (0, 1)]
        x = jnp.concatenate([conv_halo[u, :] for u in units], axis=1)
        g = jnp.concatenate([cots[u, :] for u in units], axis=1)
        dx, _ = norm_and_back(x, g, vecs, up_aug, up_t, down_t)
        for k, u in enumerate(units):
            dcv_halo[u, :] = dx[:, wide[k]]
        return 0

    lax.fori_loop(0, 4, halo_block, 0, unroll=2)


def adjoint_kernel(part, *refs):
    dcv, dcv_halo, gt, plain, turned = refs[:5]
    grad, rhs, plane, band, band_up, prod_1, prod_3 = refs[-7:]
    rows, chans, cols = gt.shape
    some = grad.shape[0]
    first = part * (some // 8)
    mid = rows + 6
    top = lax.axis_index("lat") == lax.axis_size("lat") - 1
    lane = lane_iota((8, LANES))
    wide = slice(0, LANES), slice(LANES, 2 * LANES)
    at_row = lambda r, g: rows_of(r, g, chans)

    def adjoint_group(g, _):
        at = pl.ds(pl.multiple_of(g * 8, 8), 8)
        left, right = dcv_halo[at_row(6, g), :], dcv_halo[at_row(7, g), :]
        for r0 in range(0, mid, 2):
            pair = []
            for r in (r0, r0 + 1):
                if r < 3:
                    value = dcv_halo[at_row(r, g), :]
                elif r < rows + 3:
                    value = dcv[at_row(r - 3, g), :]
                else:
                    value = dcv_halo[at_row(r - rows, g), :]
                beyond = jnp.where(lane < 64, shift(right, -3 * r), shift(left, LANES - 3 - 3 * r))
                pair.append(jnp.concatenate([value, beyond], axis=1))
            rhs[8 * r0 : 8 * r0 + 16, :] = jnp.concatenate(pair, axis=0).astype(BF)
        for q in range(7):
            one, two = turned[q, at, :], plain[q, at, :]
            above = jnp.where(top, two, one)
            moved = [pltpu.roll(one, 8 * i, 1, stride=1, stride_axis=0) for i in range(10)]
            band[q * 80 : q * 80 + 80, :] = jnp.concatenate(moved, axis=0).astype(BF)
            late = moved[:3]
            for i in range(3, 6):
                other = pltpu.roll(above, 8 * i, 1, stride=1, stride_axis=0)
                late.append(jnp.where(lane >= 8 * (rows + 3 - 10), other, moved[i]))
            band_up[q * 48 : q * 48 + 48, :] = jnp.concatenate(late, axis=0).astype(BF)
        prod_1[...] = jnp.dot(band[...], rhs[0:128, :], preferred_element_type=F32)
        prod_3[...] = jnp.dot(band_up[:, 0:96], rhs[80:176, :], preferred_element_type=F32)
        for o in range(rows):
            prod, step, i = (prod_1, 80, o) if o < 10 else (prod_3, 48, o - 10)
            inner = gt[o, at, :].astype(F32)
            for q in range(7):
                part = slice(q * step + 8 * i, q * step + 8 * i + 8)
                mine = prod[part, wide[0]]
                if q != 3:
                    mine = shift(jnp.where(edge_mask(lane, q - 3), prod[part, wide[1]], mine), 3 - q)
                inner = inner + mine
            plane[pl.ds((g - first) * (8 * rows) + o, 8, stride=rows), :] = inner
        return 0

    lax.fori_loop(first, first + some // 8, adjoint_group, 0)
    for c in range(some):
        grad[c] = plane[c * rows : (c + 1) * rows, :].astype(BF)


def finish_kernel(total, other, g_depth, g_gain, g_bias, g_up, g_up_b, g_down, g_scale):
    chans, hidden_n = g_down.shape

    def unpack(lower, upper):
        for h in range(hidden_n // LANES):
            w = slice(h * LANES, (h + 1) * LANES)
            g_down[:, w] = lower[h * chans : (h + 1) * chans, :]
            g_up[:, w] = upper[h * chans : (h + 1) * chans, :]
            at = 2 * chans + 24 + 8 * h
            g_up_b[w] = upper[at : at + 1, :].reshape(LANES)
        small = jnp.concatenate(
            [
                lower[2 * chans : 2 * chans + 40, :],
                upper[2 * chans : 2 * chans + 24, :],
                jnp.zeros((LANES - chans, LANES), F32),
            ],
            axis=0,
        ).T
        for k, dst in enumerate((g_gain, g_bias, g_scale)):
            dst[...] = small[56 + k : 57 + k, :chans].reshape(chans)
        for a in range(7):
            g_depth[a] = small[8 * a : 8 * a + 7, :chans]

    odd_core = lax.axis_index("lon") % 2

    @pl.when(odd_core == 0)
    def _():
        unpack(total, other)

    @pl.when(odd_core == 1)
    def _():
        unpack(other, total)


def vmem(n):
    return [pl.BlockSpec(memory_space=pltpu.VMEM)] * n


def shards(
    fields,
    cotangent,
    ocean_mask,
    seam_partner,
    depth_weight,
    norm_gain,
    layer_norm_bias,
    up_weight,
    up_bias,
    down_weight,
    layer_scale,
):
    _, chans, rows, cols = fields.shape
    hidden_n = up_weight.shape[0]
    n_lon, n_lat = lax.axis_size("lon"), lax.axis_size("lat")
    sds = jax.ShapeDtypeStruct
    hbm = pl.BlockSpec(memory_space=pltpu.HBM)
    ft, gt, first, second, partner, turn = pl.pallas_call(
        pack_kernel,
        out_shape=[sds((rows, chans, cols), BF)] * 2
        + [sds((9, chans, cols), BF)] * 2
        + [sds((1, cols), jnp.int32), sds((1,), jnp.int32)],
        in_specs=[hbm] * 4,
        out_specs=vmem(5) + [hbm],
        scratch_shapes=[
            pltpu.VMEM((2, chans * rows, cols), F32),
            pltpu.VMEM((chans, rows, cols), BF),
            pltpu.VMEM((chans, rows, cols), BF),
            pltpu.VMEM((rows, cols), jnp.int32),
            pltpu.SMEM((1, cols), jnp.int32),
            pltpu.SMEM((1,), jnp.int32),
            pltpu.SemaphoreType.DMA((6,)),
        ],
        compiler_params=pltpu.CompilerParams(vmem_limit_bytes=8 * 2**20),
        name="pack",
    )(
        *[
            pltpu.with_memory_space_constraint(v, pltpu.HBM)
            for v in (seam_partner.reshape(n_lon, cols), fields[0], cotangent[0], ocean_mask)
        ]
    )

    at = lambda lon, lat: (lon % n_lon) * n_lat + lat
    rounds = [[], []]
    for lat in range(n_lat - 1):
        for lon in range(n_lon):
            rounds[lat % 2] += [(at(lon, lat), at(lon, lat + 1)), (at(lon, lat + 1), at(lon, lat))]
    fold_round = (n_lat - 1) % 2

    axes = ("lon", "lat")
    plain_round = 1 - fold_round
    sends = (first, second)
    met = lax.ppermute(sends[plain_round], axes, rounds[plain_round])
    top = sends[fold_round]

    def exchange(k):
        def run(top):
            mirror = [
                [(at(lon, n_lat - 1), at(k - j - lon, n_lat - 1)) for lon in range(n_lon)] for j in (0, 1)
            ]
            plan = rounds[fold_round] + mirror[0]
            return lax.ppermute(top, axes, mirror[1]), lax.ppermute(top, axes, plan)

        return run

    got_c, folded = lax.switch(turn[0], [exchange(k) for k in range(n_lon)], top)
    got_a, got_b = (folded, met) if fold_round == 0 else (met, folded)
    low, up, sent_l, sent_r = pl.pallas_call(
        functools.partial(edge_kernel, fold_round == 0),
        out_shape=[sds((9, chans, cols), BF)] * 2 + [sds((chans, 2 * cols), BF)] * 2,
        in_specs=vmem(6),
        out_specs=vmem(4),
        compiler_params=pltpu.CompilerParams(vmem_limit_bytes=8 * 2**20),
        name="edges",
    )(partner, got_a, got_b, got_c, ft, gt)
    got_l = lax.ppermute(sent_r, "lon", [(i, (i + 1) % n_lon) for i in range(n_lon)])
    got_r = lax.ppermute(sent_l, "lon", [(i, (i - 1) % n_lon) for i in range(n_lon)])

    plain, turned, vecs, up_aug, down_t, band, band_up = pl.pallas_call(
        weight_kernel,
        out_shape=[
            sds((7, chans, LANES), F32),
            sds((7, chans, LANES), F32),
            sds((3, chans, LANES), F32),
            sds((hidden_n, chans + 16), BF),
            sds((hidden_n, chans), BF),
            sds((chans // 8, 7 * 80, LANES), BF),
            sds((chans // 8, 7 * 32, LANES), BF),
        ],
        in_specs=vmem(7),
        out_specs=vmem(7),
        scratch_shapes=[pltpu.VMEM((2, 7, LANES, LANES), F32)],
        compiler_params=pltpu.CompilerParams(vmem_limit_bytes=8 * 2**20),
        name="weights",
    )(
        depth_weight.transpose(1, 2, 0),
        norm_gain,
        layer_norm_bias,
        layer_scale,
        up_bias,
        up_weight.T,
        down_weight,
    )
    big, small = 2 * chans, 40
    up_t = up_weight.T
    band_rows = (rows + 12) * 8
    output, conv_halo, dcv, kept, passed = pl.pallas_call(
        own_kernel,
        out_shape=[
            sds((chans, rows, cols), BF),
            sds((8 * chans, cols), F32),
            sds((rows * chans, cols), F32),
            sds((big + small, LANES), F32),
            sds((big + small, LANES), F32),
        ],
        in_specs=vmem(14),
        out_specs=vmem(5),
        scratch_shapes=[
            pltpu.VMEM(((rows + 12) * chans, cols), F32),
            pltpu.VMEM(((rows + 12) * chans, cols), F32),
            pltpu.VMEM((band_rows, 2 * cols), BF),
            pltpu.VMEM((rows * chans, cols), F32),
            pltpu.VMEM((chans * rows, cols), F32),
            pltpu.VMEM((7 * 80, 2 * cols), F32),
            pltpu.VMEM((7 * 80, 2 * cols), F32),
            pltpu.VMEM((7 * 32, 2 * cols), F32),
            pltpu.VMEM((chans, hidden_n), F32),
            pltpu.VMEM((chans + 16, hidden_n), F32),
            pltpu.VMEM((3, chans, LANES), F32),
            pltpu.VMEM((chans, LANES), F32),
        ],
        compiler_params=pltpu.CompilerParams(vmem_limit_bytes=20 * 2**20),
        name="own",
    )(
        ft,
        gt,
        low,
        up,
        got_l,
        got_r,
        ocean_mask,
        band,
        band_up,
        vecs,
        up_aug,
        up_t,
        down_weight,
        down_t,
    )

    dcv_halo = pl.pallas_call(
        halo_kernel,
        out_shape=sds((8 * chans, cols), F32),
        in_specs=vmem(9),
        out_specs=vmem(1)[0],
        scratch_shapes=[pltpu.VMEM((8 * chans, cols), F32)],
        cost_estimate=pl.CostEstimate(flops=150_000_000, bytes_accessed=2**20, transcendentals=2**18),
        compiler_params=pltpu.CompilerParams(vmem_limit_bytes=8 * 2**20),
        name="halo",
    )(conv_halo, low, up, got_l, got_r, vecs, up_aug, up_t, down_t)

    def adjoint(part, *earlier):
        half = chans // 2
        return pl.pallas_call(
            functools.partial(adjoint_kernel, part),
            grid=(1,),
            out_shape=sds((chans, rows, cols), BF),
            in_specs=vmem(5) + [pl.BlockSpec(memory_space=pl.ANY)] * len(earlier),
            out_specs=pl.BlockSpec((half, rows, cols), lambda _: (part, 0, 0)),
            scratch_shapes=[
                pltpu.VMEM((band_rows, 2 * cols), BF),
                pltpu.VMEM((half * rows, cols), F32),
                pltpu.VMEM((7 * 80, LANES), BF),
                pltpu.VMEM((7 * 48, LANES), BF),
                pltpu.VMEM((7 * 80, 2 * cols), F32),
                pltpu.VMEM((7 * 48, 2 * cols), F32),
            ],
            input_output_aliases={5: 0} if earlier else {},
            cost_estimate=pl.CostEstimate(flops=200_000_000, bytes_accessed=2**21, transcendentals=0),
            compiler_params=pltpu.CompilerParams(vmem_limit_bytes=12 * 2**20),
            name="adjoint",
        )(dcv, dcv_halo, gt, plain, turned, *earlier)

    flip = lambda y, axis, b: lax.ppermute(y, axis, [(i, i ^ b) for i in range(lax.axis_size(axis))])
    total = kept + flip(passed, "lon", 1)
    steps = [("lon", 1 << i) for i in range(1, n_lon.bit_length() - 1)]
    steps += [("lat", 1 << i) for i in range(n_lat.bit_length() - 1)]
    grad = None
    for k, (axis, b) in enumerate(steps):
        total = total + flip(total, axis, b)
        if k == 0:
            total, dcv_halo = lax.optimization_barrier((total, dcv_halo))
        elif k == 1:
            grad = adjoint(0)
            total, grad = lax.optimization_barrier((total, grad))
        elif k == 2:
            grad = adjoint(1, grad)
            total, grad = lax.optimization_barrier((total, grad))
    other = flip(total, "lon", 1)
    g_depth, g_gain, g_bias, g_up, g_up_b, g_down, g_scale = pl.pallas_call(
        finish_kernel,
        out_shape=[
            sds((7, 7, chans), F32),
            sds((chans,), F32),
            sds((chans,), F32),
            sds((chans, hidden_n), F32),
            sds((hidden_n,), F32),
            sds((chans, hidden_n), F32),
            sds((chans,), F32),
        ],
        in_specs=vmem(2),
        out_specs=vmem(7),
        compiler_params=pltpu.CompilerParams(vmem_limit_bytes=6 * 2**20),
        name="finish",
    )(total, other)
    return (
        output[None],
        grad[None],
        g_depth.transpose(2, 0, 1),
        g_gain,
        g_bias,
        g_up.T,
        g_up_b,
        g_down,
        g_scale,
    )


def solution(mesh):
    block = P(None, None, "lat", "lon")
    placed = (block, block, P("lat", "lon")) + (P(),) * 8
    return jax.shard_map(
        shards, mesh=mesh, in_specs=placed, out_specs=(block, block) + (P(),) * 7, check_vma=False
    )
```

```python
import functools
import math

import jax
import jax.numpy as jnp
from jax import lax
from jax.experimental import pallas as pl
from jax.experimental.pallas import tpu as pltpu
from jax.sharding import PartitionSpec as P

BF = jnp.bfloat16
F32 = jnp.float32
LANES = 128
NT = (((1,), (1,)), ((), ()))


def shift(x, amount, axis=1):
    size = x.shape[axis]
    amount %= size
    return x if amount == 0 else pltpu.roll(x, amount, axis)


def lane_iota(shape):
    return lax.broadcasted_iota(jnp.int32, shape, 1)


def pack_kernel(
    seam, fields_far, cot_far, mask_far, ft, gt, first, second, partner, turn, *scratch
):
    plane, fields, cot, mask, head, index, arrived = scratch
    chans, rows, cols = fields.shape
    groups = chans // 8
    pairs = (
        (fields_far, fields),
        (cot_far, cot),
        (mask_far, mask),
        (seam.at[pl.ds(0, 1), :], head),
        (seam.at[pl.ds(lax.axis_index("lon"), 1), :], partner),
    )
    copies = [pltpu.make_async_copy(src, dst, arrived.at[k]) for k, (src, dst) in enumerate(pairs)]
    for k in (3, 0, 1, 2, 4):
        copies[k].start()
    copies[3].wait()
    index[0] = head[0, 0] // cols
    answer = pltpu.make_async_copy(index, turn, arrived.at[5])
    answer.start()
    for k, dst in ((0, ft), (1, gt)):
        copies[k].wait()
        if k == 1:
            copies[2].wait()
            sea = mask[...].astype(F32)
        for c in range(chans):
            if k == 0:
                cell = fields[c].astype(F32)
            else:
                cell = cot[c].astype(F32) * sea
            plane[k, c * rows : (c + 1) * rows, :] = cell
        for r in range(rows):
            parts = [plane[k, pl.ds(g * 8 * rows + r, 8, stride=rows), :] for g in range(groups)]
            dst[r] = jnp.concatenate(parts, axis=0).astype(BF)

    def edge(dst, top):
        base = rows - 6 if top else 0
        gbase = rows - 3 if top else 0
        dst[0:6] = ft[base : base + 6]
        dst[6:9] = gt[gbase : gbase + 3]

    odd = lax.axis_index("lat") % 2

    @pl.when(odd == 0)
    def _():
        edge(first, True)
        edge(second, False)

    @pl.when(odd == 1)
    def _():
        edge(first, False)
        edge(second, True)

    copies[4].wait()
    answer.wait()


def field_lane(r):
    return LANES * (r // 14) + 6 * (r % 14)


def cot_lane(g):
    return LANES * (g // 11) + 84 + 3 * (g % 11)


def edge_kernel(fold_first, partner, got_a, got_b, got_c, ft, gt, low, up, sent_l, sent_r):
    rows, chans, cols = ft.shape
    total = lax.axis_size("lon") * cols
    z = lax.axis_index("lat")
    odd = z % 2
    top = z == lax.axis_size("lat") - 1

    @pl.when(odd == 1)
    def _():
        low[...] = got_a[...]

    @pl.when(odd == 0)
    def _():
        low[...] = got_b[...]

    @pl.when(top)
    def _():
        got_1 = got_a if fold_first else got_b
        src = lax.broadcasted_iota(jnp.int32, (cols, cols), 0)
        want = jnp.broadcast_to(partner[...], (cols, cols))
        leading = jnp.broadcast_to(partner[:, 0:1], (cols, cols))
        near = leading - lax.rem(leading, jnp.full_like(leading, cols))
        far = jnp.where(near == 0, total, near) - cols
        pick_1 = (src + near == want).astype(F32).astype(BF)
        pick_2 = (src + far == want).astype(F32).astype(BF)
        for k in range(9):
            m = 5 - k if k < 6 else 14 - k
            mixed = jnp.dot(got_1[m], pick_1, preferred_element_type=F32)
            mixed = mixed + jnp.dot(got_c[m], pick_2, preferred_element_type=F32)
            up[k] = mixed.astype(BF)

    @pl.when(jnp.logical_not(top) & (odd == 0))
    def _():
        up[...] = got_a[...]

    @pl.when(jnp.logical_not(top) & (odd == 1))
    def _():
        up[...] = got_b[...]

    lane = lane_iota((chans, LANES))
    acc = {key: jnp.zeros((chans, LANES), F32) for key in ((0, 0), (0, 1), (1, 0), (1, 1))}

    def place(side, value, source, lane_to, width):
        half, at = lane_to // LANES, lane_to % LANES
        moved = shift(value, at - source)
        acc[side, half] = jnp.where((lane >= at) & (lane < at + width), moved, acc[side, half])

    for r in range(rows + 12):
        if r < 6:
            value = low[r]
        elif r < rows + 6:
            value = ft[r - 6]
        else:
            value = up[r - rows - 6]
        value = value.astype(F32)
        place(1, value, cols - 6, field_lane(r), 6)
        place(0, value, 0, field_lane(r), 6)
    for r in range(rows + 6):
        if r < 3:
            value = low[6 + r]
        elif r < rows + 3:
            value = gt[r - 3]
        else:
            value = up[6 + r - rows - 3]
        value = value.astype(F32)
        place(1, value, cols - 3, cot_lane(r), 3)
        place(0, value, 0, cot_lane(r), 3)
    for side, dst in ((0, sent_l), (1, sent_r)):
        dst[...] = jnp.concatenate([acc[side, 0], acc[side, 1]], axis=1).astype(BF)


def weight_kernel(
    taps, gain, bias, scale, up_b, up_t, down, plain, turned, vecs, up_aug, down_t, band, band_up, line
):
    chans, hidden_n = up_t.shape
    top = lax.axis_index("lat") == lax.axis_size("lat") - 1
    line[...] = jnp.zeros_like(line)
    for a in range(7):
        block = taps[a].astype(F32)
        for q in range(7):
            line[0, q, 8 * a : 8 * a + 1, 0:chans] = block[q : q + 1]
            line[1, 6 - q, 48 - 8 * a : 49 - 8 * a, 0:chans] = block[q : q + 1]
    for q in range(7):
        plain[q] = line[0, q].T[:chans]
        turned[q] = line[1, q].T[:chans]

    def spread(g, _):
        at = pl.ds(pl.multiple_of(g * 8, 8), 8)
        for q in range(7):
            one, two = plain[q, at, :], turned[q, at, :]
            above = jnp.where(top, two, one)
            band[g, q * 80 : q * 80 + 80, :] = jnp.concatenate(
                [pltpu.roll(one, 8 * i, 1, stride=1, stride_axis=0) for i in range(10)], axis=0
            ).astype(BF)
            band_up[g, q * 32 : q * 32 + 32, :] = jnp.concatenate(
                [pltpu.roll(above, 8 * i, 1, stride=1, stride_axis=0) for i in range(6, 10)], axis=0
            ).astype(BF)
        return 0

    lax.fori_loop(0, chans // 8, spread, 0)
    wide = LANES - chans
    columns = jnp.concatenate(
        [v[...].astype(F32).reshape(1, chans) for v in (gain, bias, scale)] + [jnp.zeros((5, chans), F32)],
        axis=0,
    )
    columns = jnp.concatenate([columns, jnp.zeros((8, wide), F32)], axis=1).T
    for k in range(3):
        vecs[k] = jnp.broadcast_to(columns[:chans, k : k + 1], (chans, LANES))
    tall = jnp.concatenate(
        [
            up_t[...].astype(F32),
            up_b[...].astype(F32).reshape(1, hidden_n),
            jnp.zeros((wide - 1, hidden_n), F32),
        ],
        axis=0,
    )
    up_aug[...] = tall.T[:, : chans + 16].astype(BF)
    tall = jnp.concatenate([down[...].astype(F32), jnp.zeros((wide, hidden_n), F32)], axis=0)
    down_t[...] = tall.T[:, :chans].astype(BF)


def normal_terms(v):
    cdf = 0.5 * (1.0 + lax.erf(v * (1.0 / math.sqrt(2.0))))
    dens = jnp.exp2(v * v * (-0.5 / math.log(2.0)) - 0.5 * math.log2(2.0 * math.pi))
    return cdf, dens


def edge_mask(lane, s):
    return lane < s if s > 0 else lane >= LANES + s


def rows_of(r, g, chans):
    return pl.ds(pl.multiple_of(r * chans + g * 8, 8), 8)


def twice(x):
    return jnp.concatenate([x, x], axis=1)


def norm_and_back(x, g, vecs, up_aug, up_t, down_t):
    gain, bias, scale = twice(vecs[0]), twice(vecs[1]), twice(vecs[2])
    centred = x - jnp.mean(x, axis=0, keepdims=True)
    var = jnp.mean(centred * centred, axis=0, keepdims=True)
    rstd = lax.rsqrt(var + 1e-06)
    xhat = centred * rstd
    pad = (up_aug.shape[1] - x.shape[0], x.shape[1])
    ones = (lax.broadcasted_iota(jnp.int32, pad, 0) == 0).astype(F32).astype(BF)
    normed = jnp.concatenate([(xhat * gain + bias).astype(BF), ones], axis=0)
    pre = jnp.dot(up_aug[...], normed, preferred_element_type=F32)
    cdf, dens = normal_terms(pre)
    d_branch = (g * scale).astype(BF)
    d_hidden = jnp.dot(down_t[...], d_branch, preferred_element_type=F32)
    d_pre = (d_hidden * (cdf + pre * dens)).astype(BF)
    d_normed = jnp.dot(up_t[...], d_pre, preferred_element_type=F32)
    gd = d_normed * gain
    m1 = jnp.mean(gd, axis=0, keepdims=True)
    m2 = jnp.mean(gd * xhat, axis=0, keepdims=True)
    dx = (rstd * (gd - m1 - xhat * m2)).astype(BF).astype(F32)
    return dx, (pre, cdf, d_branch, d_pre, d_normed, normed, xhat, scale)


def own_kernel(
    ft,
    gt,
    low,
    up,
    got_l,
    got_r,
    mask,
    band,
    band_up,
    vecs,
    up_aug,
    up_t,
    down,
    down_t,
    out,
    conv_halo,
    dcv,
    kept,
    passed,
    ext,
    rim,
    rhs,
    conv,
    plane,
    prod_1,
    prod_2,
    prod_3,
    g_down,
    g_up,
    sums,
    taps_g,
):
    rows, chans, cols = ft.shape
    groups = chans // 8
    mid = rows + 6
    odd_core = lax.axis_index("lon") % 2
    lane = lane_iota((8, LANES))
    wide = slice(0, LANES), slice(LANES, 2 * LANES)
    at_row = lambda r, g: rows_of(r, g, chans)

    def conv_group(g, _):
        at = pl.ds(pl.multiple_of(g * 8, 8), 8)
        left = [got_l[at, w].astype(F32) for w in wide]
        right = [got_r[at, w].astype(F32) for w in wide]
        for r0 in range(0, rows + 12, 2):
            pair = []
            for r in (r0, r0 + 1):
                if r < 6:
                    value = low[r, at, :]
                elif r < rows + 6:
                    value = ft[r - 6, at, :]
                else:
                    value = up[r - rows - 6, at, :]
                value = value.astype(F32)
                half, start = field_lane(r) // LANES, field_lane(r) % LANES
                beyond = jnp.where(lane < 64, shift(right[half], -start), shift(left[half], LANES - 6 - start))
                ext[at_row(r, g), :] = value
                rim[at_row(r, g), :] = beyond
                pair.append(jnp.concatenate([value, beyond], axis=1))
            rhs[8 * r0 : 8 * r0 + 16, :] = jnp.concatenate(pair, axis=0).astype(BF)
        prod_1[...] = jnp.dot(band[g], rhs[0:128, :], preferred_element_type=F32)
        prod_2[...] = jnp.dot(band[g], rhs[80:208, :], preferred_element_type=F32)
        prod_3[...] = jnp.dot(band_up[g], rhs[96:224, :], preferred_element_type=F32)
        sides = [jnp.zeros((8, LANES), F32)] * 2
        for o in range(mid):
            if o < 10:
                prod, step, i = prod_1, 80, o
            elif o < rows + 3:
                prod, step, i = prod_2, 80, o - 10
            else:
                prod, step, i = prod_3, 32, o - 18
            inner = outer = None
            for q in range(7):
                part = slice(q * step + 8 * i, q * step + 8 * i + 8)
                mine, edge = prod[part, wide[0]], prod[part, wide[1]]
                if q != 3:
                    swap = edge_mask(lane, q - 3)
                    mine, edge = jnp.where(swap, edge, mine), jnp.where(swap, mine, edge)
                    mine, edge = shift(mine, 3 - q), shift(edge, 3 - q)
                inner = mine if inner is None else inner + mine
                outer = edge if outer is None else outer + edge
            if o < 3:
                conv_halo[at_row(o, g), :] = inner
            elif o < rows + 3:
                conv[at_row(o - 3, g), :] = inner
            else:
                conv_halo[at_row(o - rows, g), :] = inner
            inside = (lane >= 3 * o) & (lane < 3 * o + 3)
            sides[0] = jnp.where(inside, shift(outer, 3 * o + 3), sides[0])
            sides[1] = jnp.where(inside, shift(outer, 3 * o), sides[1])
        for k in (0, 1):
            conv_halo[at_row(6 + k, g), :] = sides[k]
        return 0

    lax.fori_loop(0, groups, conv_group, 0)

    g_down[...] = jnp.zeros_like(g_down)
    g_up[...] = jnp.zeros_like(g_up)
    sums[...] = jnp.zeros_like(sums)

    def unit(u):
        return pl.ds(pl.multiple_of(u * chans, chans), chans)

    def own_block(b, _):
        units = (b * 2, b * 2 + 1)
        x = jnp.concatenate([conv[unit(u), :] for u in units], axis=1)
        g = jnp.concatenate([gt[u].astype(F32) for u in units], axis=1)
        dx, (pre, cdf, d_branch, d_pre, d_normed, normed, xhat, scale) = norm_and_back(
            x, g, vecs, up_aug, up_t, down_t
        )
        hidden = (pre * cdf).astype(BF)
        branch = jnp.dot(down[...], hidden, preferred_element_type=F32)
        sea = [mask[pl.ds(u, 1), :].astype(F32) for u in units]
        fields = jnp.concatenate([ft[u].astype(F32) for u in units], axis=1)
        res = (fields + scale * branch) * jnp.concatenate(sea, axis=1)
        for k, u in enumerate(units):
            for gr in range(groups):
                plane[pl.ds(gr * 8 * rows + u, 8, stride=rows), :] = res[gr * 8 : gr * 8 + 8, wide[k]]
            dcv[unit(u), :] = dx[:, wide[k]]
        g_down[...] += lax.dot_general(d_branch, hidden, NT, preferred_element_type=F32)
        g_up[...] += lax.dot_general(normed, d_pre, NT, preferred_element_type=F32)
        for k, value in enumerate((d_normed * xhat, d_normed, g * branch)):
            sums[k] += value[:, :LANES] + value[:, LANES:]
        return 0

    lax.fori_loop(0, rows // 2, own_block, 0, unroll=2)

    def taps_group(g, _):
        at = pl.ds(pl.multiple_of(g * 8, 8), 8)
        line = jnp.zeros((8, LANES), F32)
        for q in range(7):
            own = [shift(dcv[at_row(o, g), :], q - 3) for o in range(rows)]
            tot = [None] * 7
            for r in range(mid):
                value = ext[at_row(r + 3, g), :]
                if q != 3:
                    value = jnp.where(edge_mask(lane, q - 3), rim[at_row(r + 3, g), :], value)
                for a in range(7):
                    o = r - a
                    if 0 <= o < rows:
                        term = value * own[o]
                        tot[a] = term if tot[a] is None else tot[a] + term
            for a in range(7):
                total = jnp.sum(tot[a], axis=1, keepdims=True)
                line = jnp.where(lane == 8 * a + q, total, line)
        for k in range(3):
            total = jnp.sum(sums[k, at, :], axis=1, keepdims=True)
            line = jnp.where(lane == 56 + k, total, line)
        taps_g[at, :] = line
        return 0

    lax.fori_loop(0, groups, taps_group, 0)
    small = taps_g[...]
    cut = 40

    def fill(lower, upper):
        for h, w in enumerate(wide):
            lower[h * chans : (h + 1) * chans, :] = g_down[:, w]
            upper[h * chans : (h + 1) * chans, :] = g_up[0:chans, w]
            upper[2 * chans + 24 + 8 * h : 2 * chans + 32 + 8 * h, :] = g_up[chans : chans + 8, w]
        lower[2 * chans : 2 * chans + cut, :] = small[:cut]
        upper[2 * chans : 2 * chans + 24, :] = small[cut:]

    @pl.when(odd_core == 0)
    def _():
        fill(kept, passed)

    @pl.when(odd_core == 1)
    def _():
        fill(passed, kept)

    for c in range(chans):
        out[c] = plane[c * rows : (c + 1) * rows, :].astype(BF)


def halo_kernel(conv_halo, low, up, got_l, got_r, vecs, up_aug, up_t, down_t, dcv_halo, cots):
    _, chans, _ = low.shape
    lane_c = lane_iota((chans, LANES))
    wide = slice(0, LANES), slice(LANES, 2 * LANES)
    for r in range(3):
        cots[r * chans : (r + 1) * chans, :] = low[6 + r].astype(F32)
        cots[(3 + r) * chans : (4 + r) * chans, :] = up[6 + r].astype(F32)
    for k, got in ((0, got_l), (1, got_r)):
        first = shift(got[:, wide[0]].astype(F32), -84)
        second = shift(got[:, wide[1]].astype(F32), 33 - 84)
        value = jnp.where(lane_c < 33, first, jnp.where(lane_c < 66, second, 0.0))
        cots[(6 + k) * chans : (7 + k) * chans, :] = value

    def halo_block(b, _):
        units = [pl.ds(pl.multiple_of((2 * b + k) * chans, chans), chans) for k in (0, 1)]
        x = jnp.concatenate([conv_halo[u, :] for u in units], axis=1)
        g = jnp.concatenate([cots[u, :] for u in units], axis=1)
        dx, _ = norm_and_back(x, g, vecs, up_aug, up_t, down_t)
        for k, u in enumerate(units):
            dcv_halo[u, :] = dx[:, wide[k]]
        return 0

    lax.fori_loop(0, 4, halo_block, 0, unroll=2)


def adjoint_kernel(part, *refs):
    dcv, dcv_halo, gt, plain, turned = refs[:5]
    grad, rhs, plane, band, band_up, prod_1, prod_3 = refs[-7:]
    rows, chans, cols = gt.shape
    some = grad.shape[0]
    first = part * (some // 8)
    mid = rows + 6
    top = lax.axis_index("lat") == lax.axis_size("lat") - 1
    lane = lane_iota((8, LANES))
    wide = slice(0, LANES), slice(LANES, 2 * LANES)
    at_row = lambda r, g: rows_of(r, g, chans)

    def adjoint_group(g, _):
        at = pl.ds(pl.multiple_of(g * 8, 8), 8)
        left, right = dcv_halo[at_row(6, g), :], dcv_halo[at_row(7, g), :]
        for r0 in range(0, mid, 2):
            pair = []
            for r in (r0, r0 + 1):
                if r < 3:
                    value = dcv_halo[at_row(r, g), :]
                elif r < rows + 3:
                    value = dcv[at_row(r - 3, g), :]
                else:
                    value = dcv_halo[at_row(r - rows, g), :]
                beyond = jnp.where(lane < 64, shift(right, -3 * r), shift(left, LANES - 3 - 3 * r))
                pair.append(jnp.concatenate([value, beyond], axis=1))
            rhs[8 * r0 : 8 * r0 + 16, :] = jnp.concatenate(pair, axis=0).astype(BF)
        for q in range(7):
            one, two = turned[q, at, :], plain[q, at, :]
            above = jnp.where(top, two, one)
            moved = [pltpu.roll(one, 8 * i, 1, stride=1, stride_axis=0) for i in range(10)]
            band[q * 80 : q * 80 + 80, :] = jnp.concatenate(moved, axis=0).astype(BF)
            late = moved[:3]
            for i in range(3, 6):
                other = pltpu.roll(above, 8 * i, 1, stride=1, stride_axis=0)
                late.append(jnp.where(lane >= 8 * (rows + 3 - 10), other, moved[i]))
            band_up[q * 48 : q * 48 + 48, :] = jnp.concatenate(late, axis=0).astype(BF)
        prod_1[...] = jnp.dot(band[...], rhs[0:128, :], preferred_element_type=F32)
        prod_3[...] = jnp.dot(band_up[:, 0:96], rhs[80:176, :], preferred_element_type=F32)
        for o in range(rows):
            prod, step, i = (prod_1, 80, o) if o < 10 else (prod_3, 48, o - 10)
            inner = gt[o, at, :].astype(F32)
            for q in range(7):
                part = slice(q * step + 8 * i, q * step + 8 * i + 8)
                mine = prod[part, wide[0]]
                if q != 3:
                    mine = shift(jnp.where(edge_mask(lane, q - 3), prod[part, wide[1]], mine), 3 - q)
                inner = inner + mine
            plane[pl.ds((g - first) * (8 * rows) + o, 8, stride=rows), :] = inner
        return 0

    lax.fori_loop(first, first + some // 8, adjoint_group, 0)
    for c in range(some):
        grad[c] = plane[c * rows : (c + 1) * rows, :].astype(BF)


def finish_kernel(total, other, g_depth, g_gain, g_bias, g_up, g_up_b, g_down, g_scale):
    chans, hidden_n = g_down.shape

    def unpack(lower, upper):
        for h in range(hidden_n // LANES):
            w = slice(h * LANES, (h + 1) * LANES)
            g_down[:, w] = lower[h * chans : (h + 1) * chans, :]
            g_up[:, w] = upper[h * chans : (h + 1) * chans, :]
            at = 2 * chans + 24 + 8 * h
            g_up_b[w] = upper[at : at + 1, :].reshape(LANES)
        small = jnp.concatenate(
            [
                lower[2 * chans : 2 * chans + 40, :],
                upper[2 * chans : 2 * chans + 24, :],
                jnp.zeros((LANES - chans, LANES), F32),
            ],
            axis=0,
        ).T
        for k, dst in enumerate((g_gain, g_bias, g_scale)):
            dst[...] = small[56 + k : 57 + k, :chans].reshape(chans)
        for a in range(7):
            g_depth[a] = small[8 * a : 8 * a + 7, :chans]

    odd_core = lax.axis_index("lon") % 2

    @pl.when(odd_core == 0)
    def _():
        unpack(total, other)

    @pl.when(odd_core == 1)
    def _():
        unpack(other, total)


def vmem(n):
    return [pl.BlockSpec(memory_space=pltpu.VMEM)] * n


def shards(
    fields,
    cotangent,
    ocean_mask,
    seam_partner,
    depth_weight,
    norm_gain,
    layer_norm_bias,
    up_weight,
    up_bias,
    down_weight,
    layer_scale,
):
    _, chans, rows, cols = fields.shape
    hidden_n = up_weight.shape[0]
    n_lon, n_lat = lax.axis_size("lon"), lax.axis_size("lat")
    sds = jax.ShapeDtypeStruct
    hbm = pl.BlockSpec(memory_space=pltpu.HBM)
    ft, gt, first, second, partner, turn = pl.pallas_call(
        pack_kernel,
        out_shape=[sds((rows, chans, cols), BF)] * 2
        + [sds((9, chans, cols), BF)] * 2
        + [sds((1, cols), jnp.int32), sds((1,), jnp.int32)],
        in_specs=[hbm] * 4,
        out_specs=vmem(5) + [hbm],
        scratch_shapes=[
            pltpu.VMEM((2, chans * rows, cols), F32),
            pltpu.VMEM((chans, rows, cols), BF),
            pltpu.VMEM((chans, rows, cols), BF),
            pltpu.VMEM((rows, cols), jnp.int32),
            pltpu.SMEM((1, cols), jnp.int32),
            pltpu.SMEM((1,), jnp.int32),
            pltpu.SemaphoreType.DMA((6,)),
        ],
        compiler_params=pltpu.CompilerParams(vmem_limit_bytes=8 * 2**20),
        name="pack",
    )(
        *[
            pltpu.with_memory_space_constraint(v, pltpu.HBM)
            for v in (seam_partner.reshape(n_lon, cols), fields[0], cotangent[0], ocean_mask)
        ]
    )

    at = lambda lon, lat: (lon % n_lon) * n_lat + lat
    rounds = [[], []]
    for lat in range(n_lat - 1):
        for lon in range(n_lon):
            rounds[lat % 2] += [(at(lon, lat), at(lon, lat + 1)), (at(lon, lat + 1), at(lon, lat))]
    fold_round = (n_lat - 1) % 2

    axes = ("lon", "lat")
    plain_round = 1 - fold_round
    sends = (first, second)
    met = lax.ppermute(sends[plain_round], axes, rounds[plain_round])
    top = sends[fold_round]

    def exchange(k):
        def run(top):
            mirror = [
                [(at(lon, n_lat - 1), at(k - j - lon, n_lat - 1)) for lon in range(n_lon)] for j in (0, 1)
            ]
            plan = rounds[fold_round] + mirror[0]
            return lax.ppermute(top, axes, mirror[1]), lax.ppermute(top, axes, plan)

        return run

    got_c, folded = lax.switch(turn[0], [exchange(k) for k in range(n_lon)], top)
    got_a, got_b = (folded, met) if fold_round == 0 else (met, folded)
    low, up, sent_l, sent_r = pl.pallas_call(
        functools.partial(edge_kernel, fold_round == 0),
        out_shape=[sds((9, chans, cols), BF)] * 2 + [sds((chans, 2 * cols), BF)] * 2,
        in_specs=vmem(6),
        out_specs=vmem(4),
        compiler_params=pltpu.CompilerParams(vmem_limit_bytes=8 * 2**20),
        name="edges",
    )(partner, got_a, got_b, got_c, ft, gt)
    got_l = lax.ppermute(sent_r, "lon", [(i, (i + 1) % n_lon) for i in range(n_lon)])
    got_r = lax.ppermute(sent_l, "lon", [(i, (i - 1) % n_lon) for i in range(n_lon)])

    plain, turned, vecs, up_aug, down_t, band, band_up = pl.pallas_call(
        weight_kernel,
        out_shape=[
            sds((7, chans, LANES), F32),
            sds((7, chans, LANES), F32),
            sds((3, chans, LANES), F32),
            sds((hidden_n, chans + 16), BF),
            sds((hidden_n, chans), BF),
            sds((chans // 8, 7 * 80, LANES), BF),
            sds((chans // 8, 7 * 32, LANES), BF),
        ],
        in_specs=vmem(7),
        out_specs=vmem(7),
        scratch_shapes=[pltpu.VMEM((2, 7, LANES, LANES), F32)],
        compiler_params=pltpu.CompilerParams(vmem_limit_bytes=8 * 2**20),
        name="weights",
    )(
        depth_weight.transpose(1, 2, 0),
        norm_gain,
        layer_norm_bias,
        layer_scale,
        up_bias,
        up_weight.T,
        down_weight,
    )
    big, small = 2 * chans, 40
    up_t = up_weight.T
    band_rows = (rows + 12) * 8
    output, conv_halo, dcv, kept, passed = pl.pallas_call(
        own_kernel,
        out_shape=[
            sds((chans, rows, cols), BF),
            sds((8 * chans, cols), F32),
            sds((rows * chans, cols), F32),
            sds((big + small, LANES), F32),
            sds((big + small, LANES), F32),
        ],
        in_specs=vmem(14),
        out_specs=vmem(5),
        scratch_shapes=[
            pltpu.VMEM(((rows + 12) * chans, cols), F32),
            pltpu.VMEM(((rows + 12) * chans, cols), F32),
            pltpu.VMEM((band_rows, 2 * cols), BF),
            pltpu.VMEM((rows * chans, cols), F32),
            pltpu.VMEM((chans * rows, cols), F32),
            pltpu.VMEM((7 * 80, 2 * cols), F32),
            pltpu.VMEM((7 * 80, 2 * cols), F32),
            pltpu.VMEM((7 * 32, 2 * cols), F32),
            pltpu.VMEM((chans, hidden_n), F32),
            pltpu.VMEM((chans + 16, hidden_n), F32),
            pltpu.VMEM((3, chans, LANES), F32),
            pltpu.VMEM((chans, LANES), F32),
        ],
        compiler_params=pltpu.CompilerParams(vmem_limit_bytes=20 * 2**20),
        name="own",
    )(
        ft,
        gt,
        low,
        up,
        got_l,
        got_r,
        ocean_mask,
        band,
        band_up,
        vecs,
        up_aug,
        up_t,
        down_weight,
        down_t,
    )

    dcv_halo = pl.pallas_call(
        halo_kernel,
        out_shape=sds((8 * chans, cols), F32),
        in_specs=vmem(9),
        out_specs=vmem(1)[0],
        scratch_shapes=[pltpu.VMEM((8 * chans, cols), F32)],
        cost_estimate=pl.CostEstimate(flops=150_000_000, bytes_accessed=2**20, transcendentals=2**18),
        compiler_params=pltpu.CompilerParams(vmem_limit_bytes=8 * 2**20),
        name="halo",
    )(conv_halo, low, up, got_l, got_r, vecs, up_aug, up_t, down_t)

    def adjoint(part, *earlier):
        half = chans // 2
        return pl.pallas_call(
            functools.partial(adjoint_kernel, part),
            grid=(1,),
            out_shape=sds((chans, rows, cols), BF),
            in_specs=vmem(5) + [pl.BlockSpec(memory_space=pl.ANY)] * len(earlier),
            out_specs=pl.BlockSpec((half, rows, cols), lambda _: (part, 0, 0)),
            scratch_shapes=[
                pltpu.VMEM((band_rows, 2 * cols), BF),
                pltpu.VMEM((half * rows, cols), F32),
                pltpu.VMEM((7 * 80, LANES), BF),
                pltpu.VMEM((7 * 48, LANES), BF),
                pltpu.VMEM((7 * 80, 2 * cols), F32),
                pltpu.VMEM((7 * 48, 2 * cols), F32),
            ],
            input_output_aliases={5: 0} if earlier else {},
            cost_estimate=pl.CostEstimate(flops=200_000_000, bytes_accessed=2**21, transcendentals=0),
            compiler_params=pltpu.CompilerParams(vmem_limit_bytes=12 * 2**20),
            name="adjoint",
        )(dcv, dcv_halo, gt, plain, turned, *earlier)

    flip = lambda y, axis, b: lax.ppermute(y, axis, [(i, i ^ b) for i in range(lax.axis_size(axis))])
    total = kept + flip(passed, "lon", 1)
    steps = [("lon", 1 << i) for i in range(1, n_lon.bit_length() - 1)]
    steps += [("lat", 1 << i) for i in range(n_lat.bit_length() - 1)]
    grad = None
    for k, (axis, b) in enumerate(steps):
        if axis == "lat" and b > 1:
            mine = total.astype(BF)
            total = lax.reduce_precision(total, 8, 7) + flip(mine, axis, b).astype(F32)
        else:
            total = total + flip(total, axis, b)
        if k == 0:
            total, dcv_halo = lax.optimization_barrier((total, dcv_halo))
        elif k == 1:
            grad = adjoint(0)
            total, grad = lax.optimization_barrier((total, grad))
        elif k == 2:
            grad = adjoint(1, grad)
            total, grad = lax.optimization_barrier((total, grad))
    other = flip(total, "lon", 1)
    g_depth, g_gain, g_bias, g_up, g_up_b, g_down, g_scale = pl.pallas_call(
        finish_kernel,
        out_shape=[
            sds((7, 7, chans), F32),
            sds((chans,), F32),
            sds((chans,), F32),
            sds((chans, hidden_n), F32),
            sds((hidden_n,), F32),
            sds((chans, hidden_n), F32),
            sds((chans,), F32),
        ],
        in_specs=vmem(2),
        out_specs=vmem(7),
        compiler_params=pltpu.CompilerParams(vmem_limit_bytes=6 * 2**20),
        name="finish",
    )(total, other)
    return (
        output[None],
        grad[None],
        g_depth.transpose(2, 0, 1),
        g_gain,
        g_bias,
        g_up.T,
        g_up_b,
        g_down,
        g_scale,
    )


def solution(mesh):
    block = P(None, None, "lat", "lon")
    placed = (block, block, P("lat", "lon")) + (P(),) * 8
    return jax.shard_map(
        shards, mesh=mesh, in_specs=placed, out_specs=(block, block) + (P(),) * 7, check_vma=False
    )
```

```python
import functools
import math

import jax
import jax.numpy as jnp
from jax import lax
from jax.experimental import pallas as pl
from jax.experimental.pallas import tpu as pltpu
from jax.sharding import PartitionSpec as P

BF = jnp.bfloat16
F32 = jnp.float32
LANES = 128
NT = (((1,), (1,)), ((), ()))


def shift(x, amount, axis=1):
    size = x.shape[axis]
    amount %= size
    return x if amount == 0 else pltpu.roll(x, amount, axis)


def lane_iota(shape):
    return lax.broadcasted_iota(jnp.int32, shape, 1)


def pack_kernel(
    seam, fields_far, cot_far, mask_far, ft, gt, first, second, partner, turn, *scratch
):
    plane, fields, cot, mask, head, index, arrived = scratch
    chans, rows, cols = fields.shape
    groups = chans // 8
    pairs = (
        (fields_far, fields),
        (cot_far, cot),
        (mask_far, mask),
        (seam.at[pl.ds(0, 1), :], head),
        (seam.at[pl.ds(lax.axis_index("lon"), 1), :], partner),
    )
    copies = [pltpu.make_async_copy(src, dst, arrived.at[k]) for k, (src, dst) in enumerate(pairs)]
    for k in (3, 0, 1, 2, 4):
        copies[k].start()
    copies[3].wait()
    index[0] = head[0, 0] // cols
    answer = pltpu.make_async_copy(index, turn, arrived.at[5])
    answer.start()
    for k, dst in ((0, ft), (1, gt)):
        copies[k].wait()
        if k == 1:
            copies[2].wait()
            sea = mask[...].astype(F32)
        for c in range(chans):
            if k == 0:
                cell = fields[c].astype(F32)
            else:
                cell = cot[c].astype(F32) * sea
            plane[k, c * rows : (c + 1) * rows, :] = cell
        for r in range(rows):
            parts = [plane[k, pl.ds(g * 8 * rows + r, 8, stride=rows), :] for g in range(groups)]
            dst[r] = jnp.concatenate(parts, axis=0).astype(BF)

    def edge(dst, top):
        base = rows - 6 if top else 0
        gbase = rows - 3 if top else 0
        dst[0:6] = ft[base : base + 6]
        dst[6:9] = gt[gbase : gbase + 3]

    odd = lax.axis_index("lat") % 2

    @pl.when(odd == 0)
    def _():
        edge(first, True)
        edge(second, False)

    @pl.when(odd == 1)
    def _():
        edge(first, False)
        edge(second, True)

    copies[4].wait()
    answer.wait()


def field_lane(r):
    return LANES * (r // 14) + 6 * (r % 14)


def cot_lane(g):
    return LANES * (g // 11) + 84 + 3 * (g % 11)


def edge_kernel(fold_first, partner, got_a, got_b, got_c, ft, gt, low, up, sent_l, sent_r):
    rows, chans, cols = ft.shape
    total = lax.axis_size("lon") * cols
    z = lax.axis_index("lat")
    odd = z % 2
    top = z == lax.axis_size("lat") - 1

    @pl.when(odd == 1)
    def _():
        low[...] = got_a[...]

    @pl.when(odd == 0)
    def _():
        low[...] = got_b[...]

    @pl.when(top)
    def _():
        got_1 = got_a if fold_first else got_b
        src = lax.broadcasted_iota(jnp.int32, (cols, cols), 0)
        want = jnp.broadcast_to(partner[...], (cols, cols))
        leading = jnp.broadcast_to(partner[:, 0:1], (cols, cols))
        near = leading - lax.rem(leading, jnp.full_like(leading, cols))
        far = jnp.where(near == 0, total, near) - cols
        pick_1 = (src + near == want).astype(F32).astype(BF)
        pick_2 = (src + far == want).astype(F32).astype(BF)
        mixed = jnp.dot(got_1[...].reshape(9 * chans, cols), pick_1, preferred_element_type=F32)
        mixed = mixed + jnp.dot(got_c[...].reshape(9 * chans, cols), pick_2, preferred_element_type=F32)
        for k in range(9):
            m = 5 - k if k < 6 else 14 - k
            up[k] = mixed[m * chans : (m + 1) * chans].astype(BF)

    @pl.when(jnp.logical_not(top) & (odd == 0))
    def _():
        up[...] = got_a[...]

    @pl.when(jnp.logical_not(top) & (odd == 1))
    def _():
        up[...] = got_b[...]

    lane = lane_iota((chans, LANES))
    acc = {key: jnp.zeros((chans, LANES), F32) for key in ((0, 0), (0, 1), (1, 0), (1, 1))}

    def place(side, value, source, lane_to, width):
        half, at = lane_to // LANES, lane_to % LANES
        moved = shift(value, at - source)
        acc[side, half] = jnp.where((lane >= at) & (lane < at + width), moved, acc[side, half])

    for r in range(rows + 12):
        if r < 6:
            value = low[r]
        elif r < rows + 6:
            value = ft[r - 6]
        else:
            value = up[r - rows - 6]
        value = value.astype(F32)
        place(1, value, cols - 6, field_lane(r), 6)
        place(0, value, 0, field_lane(r), 6)
    for r in range(rows + 6):
        if r < 3:
            value = low[6 + r]
        elif r < rows + 3:
            value = gt[r - 3]
        else:
            value = up[6 + r - rows - 3]
        value = value.astype(F32)
        place(1, value, cols - 3, cot_lane(r), 3)
        place(0, value, 0, cot_lane(r), 3)
    for side, dst in ((0, sent_l), (1, sent_r)):
        dst[...] = jnp.concatenate([acc[side, 0], acc[side, 1]], axis=1).astype(BF)


def weight_kernel(
    taps, gain, bias, scale, up_b, up_t, down, plain, turned, vecs, up_aug, down_t, band, band_up, line
):
    chans, hidden_n = up_t.shape
    top = lax.axis_index("lat") == lax.axis_size("lat") - 1
    line[...] = jnp.zeros_like(line)
    for a in range(7):
        block = taps[a].astype(F32)
        for q in range(7):
            line[0, q, 8 * a : 8 * a + 1, 0:chans] = block[q : q + 1]
            line[1, 6 - q, 48 - 8 * a : 49 - 8 * a, 0:chans] = block[q : q + 1]
    for q in range(7):
        plain[q] = line[0, q].T[:chans]
        turned[q] = line[1, q].T[:chans]

    def spread(g, _):
        at = pl.ds(pl.multiple_of(g * 8, 8), 8)
        for q in range(7):
            one, two = plain[q, at, :], turned[q, at, :]
            above = jnp.where(top, two, one)
            band[g, q * 80 : q * 80 + 80, :] = jnp.concatenate(
                [pltpu.roll(one, 8 * i, 1, stride=1, stride_axis=0) for i in range(10)], axis=0
            ).astype(BF)
            band_up[g, q * 32 : q * 32 + 32, :] = jnp.concatenate(
                [pltpu.roll(above, 8 * i, 1, stride=1, stride_axis=0) for i in range(6, 10)], axis=0
            ).astype(BF)
        return 0

    lax.fori_loop(0, chans // 8, spread, 0)
    wide = LANES - chans
    columns = jnp.concatenate(
        [v[...].astype(F32).reshape(1, chans) for v in (gain, bias, scale)] + [jnp.zeros((5, chans), F32)],
        axis=0,
    )
    columns = jnp.concatenate([columns, jnp.zeros((8, wide), F32)], axis=1).T
    for k in range(3):
        vecs[k] = jnp.broadcast_to(columns[:chans, k : k + 1], (chans, LANES))
    tall = jnp.concatenate(
        [
            up_t[...].astype(F32),
            up_b[...].astype(F32).reshape(1, hidden_n),
            jnp.zeros((wide - 1, hidden_n), F32),
        ],
        axis=0,
    )
    up_aug[...] = tall.T[:, : chans + 16].astype(BF)
    tall = jnp.concatenate([down[...].astype(F32), jnp.zeros((wide, hidden_n), F32)], axis=0)
    down_t[...] = tall.T[:, :chans].astype(BF)


def normal_terms(v):
    cdf = 0.5 * (1.0 + lax.erf(v * (1.0 / math.sqrt(2.0))))
    dens = jnp.exp2(v * v * (-0.5 / math.log(2.0)) - 0.5 * math.log2(2.0 * math.pi))
    return cdf, dens


def edge_mask(lane, s):
    return lane < s if s > 0 else lane >= LANES + s


def rows_of(r, g, chans):
    return pl.ds(pl.multiple_of(r * chans + g * 8, 8), 8)


def twice(x):
    return jnp.concatenate([x, x], axis=1)


def norm_and_back(x, g, vecs, up_aug, up_t, down_t):
    gain, bias, scale = twice(vecs[0]), twice(vecs[1]), twice(vecs[2])
    centred = x - jnp.mean(x, axis=0, keepdims=True)
    var = jnp.mean(centred * centred, axis=0, keepdims=True)
    rstd = lax.rsqrt(var + 1e-06)
    xhat = centred * rstd
    pad = (up_aug.shape[1] - x.shape[0], x.shape[1])
    ones = (lax.broadcasted_iota(jnp.int32, pad, 0) == 0).astype(F32).astype(BF)
    normed = jnp.concatenate([(xhat * gain + bias).astype(BF), ones], axis=0)
    pre = jnp.dot(up_aug[...], normed, preferred_element_type=F32)
    cdf, dens = normal_terms(pre)
    d_branch = (g * scale).astype(BF)
    d_hidden = jnp.dot(down_t[...], d_branch, preferred_element_type=F32)
    d_pre = (d_hidden * (cdf + pre * dens)).astype(BF)
    d_normed = jnp.dot(up_t[...], d_pre, preferred_element_type=F32)
    gd = d_normed * gain
    m1 = jnp.mean(gd, axis=0, keepdims=True)
    m2 = jnp.mean(gd * xhat, axis=0, keepdims=True)
    dx = (rstd * (gd - m1 - xhat * m2)).astype(BF).astype(F32)
    return dx, (pre, cdf, d_branch, d_pre, d_normed, normed, xhat, scale)


def own_kernel(
    ft,
    gt,
    low,
    up,
    got_l,
    got_r,
    mask,
    band,
    band_up,
    vecs,
    up_aug,
    up_t,
    down,
    down_t,
    out,
    conv_halo,
    dcv,
    kept,
    passed,
    ext,
    rim,
    rhs,
    conv,
    plane,
    prod_1,
    prod_2,
    prod_3,
    g_down,
    g_up,
    sums,
    taps_g,
):
    rows, chans, cols = ft.shape
    groups = chans // 8
    mid = rows + 6
    odd_core = lax.axis_index("lon") % 2
    lane = lane_iota((8, LANES))
    wide = slice(0, LANES), slice(LANES, 2 * LANES)
    at_row = lambda r, g: rows_of(r, g, chans)

    def conv_group(g, _):
        at = pl.ds(pl.multiple_of(g * 8, 8), 8)
        left = [got_l[at, w].astype(F32) for w in wide]
        right = [got_r[at, w].astype(F32) for w in wide]
        for r0 in range(0, rows + 12, 2):
            pair = []
            for r in (r0, r0 + 1):
                if r < 6:
                    value = low[r, at, :]
                elif r < rows + 6:
                    value = ft[r - 6, at, :]
                else:
                    value = up[r - rows - 6, at, :]
                value = value.astype(F32)
                half, start = field_lane(r) // LANES, field_lane(r) % LANES
                beyond = jnp.where(lane < 64, shift(right[half], -start), shift(left[half], LANES - 6 - start))
                ext[at_row(r, g), :] = value
                rim[at_row(r, g), :] = beyond
                pair.append(jnp.concatenate([value, beyond], axis=1))
            rhs[8 * r0 : 8 * r0 + 16, :] = jnp.concatenate(pair, axis=0).astype(BF)
        prod_1[...] = jnp.dot(band[g], rhs[0:128, :], preferred_element_type=F32)
        prod_2[...] = jnp.dot(band[g], rhs[80:208, :], preferred_element_type=F32)
        prod_3[...] = jnp.dot(band_up[g], rhs[96:224, :], preferred_element_type=F32)
        sides = [jnp.zeros((8, LANES), F32)] * 2
        for o in range(mid):
            if o < 10:
                prod, step, i = prod_1, 80, o
            elif o < rows + 3:
                prod, step, i = prod_2, 80, o - 10
            else:
                prod, step, i = prod_3, 32, o - 18
            inner = outer = None
            for q in range(7):
                part = slice(q * step + 8 * i, q * step + 8 * i + 8)
                mine, edge = prod[part, wide[0]], prod[part, wide[1]]
                if q != 3:
                    swap = edge_mask(lane, q - 3)
                    mine, edge = jnp.where(swap, edge, mine), jnp.where(swap, mine, edge)
                    mine, edge = shift(mine, 3 - q), shift(edge, 3 - q)
                inner = mine if inner is None else inner + mine
                outer = edge if outer is None else outer + edge
            if o < 3:
                conv_halo[at_row(o, g), :] = inner
            elif o < rows + 3:
                conv[at_row(o - 3, g), :] = inner
            else:
                conv_halo[at_row(o - rows, g), :] = inner
            inside = (lane >= 3 * o) & (lane < 3 * o + 3)
            sides[0] = jnp.where(inside, shift(outer, 3 * o + 3), sides[0])
            sides[1] = jnp.where(inside, shift(outer, 3 * o), sides[1])
        for k in (0, 1):
            conv_halo[at_row(6 + k, g), :] = sides[k]
        return 0

    lax.fori_loop(0, groups, conv_group, 0)

    g_down[...] = jnp.zeros_like(g_down)
    g_up[...] = jnp.zeros_like(g_up)
    sums[...] = jnp.zeros_like(sums)

    def unit(u):
        return pl.ds(pl.multiple_of(u * chans, chans), chans)

    def own_block(b, _):
        units = (b * 2, b * 2 + 1)
        x = jnp.concatenate([conv[unit(u), :] for u in units], axis=1)
        g = jnp.concatenate([gt[u].astype(F32) for u in units], axis=1)
        dx, (pre, cdf, d_branch, d_pre, d_normed, normed, xhat, scale) = norm_and_back(
            x, g, vecs, up_aug, up_t, down_t
        )
        hidden = (pre * cdf).astype(BF)
        branch = jnp.dot(down[...], hidden, preferred_element_type=F32)
        sea = [mask[pl.ds(u, 1), :].astype(F32) for u in units]
        fields = jnp.concatenate([ft[u].astype(F32) for u in units], axis=1)
        res = (fields + scale * branch) * jnp.concatenate(sea, axis=1)
        for k, u in enumerate(units):
            for gr in range(groups):
                plane[pl.ds(gr * 8 * rows + u, 8, stride=rows), :] = res[gr * 8 : gr * 8 + 8, wide[k]]
            dcv[unit(u), :] = dx[:, wide[k]]
        g_down[...] += lax.dot_general(d_branch, hidden, NT, preferred_element_type=F32)
        g_up[...] += lax.dot_general(normed, d_pre, NT, preferred_element_type=F32)
        for k, value in enumerate((d_normed * xhat, d_normed, g * branch)):
            sums[k] += value[:, :LANES] + value[:, LANES:]
        return 0

    lax.fori_loop(0, rows // 2, own_block, 0, unroll=2)

    def taps_group(g, _):
        at = pl.ds(pl.multiple_of(g * 8, 8), 8)
        line = jnp.zeros((8, LANES), F32)
        for q in range(7):
            own = [shift(dcv[at_row(o, g), :], q - 3) for o in range(rows)]
            tot = [None] * 7
            for r in range(mid):
                value = ext[at_row(r + 3, g), :]
                if q != 3:
                    value = jnp.where(edge_mask(lane, q - 3), rim[at_row(r + 3, g), :], value)
                for a in range(7):
                    o = r - a
                    if 0 <= o < rows:
                        term = value * own[o]
                        tot[a] = term if tot[a] is None else tot[a] + term
            for a in range(7):
                total = jnp.sum(tot[a], axis=1, keepdims=True)
                line = jnp.where(lane == 8 * a + q, total, line)
        for k in range(3):
            total = jnp.sum(sums[k, at, :], axis=1, keepdims=True)
            line = jnp.where(lane == 56 + k, total, line)
        taps_g[at, :] = line
        return 0

    lax.fori_loop(0, groups, taps_group, 0)
    small = taps_g[...]
    cut = 40

    def fill(lower, upper):
        for h, w in enumerate(wide):
            lower[h * chans : (h + 1) * chans, :] = g_down[:, w]
            upper[h * chans : (h + 1) * chans, :] = g_up[0:chans, w]
            upper[2 * chans + 24 + 8 * h : 2 * chans + 32 + 8 * h, :] = g_up[chans : chans + 8, w]
        lower[2 * chans : 2 * chans + cut, :] = small[:cut]
        upper[2 * chans : 2 * chans + 24, :] = small[cut:]

    @pl.when(odd_core == 0)
    def _():
        fill(kept, passed)

    @pl.when(odd_core == 1)
    def _():
        fill(passed, kept)

    for c in range(chans):
        out[c] = plane[c * rows : (c + 1) * rows, :].astype(BF)


def halo_kernel(conv_halo, low, up, got_l, got_r, vecs, up_aug, up_t, down_t, dcv_halo, cots):
    _, chans, _ = low.shape
    lane_c = lane_iota((chans, LANES))
    wide = slice(0, LANES), slice(LANES, 2 * LANES)
    for r in range(3):
        cots[r * chans : (r + 1) * chans, :] = low[6 + r].astype(F32)
        cots[(3 + r) * chans : (4 + r) * chans, :] = up[6 + r].astype(F32)
    for k, got in ((0, got_l), (1, got_r)):
        first = shift(got[:, wide[0]].astype(F32), -84)
        second = shift(got[:, wide[1]].astype(F32), 33 - 84)
        value = jnp.where(lane_c < 33, first, jnp.where(lane_c < 66, second, 0.0))
        cots[(6 + k) * chans : (7 + k) * chans, :] = value

    def halo_block(b, _):
        units = [pl.ds(pl.multiple_of((2 * b + k) * chans, chans), chans) for k in (0, 1)]
        x = jnp.concatenate([conv_halo[u, :] for u in units], axis=1)
        g = jnp.concatenate([cots[u, :] for u in units], axis=1)
        dx, _ = norm_and_back(x, g, vecs, up_aug, up_t, down_t)
        for k, u in enumerate(units):
            dcv_halo[u, :] = dx[:, wide[k]]
        return 0

    lax.fori_loop(0, 4, halo_block, 0, unroll=2)


def adjoint_kernel(part, *refs):
    dcv, dcv_halo, gt, plain, turned = refs[:5]
    grad, rhs, plane, band, band_up, prod_1, prod_3 = refs[-7:]
    rows, chans, cols = gt.shape
    some = grad.shape[0]
    first = part * (some // 8)
    mid = rows + 6
    top = lax.axis_index("lat") == lax.axis_size("lat") - 1
    lane = lane_iota((8, LANES))
    wide = slice(0, LANES), slice(LANES, 2 * LANES)
    at_row = lambda r, g: rows_of(r, g, chans)

    def adjoint_group(g, _):
        at = pl.ds(pl.multiple_of(g * 8, 8), 8)
        left, right = dcv_halo[at_row(6, g), :], dcv_halo[at_row(7, g), :]
        for r0 in range(0, mid, 2):
            pair = []
            for r in (r0, r0 + 1):
                if r < 3:
                    value = dcv_halo[at_row(r, g), :]
                elif r < rows + 3:
                    value = dcv[at_row(r - 3, g), :]
                else:
                    value = dcv_halo[at_row(r - rows, g), :]
                beyond = jnp.where(lane < 64, shift(right, -3 * r), shift(left, LANES - 3 - 3 * r))
                pair.append(jnp.concatenate([value, beyond], axis=1))
            rhs[8 * r0 : 8 * r0 + 16, :] = jnp.concatenate(pair, axis=0).astype(BF)
        for q in range(7):
            one, two = turned[q, at, :], plain[q, at, :]
            above = jnp.where(top, two, one)
            moved = [pltpu.roll(one, 8 * i, 1, stride=1, stride_axis=0) for i in range(10)]
            band[q * 80 : q * 80 + 80, :] = jnp.concatenate(moved, axis=0).astype(BF)
            late = moved[:3]
            for i in range(3, 6):
                other = pltpu.roll(above, 8 * i, 1, stride=1, stride_axis=0)
                late.append(jnp.where(lane >= 8 * (rows + 3 - 10), other, moved[i]))
            band_up[q * 48 : q * 48 + 48, :] = jnp.concatenate(late, axis=0).astype(BF)
        prod_1[...] = jnp.dot(band[...], rhs[0:128, :], preferred_element_type=F32)
        prod_3[...] = jnp.dot(band_up[:, 0:96], rhs[80:176, :], preferred_element_type=F32)
        for o in range(rows):
            prod, step, i = (prod_1, 80, o) if o < 10 else (prod_3, 48, o - 10)
            inner = gt[o, at, :].astype(F32)
            for q in range(7):
                part = slice(q * step + 8 * i, q * step + 8 * i + 8)
                mine = prod[part, wide[0]]
                if q != 3:
                    mine = shift(jnp.where(edge_mask(lane, q - 3), prod[part, wide[1]], mine), 3 - q)
                inner = inner + mine
            plane[pl.ds((g - first) * (8 * rows) + o, 8, stride=rows), :] = inner
        return 0

    lax.fori_loop(first, first + some // 8, adjoint_group, 0)
    for c in range(some):
        grad[c] = plane[c * rows : (c + 1) * rows, :].astype(BF)


def finish_kernel(total, other, g_depth, g_gain, g_bias, g_up, g_up_b, g_down, g_scale):
    chans, hidden_n = g_down.shape

    def unpack(lower, upper):
        for h in range(hidden_n // LANES):
            w = slice(h * LANES, (h + 1) * LANES)
            g_down[:, w] = lower[h * chans : (h + 1) * chans, :]
            g_up[:, w] = upper[h * chans : (h + 1) * chans, :]
            at = 2 * chans + 24 + 8 * h
            g_up_b[w] = upper[at : at + 1, :].reshape(LANES)
        small = jnp.concatenate(
            [
                lower[2 * chans : 2 * chans + 40, :],
                upper[2 * chans : 2 * chans + 24, :],
                jnp.zeros((LANES - chans, LANES), F32),
            ],
            axis=0,
        ).T
        for k, dst in enumerate((g_gain, g_bias, g_scale)):
            dst[...] = small[56 + k : 57 + k, :chans].reshape(chans)
        for a in range(7):
            g_depth[a] = small[8 * a : 8 * a + 7, :chans]

    odd_core = lax.axis_index("lon") % 2

    @pl.when(odd_core == 0)
    def _():
        unpack(total, other)

    @pl.when(odd_core == 1)
    def _():
        unpack(other, total)


def vmem(n):
    return [pl.BlockSpec(memory_space=pltpu.VMEM)] * n


def shards(
    fields,
    cotangent,
    ocean_mask,
    seam_partner,
    depth_weight,
    norm_gain,
    layer_norm_bias,
    up_weight,
    up_bias,
    down_weight,
    layer_scale,
):
    _, chans, rows, cols = fields.shape
    hidden_n = up_weight.shape[0]
    n_lon, n_lat = lax.axis_size("lon"), lax.axis_size("lat")
    sds = jax.ShapeDtypeStruct
    hbm = pl.BlockSpec(memory_space=pltpu.HBM)
    ft, gt, first, second, partner, turn = pl.pallas_call(
        pack_kernel,
        out_shape=[sds((rows, chans, cols), BF)] * 2
        + [sds((9, chans, cols), BF)] * 2
        + [sds((1, cols), jnp.int32), sds((1,), jnp.int32)],
        in_specs=[hbm] * 4,
        out_specs=vmem(5) + [hbm],
        scratch_shapes=[
            pltpu.VMEM((2, chans * rows, cols), F32),
            pltpu.VMEM((chans, rows, cols), BF),
            pltpu.VMEM((chans, rows, cols), BF),
            pltpu.VMEM((rows, cols), jnp.int32),
            pltpu.SMEM((1, cols), jnp.int32),
            pltpu.SMEM((1,), jnp.int32),
            pltpu.SemaphoreType.DMA((6,)),
        ],
        compiler_params=pltpu.CompilerParams(vmem_limit_bytes=8 * 2**20),
        name="pack",
    )(
        *[
            pltpu.with_memory_space_constraint(v, pltpu.HBM)
            for v in (seam_partner.reshape(n_lon, cols), fields[0], cotangent[0], ocean_mask)
        ]
    )

    at = lambda lon, lat: (lon % n_lon) * n_lat + lat
    rounds = [[], []]
    for lat in range(n_lat - 1):
        for lon in range(n_lon):
            rounds[lat % 2] += [(at(lon, lat), at(lon, lat + 1)), (at(lon, lat + 1), at(lon, lat))]
    fold_round = (n_lat - 1) % 2

    axes = ("lon", "lat")
    plain_round = 1 - fold_round
    sends = (first, second)
    met = lax.ppermute(sends[plain_round], axes, rounds[plain_round])
    top = sends[fold_round]

    weights = pl.pallas_call(
        weight_kernel,
        out_shape=[
            sds((7, chans, LANES), F32),
            sds((7, chans, LANES), F32),
            sds((3, chans, LANES), F32),
            sds((hidden_n, chans + 16), BF),
            sds((hidden_n, chans), BF),
            sds((chans // 8, 7 * 80, LANES), BF),
            sds((chans // 8, 7 * 32, LANES), BF),
        ],
        in_specs=vmem(7),
        out_specs=vmem(7),
        scratch_shapes=[pltpu.VMEM((2, 7, LANES, LANES), F32)],
        cost_estimate=pl.CostEstimate(flops=20_000_000, bytes_accessed=2**21, transcendentals=0),
        compiler_params=pltpu.CompilerParams(vmem_limit_bytes=8 * 2**20),
        name="weights",
    )
    params = (
        depth_weight.transpose(1, 2, 0),
        norm_gain,
        layer_norm_bias,
        layer_scale,
        up_bias,
        up_weight.T,
        down_weight,
    )

    def exchange(k):
        def run(top, *params):
            mirror = [
                [(at(lon, n_lat - 1), at(k - j - lon, n_lat - 1)) for lon in range(n_lon)] for j in (0, 1)
            ]
            plan = rounds[fold_round] + mirror[0]
            return lax.ppermute(top, axes, mirror[1]), lax.ppermute(top, axes, plan), weights(*params)

        return run

    got_c, folded, made = lax.switch(turn[0], [exchange(k) for k in range(n_lon)], top, *params)
    plain, turned, vecs, up_aug, down_t, band, band_up = made
    got_a, got_b = (folded, met) if fold_round == 0 else (met, folded)
    low, up, sent_l, sent_r = pl.pallas_call(
        functools.partial(edge_kernel, fold_round == 0),
        out_shape=[sds((9, chans, cols), BF)] * 2 + [sds((chans, 2 * cols), BF)] * 2,
        in_specs=vmem(6),
        out_specs=vmem(4),
        compiler_params=pltpu.CompilerParams(vmem_limit_bytes=8 * 2**20),
        name="edges",
    )(partner, got_a, got_b, got_c, ft, gt)
    got_l = lax.ppermute(sent_r, "lon", [(i, (i + 1) % n_lon) for i in range(n_lon)])
    got_r = lax.ppermute(sent_l, "lon", [(i, (i - 1) % n_lon) for i in range(n_lon)])

    big, small = 2 * chans, 40
    up_t = up_weight.T
    band_rows = (rows + 12) * 8
    output, conv_halo, dcv, kept, passed = pl.pallas_call(
        own_kernel,
        out_shape=[
            sds((chans, rows, cols), BF),
            sds((8 * chans, cols), F32),
            sds((rows * chans, cols), F32),
            sds((big + small, LANES), F32),
            sds((big + small, LANES), F32),
        ],
        in_specs=vmem(14),
        out_specs=vmem(5),
        scratch_shapes=[
            pltpu.VMEM(((rows + 12) * chans, cols), F32),
            pltpu.VMEM(((rows + 12) * chans, cols), F32),
            pltpu.VMEM((band_rows, 2 * cols), BF),
            pltpu.VMEM((rows * chans, cols), F32),
            pltpu.VMEM((chans * rows, cols), F32),
            pltpu.VMEM((7 * 80, 2 * cols), F32),
            pltpu.VMEM((7 * 80, 2 * cols), F32),
            pltpu.VMEM((7 * 32, 2 * cols), F32),
            pltpu.VMEM((chans, hidden_n), F32),
            pltpu.VMEM((chans + 16, hidden_n), F32),
            pltpu.VMEM((3, chans, LANES), F32),
            pltpu.VMEM((chans, LANES), F32),
        ],
        compiler_params=pltpu.CompilerParams(vmem_limit_bytes=20 * 2**20),
        name="own",
    )(
        ft,
        gt,
        low,
        up,
        got_l,
        got_r,
        ocean_mask,
        band,
        band_up,
        vecs,
        up_aug,
        up_t,
        down_weight,
        down_t,
    )

    dcv_halo = pl.pallas_call(
        halo_kernel,
        out_shape=sds((8 * chans, cols), F32),
        in_specs=vmem(9),
        out_specs=vmem(1)[0],
        scratch_shapes=[pltpu.VMEM((8 * chans, cols), F32)],
        cost_estimate=pl.CostEstimate(flops=150_000_000, bytes_accessed=2**20, transcendentals=2**18),
        compiler_params=pltpu.CompilerParams(vmem_limit_bytes=8 * 2**20),
        name="halo",
    )(conv_halo, low, up, got_l, got_r, vecs, up_aug, up_t, down_t)

    def adjoint(part, *earlier):
        half = chans // 2
        return pl.pallas_call(
            functools.partial(adjoint_kernel, part),
            grid=(1,),
            out_shape=sds((chans, rows, cols), BF),
            in_specs=vmem(5) + [pl.BlockSpec(memory_space=pl.ANY)] * len(earlier),
            out_specs=pl.BlockSpec((half, rows, cols), lambda _: (part, 0, 0)),
            scratch_shapes=[
                pltpu.VMEM((band_rows, 2 * cols), BF),
                pltpu.VMEM((half * rows, cols), F32),
                pltpu.VMEM((7 * 80, LANES), BF),
                pltpu.VMEM((7 * 48, LANES), BF),
                pltpu.VMEM((7 * 80, 2 * cols), F32),
                pltpu.VMEM((7 * 48, 2 * cols), F32),
            ],
            input_output_aliases={5: 0} if earlier else {},
            cost_estimate=pl.CostEstimate(flops=200_000_000, bytes_accessed=2**21, transcendentals=0),
            compiler_params=pltpu.CompilerParams(vmem_limit_bytes=12 * 2**20),
            name="adjoint",
        )(dcv, dcv_halo, gt, plain, turned, *earlier)

    flip = lambda y, axis, b: lax.ppermute(y, axis, [(i, i ^ b) for i in range(lax.axis_size(axis))])
    total = kept + flip(passed, "lon", 1)
    steps = [("lon", 1 << i) for i in range(1, n_lon.bit_length() - 1)]
    steps += [("lat", 1 << i) for i in range(n_lat.bit_length() - 1)]
    grad = None
    for k, (axis, b) in enumerate(steps):
        total = total + flip(total, axis, b)
        if k == 0:
            total, dcv_halo = lax.optimization_barrier((total, dcv_halo))
        elif k == 1:
            grad = adjoint(0)
            total, grad = lax.optimization_barrier((total, grad))
        elif k == 2:
            grad = adjoint(1, grad)
            total, grad = lax.optimization_barrier((total, grad))
    other = flip(total, "lon", 1)
    g_depth, g_gain, g_bias, g_up, g_up_b, g_down, g_scale = pl.pallas_call(
        finish_kernel,
        out_shape=[
            sds((7, 7, chans), F32),
            sds((chans,), F32),
            sds((chans,), F32),
            sds((chans, hidden_n), F32),
            sds((hidden_n,), F32),
            sds((chans, hidden_n), F32),
            sds((chans,), F32),
        ],
        in_specs=vmem(2),
        out_specs=vmem(7),
        compiler_params=pltpu.CompilerParams(vmem_limit_bytes=6 * 2**20),
        name="finish",
    )(total, other)
    return (
        output[None],
        grad[None],
        g_depth.transpose(2, 0, 1),
        g_gain,
        g_bias,
        g_up.T,
        g_up_b,
        g_down,
        g_scale,
    )


def solution(mesh):
    block = P(None, None, "lat", "lon")
    placed = (block, block, P("lat", "lon")) + (P(),) * 8
    return jax.shard_map(
        shards, mesh=mesh, in_specs=placed, out_specs=(block, block) + (P(),) * 7, check_vma=False
    )
```

```python
import functools
import math

import jax
import jax.numpy as jnp
from jax import lax
from jax.experimental import pallas as pl
from jax.experimental.pallas import tpu as pltpu
from jax.sharding import PartitionSpec as P

BF = jnp.bfloat16
F32 = jnp.float32
LANES = 128
NT = (((1,), (1,)), ((), ()))


def shift(x, amount, axis=1):
    size = x.shape[axis]
    amount %= size
    return x if amount == 0 else pltpu.roll(x, amount, axis)


def lane_iota(shape):
    return lax.broadcasted_iota(jnp.int32, shape, 1)


def pack_kernel(
    seam, fields_far, cot_far, mask_far, ft, gt, first, second, partner, turn, *scratch
):
    plane, fields, cot, mask, head, index, arrived = scratch
    chans, rows, cols = fields.shape
    groups = chans // 8
    pairs = (
        (fields_far, fields),
        (cot_far, cot),
        (mask_far, mask),
        (seam.at[pl.ds(0, 1), :], head),
        (seam.at[pl.ds(lax.axis_index("lon"), 1), :], partner),
    )
    copies = [pltpu.make_async_copy(src, dst, arrived.at[k]) for k, (src, dst) in enumerate(pairs)]
    for k in (3, 0, 1, 2, 4):
        copies[k].start()
    copies[3].wait()
    index[0] = head[0, 0] // cols
    answer = pltpu.make_async_copy(index, turn, arrived.at[5])
    answer.start()
    for k, dst in ((0, ft), (1, gt)):
        copies[k].wait()
        if k == 1:
            copies[2].wait()
            sea = mask[...].astype(F32)
        for c in range(chans):
            if k == 0:
                cell = fields[c].astype(F32)
            else:
                cell = cot[c].astype(F32) * sea
            plane[k, c * rows : (c + 1) * rows, :] = cell
        for r in range(rows):
            parts = [plane[k, pl.ds(g * 8 * rows + r, 8, stride=rows), :] for g in range(groups)]
            dst[r] = jnp.concatenate(parts, axis=0).astype(BF)

    def edge(dst, top):
        base = rows - 6 if top else 0
        gbase = rows - 3 if top else 0
        dst[0:6] = ft[base : base + 6]
        dst[6:9] = gt[gbase : gbase + 3]

    odd = lax.axis_index("lat") % 2

    @pl.when(odd == 0)
    def _():
        edge(first, True)
        edge(second, False)

    @pl.when(odd == 1)
    def _():
        edge(first, False)
        edge(second, True)

    copies[4].wait()
    answer.wait()


def field_lane(r):
    return LANES * (r // 14) + 6 * (r % 14)


def cot_lane(g):
    return LANES * (g // 11) + 84 + 3 * (g % 11)


def edge_kernel(fold_first, partner, got_a, got_b, got_c, ft, gt, low, up, sent_l, sent_r):
    rows, chans, cols = ft.shape
    total = lax.axis_size("lon") * cols
    z = lax.axis_index("lat")
    odd = z % 2
    top = z == lax.axis_size("lat") - 1

    @pl.when(odd == 1)
    def _():
        low[...] = got_a[...]

    @pl.when(odd == 0)
    def _():
        low[...] = got_b[...]

    @pl.when(top)
    def _():
        got_1 = got_a if fold_first else got_b
        src = lax.broadcasted_iota(jnp.int32, (cols, cols), 0)
        want = jnp.broadcast_to(partner[...], (cols, cols))
        leading = jnp.broadcast_to(partner[:, 0:1], (cols, cols))
        near = leading - lax.rem(leading, jnp.full_like(leading, cols))
        far = jnp.where(near == 0, total, near) - cols
        pick_1 = (src + near == want).astype(F32).astype(BF)
        pick_2 = (src + far == want).astype(F32).astype(BF)
        mixed = jnp.dot(got_1[...].reshape(9 * chans, cols), pick_1, preferred_element_type=F32)
        mixed = mixed + jnp.dot(got_c[...].reshape(9 * chans, cols), pick_2, preferred_element_type=F32)
        for k in range(9):
            m = 5 - k if k < 6 else 14 - k
            up[k] = mixed[m * chans : (m + 1) * chans].astype(BF)

    @pl.when(jnp.logical_not(top) & (odd == 0))
    def _():
        up[...] = got_a[...]

    @pl.when(jnp.logical_not(top) & (odd == 1))
    def _():
        up[...] = got_b[...]

    lane = lane_iota((chans, LANES))
    acc = {key: jnp.zeros((chans, LANES), F32) for key in ((0, 0), (0, 1), (1, 0), (1, 1))}

    def place(side, value, source, lane_to, width):
        half, at = lane_to // LANES, lane_to % LANES
        moved = shift(value, at - source)
        acc[side, half] = jnp.where((lane >= at) & (lane < at + width), moved, acc[side, half])

    for r in range(rows + 12):
        if r < 6:
            value = low[r]
        elif r < rows + 6:
            value = ft[r - 6]
        else:
            value = up[r - rows - 6]
        value = value.astype(F32)
        place(1, value, cols - 6, field_lane(r), 6)
        place(0, value, 0, field_lane(r), 6)
    for r in range(rows + 6):
        if r < 3:
            value = low[6 + r]
        elif r < rows + 3:
            value = gt[r - 3]
        else:
            value = up[6 + r - rows - 3]
        value = value.astype(F32)
        place(1, value, cols - 3, cot_lane(r), 3)
        place(0, value, 0, cot_lane(r), 3)
    for side, dst in ((0, sent_l), (1, sent_r)):
        dst[...] = jnp.concatenate([acc[side, 0], acc[side, 1]], axis=1).astype(BF)


def weight_kernel(
    taps, gain, bias, scale, up_b, up_t, down, plain, turned, vecs, up_aug, down_t, band, band_up, line
):
    chans, hidden_n = up_t.shape
    top = lax.axis_index("lat") == lax.axis_size("lat") - 1
    line[...] = jnp.zeros_like(line)
    for a in range(7):
        block = taps[a].astype(F32)
        for q in range(7):
            line[0, q, 8 * a : 8 * a + 1, 0:chans] = block[q : q + 1]
            line[1, 6 - q, 48 - 8 * a : 49 - 8 * a, 0:chans] = block[q : q + 1]
    for q in range(7):
        plain[q] = line[0, q].T[:chans]
        turned[q] = line[1, q].T[:chans]

    def spread(g, _):
        at = pl.ds(pl.multiple_of(g * 8, 8), 8)
        for q in range(7):
            one, two = plain[q, at, :], turned[q, at, :]
            above = jnp.where(top, two, one)
            band[g, q * 80 : q * 80 + 80, :] = jnp.concatenate(
                [pltpu.roll(one, 8 * i, 1, stride=1, stride_axis=0) for i in range(10)], axis=0
            ).astype(BF)
            band_up[g, q * 32 : q * 32 + 32, :] = jnp.concatenate(
                [pltpu.roll(above, 8 * i, 1, stride=1, stride_axis=0) for i in range(6, 10)], axis=0
            ).astype(BF)
        return 0

    lax.fori_loop(0, chans // 8, spread, 0)
    wide = LANES - chans
    columns = jnp.concatenate(
        [v[...].astype(F32).reshape(1, chans) for v in (gain, bias, scale)] + [jnp.zeros((5, chans), F32)],
        axis=0,
    )
    columns = jnp.concatenate([columns, jnp.zeros((8, wide), F32)], axis=1).T
    for k in range(3):
        vecs[k] = jnp.broadcast_to(columns[:chans, k : k + 1], (chans, LANES))
    tall = jnp.concatenate(
        [
            up_t[...].astype(F32),
            up_b[...].astype(F32).reshape(1, hidden_n),
            jnp.zeros((wide - 1, hidden_n), F32),
        ],
        axis=0,
    )
    up_aug[...] = tall.T[:, : chans + 16].astype(BF)
    tall = jnp.concatenate([down[...].astype(F32), jnp.zeros((wide, hidden_n), F32)], axis=0)
    down_t[...] = tall.T[:, :chans].astype(BF)


def normal_terms(v):
    cdf = 0.5 * (1.0 + lax.erf(v * (1.0 / math.sqrt(2.0))))
    dens = jnp.exp2(v * v * (-0.5 / math.log(2.0)) - 0.5 * math.log2(2.0 * math.pi))
    return cdf, dens


def edge_mask(lane, s):
    return lane < s if s > 0 else lane >= LANES + s


def rows_of(r, g, chans):
    return pl.ds(pl.multiple_of(r * chans + g * 8, 8), 8)


def twice(x):
    return jnp.concatenate([x, x], axis=1)


def norm_and_back(x, g, vecs, up_aug, up_t, down_t):
    gain, bias, scale = twice(vecs[0]), twice(vecs[1]), twice(vecs[2])
    centred = x - jnp.mean(x, axis=0, keepdims=True)
    var = jnp.mean(centred * centred, axis=0, keepdims=True)
    rstd = lax.rsqrt(var + 1e-06)
    xhat = centred * rstd
    pad = (up_aug.shape[1] - x.shape[0], x.shape[1])
    ones = (lax.broadcasted_iota(jnp.int32, pad, 0) == 0).astype(F32).astype(BF)
    normed = jnp.concatenate([(xhat * gain + bias).astype(BF), ones], axis=0)
    pre = jnp.dot(up_aug[...], normed, preferred_element_type=F32)
    cdf, dens = normal_terms(pre)
    d_branch = (g * scale).astype(BF)
    d_hidden = jnp.dot(down_t[...], d_branch, preferred_element_type=F32)
    d_pre = (d_hidden * (cdf + pre * dens)).astype(BF)
    d_normed = jnp.dot(up_t[...], d_pre, preferred_element_type=F32)
    gd = d_normed * gain
    m1 = jnp.mean(gd, axis=0, keepdims=True)
    m2 = jnp.mean(gd * xhat, axis=0, keepdims=True)
    dx = (rstd * (gd - m1 - xhat * m2)).astype(BF).astype(F32)
    return dx, (pre, cdf, d_branch, d_pre, d_normed, normed, xhat, scale)


def own_kernel(
    ft,
    gt,
    low,
    up,
    got_l,
    got_r,
    mask,
    band,
    band_up,
    vecs,
    up_aug,
    up_t,
    down,
    down_t,
    out,
    conv_halo,
    dcv,
    kept,
    passed,
    ext,
    rim,
    rhs,
    conv,
    plane,
    prod_1,
    prod_2,
    prod_3,
    g_down,
    g_up,
    sums,
    taps_g,
):
    rows, chans, cols = ft.shape
    groups = chans // 8
    mid = rows + 6
    odd_core = lax.axis_index("lon") % 2
    lane = lane_iota((8, LANES))
    wide = slice(0, LANES), slice(LANES, 2 * LANES)
    at_row = lambda r, g: rows_of(r, g, chans)

    def conv_group(g, _):
        at = pl.ds(pl.multiple_of(g * 8, 8), 8)
        left = [got_l[at, w].astype(F32) for w in wide]
        right = [got_r[at, w].astype(F32) for w in wide]
        for r0 in range(0, rows + 12, 2):
            pair = []
            for r in (r0, r0 + 1):
                if r < 6:
                    value = low[r, at, :]
                elif r < rows + 6:
                    value = ft[r - 6, at, :]
                else:
                    value = up[r - rows - 6, at, :]
                value = value.astype(F32)
                half, start = field_lane(r) // LANES, field_lane(r) % LANES
                beyond = jnp.where(lane < 64, shift(right[half], -start), shift(left[half], LANES - 6 - start))
                ext[at_row(r, g), :] = value
                rim[at_row(r, g), :] = beyond
                pair.append(jnp.concatenate([value, beyond], axis=1))
            rhs[8 * r0 : 8 * r0 + 16, :] = jnp.concatenate(pair, axis=0).astype(BF)
        prod_1[...] = jnp.dot(band[g], rhs[0:128, :], preferred_element_type=F32)
        prod_2[...] = jnp.dot(band[g], rhs[80:208, :], preferred_element_type=F32)
        prod_3[...] = jnp.dot(band_up[g], rhs[96:224, :], preferred_element_type=F32)
        sides = [jnp.zeros((8, LANES), F32)] * 2
        for o in range(mid):
            if o < 10:
                prod, step, i = prod_1, 80, o
            elif o < rows + 3:
                prod, step, i = prod_2, 80, o - 10
            else:
                prod, step, i = prod_3, 32, o - 18
            inner = outer = None
            for q in range(7):
                part = slice(q * step + 8 * i, q * step + 8 * i + 8)
                mine, edge = prod[part, wide[0]], prod[part, wide[1]]
                if q != 3:
                    swap = edge_mask(lane, q - 3)
                    mine, edge = jnp.where(swap, edge, mine), jnp.where(swap, mine, edge)
                    mine, edge = shift(mine, 3 - q), shift(edge, 3 - q)
                inner = mine if inner is None else inner + mine
                outer = edge if outer is None else outer + edge
            if o < 3:
                conv_halo[at_row(o, g), :] = inner
            elif o < rows + 3:
                conv[at_row(o - 3, g), :] = inner
            else:
                conv_halo[at_row(o - rows, g), :] = inner
            inside = (lane >= 3 * o) & (lane < 3 * o + 3)
            sides[0] = jnp.where(inside, shift(outer, 3 * o + 3), sides[0])
            sides[1] = jnp.where(inside, shift(outer, 3 * o), sides[1])
        for k in (0, 1):
            conv_halo[at_row(6 + k, g), :] = sides[k]
        return 0

    lax.fori_loop(0, groups, conv_group, 0)

    g_down[...] = jnp.zeros_like(g_down)
    g_up[...] = jnp.zeros_like(g_up)
    sums[...] = jnp.zeros_like(sums)

    def unit(u):
        return pl.ds(pl.multiple_of(u * chans, chans), chans)

    def own_block(b, _):
        units = (b * 2, b * 2 + 1)
        x = jnp.concatenate([conv[unit(u), :] for u in units], axis=1)
        g = jnp.concatenate([gt[u].astype(F32) for u in units], axis=1)
        dx, (pre, cdf, d_branch, d_pre, d_normed, normed, xhat, scale) = norm_and_back(
            x, g, vecs, up_aug, up_t, down_t
        )
        hidden = (pre * cdf).astype(BF)
        branch = jnp.dot(down[...], hidden, preferred_element_type=F32)
        sea = [mask[pl.ds(u, 1), :].astype(F32) for u in units]
        fields = jnp.concatenate([ft[u].astype(F32) for u in units], axis=1)
        res = (fields + scale * branch) * jnp.concatenate(sea, axis=1)
        for k, u in enumerate(units):
            for gr in range(groups):
                plane[pl.ds(gr * 8 * rows + u, 8, stride=rows), :] = res[gr * 8 : gr * 8 + 8, wide[k]]
            dcv[unit(u), :] = dx[:, wide[k]]
        g_down[...] += lax.dot_general(d_branch, hidden, NT, preferred_element_type=F32)
        g_up[...] += lax.dot_general(normed, d_pre, NT, preferred_element_type=F32)
        for k, value in enumerate((d_normed * xhat, d_normed, g * branch)):
            sums[k] += value[:, :LANES] + value[:, LANES:]
        return 0

    lax.fori_loop(0, rows // 2, own_block, 0, unroll=2)

    def taps_group(g, _):
        at = pl.ds(pl.multiple_of(g * 8, 8), 8)
        line = jnp.zeros((8, LANES), F32)
        for q in range(7):
            own = [shift(dcv[at_row(o, g), :], q - 3) for o in range(rows)]
            tot = [None] * 7
            for r in range(mid):
                value = ext[at_row(r + 3, g), :]
                if q != 3:
                    value = jnp.where(edge_mask(lane, q - 3), rim[at_row(r + 3, g), :], value)
                for a in range(7):
                    o = r - a
                    if 0 <= o < rows:
                        term = value * own[o]
                        tot[a] = term if tot[a] is None else tot[a] + term
            for a in range(7):
                total = jnp.sum(tot[a], axis=1, keepdims=True)
                line = jnp.where(lane == 8 * a + q, total, line)
        for k in range(3):
            total = jnp.sum(sums[k, at, :], axis=1, keepdims=True)
            line = jnp.where(lane == 56 + k, total, line)
        taps_g[at, :] = line
        return 0

    lax.fori_loop(0, groups, taps_group, 0)
    small = taps_g[...]
    cut = 40

    def fill(lower, upper):
        for h, w in enumerate(wide):
            lower[h * chans : (h + 1) * chans, :] = g_down[:, w]
            upper[h * chans : (h + 1) * chans, :] = g_up[0:chans, w]
            upper[2 * chans + 24 + 8 * h : 2 * chans + 32 + 8 * h, :] = g_up[chans : chans + 8, w]
        lower[2 * chans : 2 * chans + cut, :] = small[:cut]
        upper[2 * chans : 2 * chans + 24, :] = small[cut:]

    @pl.when(odd_core == 0)
    def _():
        fill(kept, passed)

    @pl.when(odd_core == 1)
    def _():
        fill(passed, kept)

    for c in range(chans):
        out[c] = plane[c * rows : (c + 1) * rows, :].astype(BF)


def halo_kernel(conv_halo, low, up, got_l, got_r, vecs, up_aug, up_t, down_t, dcv_halo, cots):
    _, chans, _ = low.shape
    lane_c = lane_iota((chans, LANES))
    wide = slice(0, LANES), slice(LANES, 2 * LANES)
    for r in range(3):
        cots[r * chans : (r + 1) * chans, :] = low[6 + r].astype(F32)
        cots[(3 + r) * chans : (4 + r) * chans, :] = up[6 + r].astype(F32)
    for k, got in ((0, got_l), (1, got_r)):
        first = shift(got[:, wide[0]].astype(F32), -84)
        second = shift(got[:, wide[1]].astype(F32), 33 - 84)
        value = jnp.where(lane_c < 33, first, jnp.where(lane_c < 66, second, 0.0))
        cots[(6 + k) * chans : (7 + k) * chans, :] = value

    def halo_block(b, _):
        units = [pl.ds(pl.multiple_of((2 * b + k) * chans, chans), chans) for k in (0, 1)]
        x = jnp.concatenate([conv_halo[u, :] for u in units], axis=1)
        g = jnp.concatenate([cots[u, :] for u in units], axis=1)
        dx, _ = norm_and_back(x, g, vecs, up_aug, up_t, down_t)
        for k, u in enumerate(units):
            dcv_halo[u, :] = dx[:, wide[k]]
        return 0

    lax.fori_loop(0, 4, halo_block, 0, unroll=2)


def adjoint_kernel(part, *refs):
    dcv, dcv_halo, gt, plain, turned = refs[:5]
    grad, rhs, plane, band, band_up, prod_1, prod_3 = refs[-7:]
    rows, chans, cols = gt.shape
    some = grad.shape[0]
    first = part * (some // 8)
    mid = rows + 6
    top = lax.axis_index("lat") == lax.axis_size("lat") - 1
    lane = lane_iota((8, LANES))
    wide = slice(0, LANES), slice(LANES, 2 * LANES)
    at_row = lambda r, g: rows_of(r, g, chans)

    def adjoint_group(g, _):
        at = pl.ds(pl.multiple_of(g * 8, 8), 8)
        left, right = dcv_halo[at_row(6, g), :], dcv_halo[at_row(7, g), :]
        for r0 in range(0, mid, 2):
            pair = []
            for r in (r0, r0 + 1):
                if r < 3:
                    value = dcv_halo[at_row(r, g), :]
                elif r < rows + 3:
                    value = dcv[at_row(r - 3, g), :]
                else:
                    value = dcv_halo[at_row(r - rows, g), :]
                beyond = jnp.where(lane < 64, shift(right, -3 * r), shift(left, LANES - 3 - 3 * r))
                pair.append(jnp.concatenate([value, beyond], axis=1))
            rhs[8 * r0 : 8 * r0 + 16, :] = jnp.concatenate(pair, axis=0).astype(BF)
        for q in range(7):
            one, two = turned[q, at, :], plain[q, at, :]
            above = jnp.where(top, two, one)
            moved = [pltpu.roll(one, 8 * i, 1, stride=1, stride_axis=0) for i in range(10)]
            band[q * 80 : q * 80 + 80, :] = jnp.concatenate(moved, axis=0).astype(BF)
            late = moved[:3]
            for i in range(3, 6):
                other = pltpu.roll(above, 8 * i, 1, stride=1, stride_axis=0)
                late.append(jnp.where(lane >= 8 * (rows + 3 - 10), other, moved[i]))
            band_up[q * 48 : q * 48 + 48, :] = jnp.concatenate(late, axis=0).astype(BF)
        prod_1[...] = jnp.dot(band[...], rhs[0:128, :], preferred_element_type=F32)
        prod_3[...] = jnp.dot(band_up[:, 0:96], rhs[80:176, :], preferred_element_type=F32)
        for o in range(rows):
            prod, step, i = (prod_1, 80, o) if o < 10 else (prod_3, 48, o - 10)
            inner = gt[o, at, :].astype(F32)
            for q in range(7):
                part = slice(q * step + 8 * i, q * step + 8 * i + 8)
                mine = prod[part, wide[0]]
                if q != 3:
                    mine = shift(jnp.where(edge_mask(lane, q - 3), prod[part, wide[1]], mine), 3 - q)
                inner = inner + mine
            plane[pl.ds((g - first) * (8 * rows) + o, 8, stride=rows), :] = inner
        return 0

    lax.fori_loop(first, first + some // 8, adjoint_group, 0)
    for c in range(some):
        grad[c] = plane[c * rows : (c + 1) * rows, :].astype(BF)


def finish_kernel(total, other, g_depth, g_gain, g_bias, g_up, g_up_b, g_down, g_scale):
    chans, hidden_n = g_down.shape

    def unpack(lower, upper):
        for h in range(hidden_n // LANES):
            w = slice(h * LANES, (h + 1) * LANES)
            g_down[:, w] = lower[h * chans : (h + 1) * chans, :]
            g_up[:, w] = upper[h * chans : (h + 1) * chans, :]
            at = 2 * chans + 24 + 8 * h
            g_up_b[w] = upper[at : at + 1, :].reshape(LANES)
        small = jnp.concatenate(
            [
                lower[2 * chans : 2 * chans + 40, :],
                upper[2 * chans : 2 * chans + 24, :],
                jnp.zeros((LANES - chans, LANES), F32),
            ],
            axis=0,
        ).T
        for k, dst in enumerate((g_gain, g_bias, g_scale)):
            dst[...] = small[56 + k : 57 + k, :chans].reshape(chans)
        for a in range(7):
            g_depth[a] = small[8 * a : 8 * a + 7, :chans]

    odd_core = lax.axis_index("lon") % 2

    @pl.when(odd_core == 0)
    def _():
        unpack(total, other)

    @pl.when(odd_core == 1)
    def _():
        unpack(other, total)


def vmem(n):
    return [pl.BlockSpec(memory_space=pltpu.VMEM)] * n


def shards(
    fields,
    cotangent,
    ocean_mask,
    seam_partner,
    depth_weight,
    norm_gain,
    layer_norm_bias,
    up_weight,
    up_bias,
    down_weight,
    layer_scale,
):
    _, chans, rows, cols = fields.shape
    hidden_n = up_weight.shape[0]
    n_lon, n_lat = lax.axis_size("lon"), lax.axis_size("lat")
    sds = jax.ShapeDtypeStruct
    hbm = pl.BlockSpec(memory_space=pltpu.HBM)
    ft, gt, first, second, partner, turn = pl.pallas_call(
        pack_kernel,
        out_shape=[sds((rows, chans, cols), BF)] * 2
        + [sds((9, chans, cols), BF)] * 2
        + [sds((1, cols), jnp.int32), sds((1,), jnp.int32)],
        in_specs=[hbm] * 4,
        out_specs=vmem(5) + [hbm],
        scratch_shapes=[
            pltpu.VMEM((2, chans * rows, cols), F32),
            pltpu.VMEM((chans, rows, cols), BF),
            pltpu.VMEM((chans, rows, cols), BF),
            pltpu.VMEM((rows, cols), jnp.int32),
            pltpu.SMEM((1, cols), jnp.int32),
            pltpu.SMEM((1,), jnp.int32),
            pltpu.SemaphoreType.DMA((6,)),
        ],
        compiler_params=pltpu.CompilerParams(vmem_limit_bytes=8 * 2**20),
        name="pack",
    )(
        *[
            pltpu.with_memory_space_constraint(v, pltpu.HBM)
            for v in (seam_partner.reshape(n_lon, cols), fields[0], cotangent[0], ocean_mask)
        ]
    )

    at = lambda lon, lat: (lon % n_lon) * n_lat + lat
    rounds = [[], []]
    for lat in range(n_lat - 1):
        for lon in range(n_lon):
            rounds[lat % 2] += [(at(lon, lat), at(lon, lat + 1)), (at(lon, lat + 1), at(lon, lat))]
    fold_round = (n_lat - 1) % 2

    axes = ("lon", "lat")
    plain_round = 1 - fold_round
    sends = (first, second)
    met = lax.ppermute(sends[plain_round], axes, rounds[plain_round])
    top = sends[fold_round]

    def exchange(k):
        def run(top):
            mirror = [
                [(at(lon, n_lat - 1), at(k - j - lon, n_lat - 1)) for lon in range(n_lon)] for j in (0, 1)
            ]
            plan = rounds[fold_round] + mirror[0]
            return lax.ppermute(top, axes, mirror[1]), lax.ppermute(top, axes, plan)

        return run

    got_c, folded = lax.switch(turn[0], [exchange(k) for k in range(n_lon)], top)
    got_a, got_b = (folded, met) if fold_round == 0 else (met, folded)
    low, up, sent_l, sent_r = pl.pallas_call(
        functools.partial(edge_kernel, fold_round == 0),
        out_shape=[sds((9, chans, cols), BF)] * 2 + [sds((chans, 2 * cols), BF)] * 2,
        in_specs=vmem(6),
        out_specs=vmem(4),
        compiler_params=pltpu.CompilerParams(vmem_limit_bytes=8 * 2**20),
        name="edges",
    )(partner, got_a, got_b, got_c, ft, gt)
    got_l = lax.ppermute(sent_r, "lon", [(i, (i + 1) % n_lon) for i in range(n_lon)])
    got_r = lax.ppermute(sent_l, "lon", [(i, (i - 1) % n_lon) for i in range(n_lon)])

    plain, turned, vecs, up_aug, down_t, band, band_up = pl.pallas_call(
        weight_kernel,
        out_shape=[
            sds((7, chans, LANES), F32),
            sds((7, chans, LANES), F32),
            sds((3, chans, LANES), F32),
            sds((hidden_n, chans + 16), BF),
            sds((hidden_n, chans), BF),
            sds((chans // 8, 7 * 80, LANES), BF),
            sds((chans // 8, 7 * 32, LANES), BF),
        ],
        in_specs=vmem(7),
        out_specs=vmem(7),
        scratch_shapes=[pltpu.VMEM((2, 7, LANES, LANES), F32)],
        compiler_params=pltpu.CompilerParams(vmem_limit_bytes=8 * 2**20),
        name="weights",
    )(
        depth_weight.transpose(1, 2, 0),
        norm_gain,
        layer_norm_bias,
        layer_scale,
        up_bias,
        up_weight.T,
        down_weight,
    )
    big, small = 2 * chans, 40
    up_t = up_weight.T
    band_rows = (rows + 12) * 8
    output, conv_halo, dcv, kept, passed = pl.pallas_call(
        own_kernel,
        out_shape=[
            sds((chans, rows, cols), BF),
            sds((8 * chans, cols), F32),
            sds((rows * chans, cols), F32),
            sds((big + small, LANES), F32),
            sds((big + small, LANES), F32),
        ],
        in_specs=vmem(14),
        out_specs=vmem(5),
        scratch_shapes=[
            pltpu.VMEM(((rows + 12) * chans, cols), F32),
            pltpu.VMEM(((rows + 12) * chans, cols), F32),
            pltpu.VMEM((band_rows, 2 * cols), BF),
            pltpu.VMEM((rows * chans, cols), F32),
            pltpu.VMEM((chans * rows, cols), F32),
            pltpu.VMEM((7 * 80, 2 * cols), F32),
            pltpu.VMEM((7 * 80, 2 * cols), F32),
            pltpu.VMEM((7 * 32, 2 * cols), F32),
            pltpu.VMEM((chans, hidden_n), F32),
            pltpu.VMEM((chans + 16, hidden_n), F32),
            pltpu.VMEM((3, chans, LANES), F32),
            pltpu.VMEM((chans, LANES), F32),
        ],
        compiler_params=pltpu.CompilerParams(
            vmem_limit_bytes=20 * 2**20
        ),
        name="own",
    )(
        ft,
        gt,
        low,
        up,
        got_l,
        got_r,
        ocean_mask,
        band,
        band_up,
        vecs,
        up_aug,
        up_t,
        down_weight,
        down_t,
    )

    dcv_halo = pl.pallas_call(
        halo_kernel,
        out_shape=sds((8 * chans, cols), F32),
        in_specs=vmem(9),
        out_specs=vmem(1)[0],
        scratch_shapes=[pltpu.VMEM((8 * chans, cols), F32)],
        cost_estimate=pl.CostEstimate(flops=150_000_000, bytes_accessed=2**20, transcendentals=2**18),
        compiler_params=pltpu.CompilerParams(vmem_limit_bytes=8 * 2**20),
        name="halo",
    )(conv_halo, low, up, got_l, got_r, vecs, up_aug, up_t, down_t)

    def adjoint(part, *earlier):
        half = chans // 2
        return pl.pallas_call(
            functools.partial(adjoint_kernel, part),
            grid=(1,),
            out_shape=sds((chans, rows, cols), BF),
            in_specs=vmem(5) + [pl.BlockSpec(memory_space=pl.ANY)] * len(earlier),
            out_specs=pl.BlockSpec((half, rows, cols), lambda _: (part, 0, 0)),
            scratch_shapes=[
                pltpu.VMEM((band_rows, 2 * cols), BF),
                pltpu.VMEM((half * rows, cols), F32),
                pltpu.VMEM((7 * 80, LANES), BF),
                pltpu.VMEM((7 * 48, LANES), BF),
                pltpu.VMEM((7 * 80, 2 * cols), F32),
                pltpu.VMEM((7 * 48, 2 * cols), F32),
            ],
            input_output_aliases={5: 0} if earlier else {},
            cost_estimate=pl.CostEstimate(flops=200_000_000, bytes_accessed=2**21, transcendentals=0),
            compiler_params=pltpu.CompilerParams(vmem_limit_bytes=12 * 2**20),
            name="adjoint",
        )(dcv, dcv_halo, gt, plain, turned, *earlier)

    flip = lambda y, axis, b: lax.ppermute(y, axis, [(i, i ^ b) for i in range(lax.axis_size(axis))])
    total = kept + flip(passed, "lon", 1)
    steps = [("lon", 1 << i) for i in range(1, n_lon.bit_length() - 1)]
    steps += [("lat", 1 << i) for i in range(n_lat.bit_length() - 1)]
    grad = None
    for k, (axis, b) in enumerate(steps):
        total = total + flip(total, axis, b)
        if k == 0:
            total, dcv_halo = lax.optimization_barrier((total, dcv_halo))
        elif k == 1:
            grad = adjoint(0)
            total, grad = lax.optimization_barrier((total, grad))
        elif k == 2:
            grad = adjoint(1, grad)
            total, grad = lax.optimization_barrier((total, grad))
    other = flip(total, "lon", 1)
    g_depth, g_gain, g_bias, g_up, g_up_b, g_down, g_scale = pl.pallas_call(
        finish_kernel,
        out_shape=[
            sds((7, 7, chans), F32),
            sds((chans,), F32),
            sds((chans,), F32),
            sds((chans, hidden_n), F32),
            sds((hidden_n,), F32),
            sds((chans, hidden_n), F32),
            sds((chans,), F32),
        ],
        in_specs=vmem(2),
        out_specs=vmem(7),
        compiler_params=pltpu.CompilerParams(vmem_limit_bytes=6 * 2**20),
        name="finish",
    )(total, other)
    return (
        output[None],
        grad[None],
        g_depth.transpose(2, 0, 1),
        g_gain,
        g_bias,
        g_up.T,
        g_up_b,
        g_down,
        g_scale,
    )


def solution(mesh):
    block = P(None, None, "lat", "lon")
    placed = (block, block, P("lat", "lon")) + (P(),) * 8
    return jax.shard_map(
        shards, mesh=mesh, in_specs=placed, out_specs=(block, block) + (P(),) * 7, check_vma=False
    )
```
